32 devices in a mesh: grp: 2 (over y), seq: 4 (over z), mp: 2 (over x), rep: 2 (over core).
Axes of the slice: x: 2, y: 2, z: 4, core: 2. Of those that a mesh axis runs over, the one named last changes fastest.
Arguments:
- hyena_q: bfloat16 [4096, 4096], P(('grp', 'seq'), ('mp', 'rep')), parts along dimension 0, may hold values from -6 to 6
- hyena_k: bfloat16 [4096, 4096], P(('grp', 'seq'), ('mp', 'rep')), parts along dimension 0, may hold values from -6 to 6
- hyena_v: bfloat16 [4096, 4096], P(('grp', 'seq'), ('mp', 'rep')), parts along dimension 0, may hold values from -6 to 6
- short_filter: float32 [3, 3, 4096], P(None, None, ('mp', 'rep')), may hold values from -3.5 to 3.5
- long_filter: float32 [128, 256], P(None, ('mp', 'rep')), may hold values from -0.5 to 0.5
- skip_bias: float32 [4096], P(('mp', 'rep')), may hold values from -4 to 4
- attn_q: bfloat16 [4096, 4096], P(('grp', 'seq'), ('mp', 'rep')), parts along dimension 0, may hold values from -8 to 8
- attn_k: bfloat16 [4096, 4096], P(('grp', 'seq'), ('mp', 'rep')), parts along dimension 0, may hold values from -8 to 8
- attn_v: bfloat16 [4096, 4096], P(('grp', 'seq'), ('mp', 'rep')), parts along dimension 0, may hold values from -6 to 6
Outputs:
- hyena_out: bfloat16 [4096, 4096], P(('grp', 'seq'), ('mp', 'rep')), parts along dimension 0
- attn_out: bfloat16 [4096, 4096], P(('grp', 'seq'), ('mp', 'rep')), parts along dimension 0
The draws below stay inside these ranges and needn't reach their ends.
There are 2 independent parts, one for each index of `grp`. The reference program is written for one: setup_inputs(seed, part) draws one part's arguments, and reference() takes and returns one part's arrays. A program takes and returns all parts, laid end to end along the dimension named above; an argument that names none is the same for every part. Nothing has to cross between parts.
All inputs are finite; a program needn't handle non-finite values.
Results may differ from the reference program's by a relative error of at most 0.0049.
Values may be sent and summed in bfloat16 or wider, within the bound.
No kernel may reach another device: no remote copies, remote signals or barrier semaphores. Data moves between devices by JAX's collectives and lax.ppermute only.
A program may use at most 64 MiB of HBM per device.

```python
import jax
import jax.numpy as jnp
from jax import lax

D = 4096
H = 32
HD = 128
FILT = 128
SHORT = 3
GSIZE = 16
SEQLEN = 2048


def draw_attn_q(key, part):
    values = jnp.clip(2.0 * jax.random.normal(jax.random.fold_in(key, 1), (SEQLEN, H * HD), jnp.float32), -8.0, 8.0)
    return values.astype(jnp.bfloat16)


def draw_attn_k(key, part):
    values = jnp.clip(1.5 * jax.random.normal(jax.random.fold_in(key, 2), (SEQLEN, H * HD), jnp.float32), -8.0, 8.0)
    return values.astype(jnp.bfloat16)


def level_of(key, extent, cuts, low, top_value):
    level = 1.0
    for dim, blocks in cuts:
        heights = jax.random.uniform(jax.random.fold_in(jax.random.fold_in(key, 6), dim), (blocks,), jnp.float32, low / len(cuts), top_value / len(cuts))
        level = level * jnp.repeat(jnp.exp(heights), extent[dim] // blocks).reshape((-1,) + (1,) * (len(extent) - 1 - dim))
    return level


def noise(own_key, extent, scale, most, shards=(), held_as=jnp.bfloat16):
    values = scale * jax.random.normal(own_key, extent, jnp.float32)
    if shards:
        values = values * level_of(own_key, extent, shards, -0.22, 0.18)
    return jnp.clip(values, -most, most).astype(held_as)


def setup_inputs(seed: int = 0, part: int = 0) -> dict:
    key_of = jax.random.split(jax.random.key(seed), 10)
    part_splits = jax.random.split(jax.random.fold_in(key_of[9], part), 10)
    return {
        "hyena_q": noise(part_splits[0], (SEQLEN, D), 1.0, 6.0, ((0, 4), (1, 4))),
        "hyena_k": noise(part_splits[1], (SEQLEN, D), 1.0, 6.0, ((0, 4), (1, 4))),
        "hyena_v": noise(part_splits[2], (SEQLEN, D), 1.0, 6.0, ((0, 4), (1, 4))),
        "short_filter": noise(key_of[3], (3, SHORT, D), SHORT ** -0.5, 3.5, ((2, 4),), jnp.float32),
        "long_filter": noise(key_of[4], (FILT, D // GSIZE), FILT ** -0.5, 0.5, ((1, 4),), jnp.float32),
        "skip_bias": noise(key_of[5], (D,), 1.0, 4.0, ((0, 4),), jnp.float32),
        "attn_q": draw_attn_q(jax.random.fold_in(jax.random.fold_in(key_of[9], part), 71), part),
        "attn_k": draw_attn_k(jax.random.fold_in(jax.random.fold_in(key_of[9], part), 71), part),
        "attn_v": noise(part_splits[8], (SEQLEN, H * HD), 1.0, 6.0, ((0, 4), (1, 4))),
    }


def causal_taps(signal, taps):
    width = taps.shape[0]
    length = signal.shape[0]
    padded = jnp.pad(signal, ((width - 1, 0), (0, 0)))
    total = jnp.zeros(signal.shape, jnp.float32)
    for offset in range(width):
        total = total + taps[offset] * padded[width - 1 - offset: width - 1 - offset + length]
    return total


def attend_head(triple):
    query, keys, values = triple
    scores = jnp.dot(query, keys.T, preferred_element_type=jnp.float32) * (HD ** -0.5)
    length = scores.shape[0]
    causal = jnp.arange(length)[:, None] >= jnp.arange(length)[None, :]
    scores = jnp.where(causal, scores, -jnp.inf)
    top_score = jnp.max(scores, axis=1, keepdims=True)
    weights = jnp.where(causal, jnp.exp(scores - top_score), 0.0)
    denom = jnp.sum(weights, axis=1, keepdims=True)
    mixed = jnp.dot(weights.astype(jnp.bfloat16), values, preferred_element_type=jnp.float32)
    return mixed / denom


def reference(hyena_q, hyena_k, hyena_v, short_filter, long_filter, skip_bias, attn_q, attn_k, attn_v):
    q_conv = causal_taps(hyena_q.astype(jnp.float32), short_filter[0])
    k_conv = causal_taps(hyena_k.astype(jnp.float32), short_filter[1])
    v_conv = causal_taps(hyena_v.astype(jnp.float32), short_filter[2])
    gated = (k_conv * v_conv).astype(jnp.bfloat16)
    gated_f = lax.optimization_barrier(gated).astype(jnp.float32)
    long_taps = jnp.repeat(long_filter, GSIZE, axis=1)
    long_conv = causal_taps(gated_f, long_taps)
    hyena_out = (q_conv * (long_conv + skip_bias * gated_f)).astype(jnp.bfloat16)
    length = attn_q.shape[0]
    q_heads = attn_q.reshape(length, H, HD).transpose(1, 0, 2)
    k_heads = attn_k.reshape(length, H, HD).transpose(1, 0, 2)
    v_heads = attn_v.reshape(length, H, HD).transpose(1, 0, 2)
    mixed = lax.map(attend_head, (q_heads, k_heads, v_heads))
    attn_out = mixed.transpose(1, 0, 2).reshape(length, H * HD).astype(jnp.bfloat16)
    return hyena_out, attn_out
```

```python
import functools

import jax
import jax.numpy as jnp
from jax import lax
from jax.experimental import pallas as pl
from jax.experimental.pallas import tpu as pltpu
from jax.sharding import PartitionSpec as P

HD = 128
FILT = 128
SHORT = 3
GSIZE = 16
LANES = 128
TAIL = 16
STATS = 16
MiB = 1 << 20
LOG2E = 1.4426950408889634
SCALE2 = HD**-0.5 * LOG2E
NEG = -1e30
F32 = jnp.float32
BF16 = jnp.bfloat16


def ceil_params(limit=48):
    return pltpu.CompilerParams(vmem_limit_bytes=limit * MiB)


def estimate(flops, moved, exps=0):
    return pl.CostEstimate(flops=int(flops), bytes_accessed=int(moved), transcendentals=int(exps))


def short_conv(extended, taps, keep):
    total = taps[0][None] * extended
    total = total + taps[1][None] * pltpu.roll(extended, 1, 0)
    total = total + taps[2][None] * pltpu.roll(extended, 2, 0)
    return total[keep:]


def halo_kernel(q_ref, k_ref, v_ref, taps_ref, out_ref):
    rows = k_ref.shape[0]
    first = rows - FILT - TAIL
    k_in = k_ref[first:].astype(F32)
    v_in = v_ref[first:].astype(F32)
    k_conv = short_conv(k_in, taps_ref[1], TAIL)
    v_conv = short_conv(v_in, taps_ref[2], TAIL)
    out_ref[:FILT] = (k_conv * v_conv).astype(BF16)
    q_tail = q_ref[rows - TAIL :].astype(F32)
    k_tail = pltpu.roll(k_in[FILT:], TAIL - 2, 0)
    v_tail = pltpu.roll(v_in[FILT:], TAIL - 4, 0)
    row = lax.broadcasted_iota(jnp.int32, q_tail.shape, 0)
    packed = jnp.where(row >= TAIL - 2, q_tail, jnp.where(row >= TAIL - 4, k_tail, v_tail))
    out_ref[FILT:] = packed.astype(BF16)


def halo_pack(hyena_q, hyena_k, hyena_v, short_filter):
    rows, chans = hyena_q.shape
    width = min(256, chans)
    tail_rows = 256
    tail = pl.BlockSpec((tail_rows, width), lambda i: (rows // tail_rows - 1, i))
    return pl.pallas_call(
        halo_kernel,
        grid=(chans // width,),
        in_specs=[tail, tail, tail, pl.BlockSpec((3, SHORT, width), lambda i: (0, 0, i))],
        out_specs=pl.BlockSpec((FILT + TAIL, width), lambda i: (0, i)),
        out_shape=jax.ShapeDtypeStruct((FILT + TAIL, chans), BF16),
        compiler_params=ceil_params(16),
        cost_estimate=estimate(20 * FILT * chans, 2 * 4 * FILT * chans),
        name="halo_pack",
    )(hyena_q, hyena_k, hyena_v, short_filter)


def hyena_kernel(q_ref, k_ref, v_ref, halo_ref, taps_ref, filt_ref, skip_ref, out_ref, long_ref):
    rows = q_ref.shape[0]
    blocks = rows // FILT
    tail = halo_ref[FILT:].astype(F32)
    tails = (tail, pltpu.roll(tail, 2, 0), pltpu.roll(tail, 4, 0))

    def conv(which, ref):
        extended = jnp.concatenate([tails[which], ref[...].astype(F32)], axis=0)
        return short_conv(extended, taps_ref[which], TAIL)

    gated = (conv(1, k_ref) * conv(2, v_ref)).astype(BF16).astype(F32)
    signal = jnp.concatenate([halo_ref[:FILT].astype(F32), gated], axis=0)
    signal = signal.T.astype(BF16)
    source = lax.broadcasted_iota(jnp.int32, (FILT, FILT), 0)
    target = lax.broadcasted_iota(jnp.int32, (FILT, FILT), 1)
    near = target >= source
    for group in range(LANES // GSIZE):
        taps = jnp.broadcast_to(filt_ref[group : group + 1], (FILT, FILT))
        turned = pltpu.roll(taps, 0, 1, stride=1, stride_axis=0)
        table = jnp.concatenate(
            [jnp.where(near, 0.0, turned), jnp.where(near, turned, 0.0)], axis=0
        ).astype(BF16)
        band = signal[group * GSIZE : (group + 1) * GSIZE]
        stacked = jnp.concatenate(
            [band[:, b * FILT : (b + 2) * FILT] for b in range(blocks)], axis=0
        )
        result = jnp.dot(stacked, table, preferred_element_type=F32)
        for b in range(blocks):
            long_ref[group * GSIZE : (group + 1) * GSIZE, b * FILT : (b + 1) * FILT] = result[
                b * GSIZE : (b + 1) * GSIZE
            ]
    long_conv = long_ref[...].T
    mixed = conv(0, q_ref) * (long_conv + skip_ref[...] * gated)
    out_ref[...] = mixed.astype(BF16)


def hyena_mix(hyena_q, hyena_k, hyena_v, halo, short_filter, filter_rows, skip_row):
    rows, chans = hyena_q.shape
    tile = pl.BlockSpec((rows, LANES), lambda i: (0, i))
    return pl.pallas_call(
        hyena_kernel,
        grid=(chans // LANES,),
        in_specs=[
            tile,
            tile,
            tile,
            pl.BlockSpec((FILT + TAIL, LANES), lambda i: (0, i)),
            pl.BlockSpec((3, SHORT, LANES), lambda i: (0, 0, i)),
            pl.BlockSpec((LANES // GSIZE, FILT), lambda i: (i, 0)),
            pl.BlockSpec((1, LANES), lambda i: (0, i)),
        ],
        out_specs=tile,
        out_shape=jax.ShapeDtypeStruct((rows, chans), BF16),
        scratch_shapes=[pltpu.VMEM((LANES, rows), F32)],
        compiler_params=ceil_params(32),
        cost_estimate=estimate(2 * rows * chans * 256 * 8, 8 * rows * chans),
        name="hyena_mix",
    )(hyena_q, hyena_k, hyena_v, halo, short_filter, filter_rows, skip_row)


def scores_of(key, query):
    return lax.dot_general(key, query, (((1,), (1,)), ((), ())), preferred_element_type=F32)


def weighted(value, probs):
    return lax.dot_general(value, probs, (((0,), (0,)), ((), ())), preferred_element_type=F32)


def attend(score_list, value_list):
    top = functools.reduce(jnp.maximum, [jnp.max(s, axis=0, keepdims=True) for s in score_list])
    top = top * SCALE2
    total = None
    mixed = None
    for scores, value in zip(score_list, value_list):
        weights = jnp.exp2(scores * SCALE2 - top)
        part = jnp.sum(weights, axis=0, keepdims=True)
        term = weighted(value, weights.astype(BF16))
        total = part if total is None else total + part
        mixed = term if mixed is None else mixed + term
    return mixed / total, top + jnp.log2(total)


def causal_scores(key, query, first_query):
    scores = scores_of(key, query)
    key_pos = lax.broadcasted_iota(jnp.int32, scores.shape, 0)
    query_pos = lax.broadcasted_iota(jnp.int32, scores.shape, 1) + first_query
    return jnp.where(key_pos <= query_pos, scores, NEG)


def remote_kernel(heads, place_ref, qa_ref, qb_ref, kr_ref, vr_ref, k_ref, v_ref, oa_ref, ob_ref,
                  stat_a, stat_b):
    head = pl.program_id(0)
    place = place_ref[0]
    rows = qa_ref.shape[0]
    tile = min(256, rows)
    out_rows = pl.ds(pl.multiple_of(head * HD, HD), HD)

    def fill(q_ref, keys, values, o_ref, stat_ref):
        for start in range(0, rows, tile):
            query = q_ref[start : start + tile]
            mixed, level = attend([scores_of(k[...], query) for k in keys], [v[...] for v in values])
            o_ref[out_rows, start : start + tile] = mixed.astype(BF16)
            stat_ref[pl.ds(head, 1), start : start + tile] = level

    @pl.when(place == 1)
    def _():
        fill(qa_ref, [kr_ref, k_ref], [vr_ref, v_ref], oa_ref, stat_a)
        fill(qb_ref, [kr_ref, k_ref], [vr_ref, v_ref], ob_ref, stat_b)

    @pl.when(place == 2)
    def _():
        fill(qa_ref, [k_ref], [v_ref], oa_ref, stat_a)

    def pack(stat_ref, o_ref):
        level = stat_ref[...]
        high = level.astype(BF16).astype(F32)
        middle = (level - high).astype(BF16).astype(F32)
        low = level - high - middle
        row = lax.broadcasted_iota(jnp.int32, level.shape, 0)
        first = jnp.where(row < 4, high, pltpu.roll(middle, 4, 0))
        o_ref[heads * HD :] = jnp.concatenate([first, low], axis=0).astype(BF16)

    @pl.when((head == heads - 1) & (place >= 1) & (place <= 2))
    def _():
        pack(stat_a, oa_ref)

    @pl.when((head == heads - 1) & (place == 1))
    def _():
        pack(stat_b, ob_ref)


def remote_part(place, offset, qa, qb, kr, vr, attn_k, attn_v):
    rows, width = qa.shape
    heads = width // HD
    moved = pl.BlockSpec((rows, HD), lambda j, p: (0, j))
    local = pl.BlockSpec((rows, HD), lambda j, p: (0, offset + j))
    whole = pl.BlockSpec((width + STATS, rows), lambda j, p: (0, 0))
    shape = jax.ShapeDtypeStruct((width + STATS, rows), BF16)
    return pl.pallas_call(
        functools.partial(remote_kernel, heads),
        grid_spec=pltpu.PrefetchScalarGridSpec(
            num_scalar_prefetch=1,
            grid=(heads,),
            in_specs=[moved, moved, moved, moved, local, local],
            out_specs=(whole, whole),
            scratch_shapes=[pltpu.VMEM((8, rows), F32), pltpu.VMEM((8, rows), F32)],
        ),
        out_shape=(shape, shape),
        compiler_params=ceil_params(),
        cost_estimate=estimate(heads * 4 * 4 * HD * rows * rows, 16 * rows * width, heads * 4 * rows * rows),
        name="remote_part",
    )(place, qa, qb, kr, vr, attn_k, attn_v)


def level_row(stats, head):
    row = lax.broadcasted_iota(jnp.int32, stats.shape, 0)
    chosen = (row == head) | (row == head + 4) | (row == head + 8)
    return jnp.sum(jnp.where(chosen, stats, 0.0), axis=0, keepdims=True)


def final_kernel(heads, place_ref, q_ref, k_ref, v_ref, kr_ref, vr_ref, oa_ref, ob_ref, *rest):
    out_ref, mixed_ref, level_ref = rest[-3:]
    head = pl.program_id(0)
    place = place_ref[0]
    rows = q_ref.shape[0]
    tile = min(256, rows)
    in_rows = pl.ds(pl.multiple_of(head * HD, HD), HD)

    for start in range(0, rows, tile):
        cols = slice(start, start + tile)
        query = q_ref[cols]
        ready = start + tile
        scores = [causal_scores(k_ref[:ready], query, start)]
        values = [v_ref[:ready]]

        @pl.when(place == 1)
        def _():
            mixed, level = attend(
                scores + [scores_of(kr_ref[...], query)], values + [vr_ref[...]]
            )
            mixed_ref[:, cols] = mixed
            level_ref[:, cols] = level

        @pl.when(place != 1)
        def _():
            mixed, level = attend(scores, values)
            mixed_ref[:, cols] = mixed
            level_ref[:, cols] = level

    def merge(o_ref):
        other = o_ref[in_rows].astype(F32)
        other_level = level_row(o_ref[heads * HD :].astype(F32), head)
        level = level_ref[...]
        top = jnp.maximum(level, other_level)
        mine = jnp.exp2(level - top)
        theirs = jnp.exp2(other_level - top)
        both = mine + theirs
        mixed_ref[...] = mixed_ref[...] * (mine / both) + other * (theirs / both)
        level_ref[...] = top + jnp.log2(both)

    @pl.when(place >= 2)
    def _():
        merge(oa_ref)

    @pl.when(place >= 3)
    def _():
        merge(ob_ref)

    out_ref[...] = mixed_ref[...].T.astype(BF16)


def final_part(place, offset, attn_q, attn_k, attn_v, kr, vr, oa, ob, so_far):
    rows, chans = attn_q.shape
    width = kr.shape[1]
    heads = width // HD
    moved = pl.BlockSpec((rows, HD), lambda j, p: (0, j))
    local = pl.BlockSpec((rows, HD), lambda j, p: (0, offset + j))
    whole = pl.BlockSpec((width + STATS, rows), lambda j, p: (0, 0))
    operands = [place, attn_q, attn_k, attn_v, kr, vr, oa, ob]
    specs = [local, local, local, moved, moved, whole, whole]
    aliases = {}
    if so_far is not None:
        aliases = {len(operands): 0}
        operands.append(so_far)
        specs.append(pl.BlockSpec(memory_space=pl.ANY))
    return pl.pallas_call(
        functools.partial(final_kernel, heads),
        grid_spec=pltpu.PrefetchScalarGridSpec(
            num_scalar_prefetch=1,
            grid=(heads,),
            in_specs=specs,
            out_specs=local,
            scratch_shapes=[pltpu.VMEM((HD, rows), F32), pltpu.VMEM((1, rows), F32)],
        ),
        out_shape=jax.ShapeDtypeStruct((rows, chans), BF16),
        input_output_aliases=aliases,
        compiler_params=ceil_params(),
        cost_estimate=estimate(heads * 4 * HD * rows * rows, 14 * rows * width, heads * rows * rows),
        name="final_part",
    )(*operands)


def attention_four(attn_q, attn_k, attn_v, place, chunks):
    moved = []
    offset = 0
    for heads in chunks:
        cols = slice(offset * HD, (offset + heads) * HD)
        query, key, value = attn_q[:, cols], attn_k[:, cols], attn_v[:, cols]
        moved.append(
            (
                offset,
                lax.ppermute(query, "seq", [(2, 1), (3, 2)]),
                lax.ppermute(query, "seq", [(3, 1)]),
                lax.ppermute(key, "seq", [(0, 1)]),
                lax.ppermute(value, "seq", [(0, 1)]),
            )
        )
        offset += heads
    returned = []
    for offset, qa, qb, kr, vr in moved:
        oa, ob = remote_part(place, offset, qa, qb, kr, vr, attn_k, attn_v)
        returned.append(
            (
                offset,
                kr,
                vr,
                lax.ppermute(oa, "seq", [(1, 2), (2, 3)]),
                lax.ppermute(ob, "seq", [(1, 3)]),
            )
        )
    out = None
    for offset, kr, vr, oa, ob in returned:
        out = final_part(place, offset, attn_q, attn_k, attn_v, kr, vr, oa, ob, out)
    return out


def gathered_kernel(place_ref, q_ref, k_ref, v_ref, out_ref, top_ref, total_ref, mixed_ref):
    shard = pl.program_id(1)
    place = place_ref[0]

    @pl.when(shard == 0)
    def _():
        top_ref[...] = jnp.full(top_ref.shape, NEG, F32)
        total_ref[...] = jnp.zeros(total_ref.shape, F32)
        mixed_ref[...] = jnp.zeros(mixed_ref.shape, F32)

    def update(scores):
        top = jnp.maximum(top_ref[...], jnp.max(scores, axis=0, keepdims=True) * SCALE2)
        weights = jnp.exp2(scores * SCALE2 - top)
        keep = jnp.exp2(top_ref[...] - top)
        total_ref[...] = keep * total_ref[...] + jnp.sum(weights, axis=0, keepdims=True)
        mixed_ref[...] = keep * mixed_ref[...] + weighted(v_ref[...], weights.astype(BF16))
        top_ref[...] = top

    @pl.when(shard < place)
    def _():
        update(scores_of(k_ref[...], q_ref[...]))

    @pl.when(shard == place)
    def _():
        update(causal_scores(k_ref[...], q_ref[...], 0))
        out_ref[...] = (mixed_ref[...] / total_ref[...]).T.astype(BF16)


def attention_gathered(attn_q, attn_k, attn_v, place):
    rows, chans = attn_q.shape
    shards = lax.axis_size("seq")
    key = lax.all_gather(attn_k, "seq", axis=0, tiled=True)
    value = lax.all_gather(attn_v, "seq", axis=0, tiled=True)
    own = pl.BlockSpec((rows, HD), lambda h, s, p: (0, h))
    other = pl.BlockSpec((rows, HD), lambda h, s, p: (jnp.minimum(s, p[0]), h))
    return pl.pallas_call(
        gathered_kernel,
        grid_spec=pltpu.PrefetchScalarGridSpec(
            num_scalar_prefetch=1,
            grid=(chans // HD, shards),
            in_specs=[own, other, other],
            out_specs=own,
            scratch_shapes=[
                pltpu.VMEM((1, rows), F32),
                pltpu.VMEM((1, rows), F32),
                pltpu.VMEM((HD, rows), F32),
            ],
        ),
        out_shape=jax.ShapeDtypeStruct((rows, chans), BF16),
        compiler_params=ceil_params(),
        name="gathered_part",
    )(place, attn_q, key, value)


def split_heads(heads):
    if heads == 8:
        return (2, 3, 3)
    return tuple(min(2, heads - start) for start in range(0, heads, 2))


def per_device(
    hyena_q, hyena_k, hyena_v, short_filter, long_filter, skip_bias, attn_q, attn_k, attn_v
):
    shards = lax.axis_size("seq")
    place = lax.axis_index("seq").astype(jnp.int32).reshape(1)
    halo = halo_pack(hyena_q, hyena_k, hyena_v, short_filter)
    halo = lax.ppermute(halo, "seq", [(s, s + 1) for s in range(shards - 1)])
    hyena_out = hyena_mix(
        hyena_q, hyena_k, hyena_v, halo, short_filter, long_filter.T, skip_bias[None]
    )
    if shards == 4:
        attn_out = attention_four(
            attn_q, attn_k, attn_v, place, split_heads(attn_q.shape[1] // HD)
        )
    else:
        attn_out = attention_gathered(attn_q, attn_k, attn_v, place)
    return hyena_out, attn_out


def solution(mesh):
    both = P(("grp", "seq"), ("mp", "rep"))
    in_specs = (
        both,
        both,
        both,
        P(None, None, ("mp", "rep")),
        P(None, ("mp", "rep")),
        P(("mp", "rep")),
        both,
        both,
        both,
    )
    return jax.shard_map(
        per_device, mesh=mesh, in_specs=in_specs, out_specs=(both, both), check_vma=False
    )
```

```python
import functools

import jax
import jax.numpy as jnp
from jax import lax
from jax.experimental import pallas as pl
from jax.experimental.pallas import tpu as pltpu
from jax.sharding import PartitionSpec as P

HD = 128
FILT = 128
SHORT = 3
GSIZE = 16
LANES = 128
TAIL = 16
STATS = 16
MiB = 1 << 20
LOG2E = 1.4426950408889634
SCALE2 = HD**-0.5 * LOG2E
NEG = -1e30
F32 = jnp.float32
BF16 = jnp.bfloat16


def ceil_params(limit=16):
    return pltpu.CompilerParams(vmem_limit_bytes=limit * MiB)


def estimate(flops, moved, exps=0):
    return pl.CostEstimate(flops=int(flops), bytes_accessed=int(moved), transcendentals=int(exps))


def short_conv(extended, taps, keep):
    total = taps[0][None] * extended
    total = total + taps[1][None] * pltpu.roll(extended, 1, 0)
    total = total + taps[2][None] * pltpu.roll(extended, 2, 0)
    return total[keep:]


def halo_kernel(q_ref, k_ref, v_ref, taps_ref, out_ref):
    rows = k_ref.shape[0]
    first = rows - FILT - TAIL
    k_in = k_ref[first:].astype(F32)
    v_in = v_ref[first:].astype(F32)
    k_conv = short_conv(k_in, taps_ref[1], TAIL)
    v_conv = short_conv(v_in, taps_ref[2], TAIL)
    out_ref[:FILT] = (k_conv * v_conv).astype(BF16)
    q_tail = q_ref[rows - TAIL :].astype(F32)
    k_tail = pltpu.roll(k_in[FILT:], TAIL - 2, 0)
    v_tail = pltpu.roll(v_in[FILT:], TAIL - 4, 0)
    row = lax.broadcasted_iota(jnp.int32, q_tail.shape, 0)
    packed = jnp.where(row >= TAIL - 2, q_tail, jnp.where(row >= TAIL - 4, k_tail, v_tail))
    out_ref[FILT:] = packed.astype(BF16)


def halo_pack(hyena_q, hyena_k, hyena_v, short_filter):
    rows, chans = hyena_q.shape
    width = min(256, chans)
    tail_rows = 256
    tail = pl.BlockSpec((tail_rows, width), lambda i: (rows // tail_rows - 1, i))
    return pl.pallas_call(
        halo_kernel,
        grid=(chans // width,),
        in_specs=[tail, tail, tail, pl.BlockSpec((3, SHORT, width), lambda i: (0, 0, i))],
        out_specs=pl.BlockSpec((FILT + TAIL, width), lambda i: (0, i)),
        out_shape=jax.ShapeDtypeStruct((FILT + TAIL, chans), BF16),
        compiler_params=ceil_params(16),
        cost_estimate=estimate(20 * FILT * chans, 2 * 4 * FILT * chans),
        name="halo_pack",
    )(hyena_q, hyena_k, hyena_v, short_filter)


def hyena_kernel(
    q_ref, k_ref, v_ref, upper_ref, lower_ref, taps_ref, filt_ref, skip_ref, out_ref, long_ref
):
    rows = q_ref.shape[0]
    blocks = rows // FILT
    halo = upper_ref[...].astype(F32) + lower_ref[...].astype(F32)
    tail = halo[FILT:]
    tails = (tail, pltpu.roll(tail, 2, 0), pltpu.roll(tail, 4, 0))

    def conv(which, ref):
        extended = jnp.concatenate([tails[which], ref[...].astype(F32)], axis=0)
        return short_conv(extended, taps_ref[which], TAIL)

    gated = (conv(1, k_ref) * conv(2, v_ref)).astype(BF16).astype(F32)
    signal = jnp.concatenate([halo[:FILT], gated], axis=0)
    signal = signal.T.astype(BF16)
    source = lax.broadcasted_iota(jnp.int32, (FILT, FILT), 0)
    target = lax.broadcasted_iota(jnp.int32, (FILT, FILT), 1)
    near = target >= source
    for group in range(LANES // GSIZE):
        taps = jnp.broadcast_to(filt_ref[group : group + 1], (FILT, FILT))
        turned = pltpu.roll(taps, 0, 1, stride=1, stride_axis=0)
        table = jnp.concatenate(
            [jnp.where(near, 0.0, turned), jnp.where(near, turned, 0.0)], axis=0
        ).astype(BF16)
        band = signal[group * GSIZE : (group + 1) * GSIZE]
        stacked = jnp.concatenate(
            [band[:, b * FILT : (b + 2) * FILT] for b in range(blocks)], axis=0
        )
        result = jnp.dot(stacked, table, preferred_element_type=F32)
        for b in range(blocks):
            long_ref[group * GSIZE : (group + 1) * GSIZE, b * FILT : (b + 1) * FILT] = result[
                b * GSIZE : (b + 1) * GSIZE
            ]
    long_conv = long_ref[...].T
    mixed = conv(0, q_ref) * (long_conv + skip_ref[...] * gated)
    out_ref[...] = mixed.astype(BF16)


def hyena_mix(hyena_q, hyena_k, hyena_v, upper, lower, short_filter, filter_rows, skip_row):
    rows, chans = hyena_q.shape
    tile = pl.BlockSpec((rows, LANES), lambda i: (0, i))
    return pl.pallas_call(
        hyena_kernel,
        grid=(chans // LANES,),
        in_specs=[
            tile,
            tile,
            tile,
            pl.BlockSpec((FILT + TAIL, LANES), lambda i: (0, i)),
            pl.BlockSpec((FILT + TAIL, LANES), lambda i: (0, i)),
            pl.BlockSpec((3, SHORT, LANES), lambda i: (0, 0, i)),
            pl.BlockSpec((LANES // GSIZE, FILT), lambda i: (i, 0)),
            pl.BlockSpec((1, LANES), lambda i: (0, i)),
        ],
        out_specs=tile,
        out_shape=jax.ShapeDtypeStruct((rows, chans), BF16),
        scratch_shapes=[pltpu.VMEM((LANES, rows), F32)],
        compiler_params=ceil_params(16),
        cost_estimate=estimate(2 * rows * chans * 256 * 8, 8 * rows * chans),
        name="hyena_mix",
    )(hyena_q, hyena_k, hyena_v, upper, lower, short_filter, filter_rows, skip_row)


def in_vmem():
    return pl.BlockSpec(memory_space=pltpu.VMEM)


def in_hbm(value):
    return pltpu.with_memory_space_constraint(value, pltpu.HBM)


def after(value, *others):
    return lax.optimization_barrier((value, *others))[0]


def scores_of(key, query):
    return lax.dot_general(key, query, (((1,), (1,)), ((), ())), preferred_element_type=F32)


def weighted(value, probs):
    return lax.dot_general(value, probs, (((0,), (0,)), ((), ())), preferred_element_type=F32)


def causal_scores(key, query):
    scores = scores_of(key, query)
    key_pos = lax.broadcasted_iota(jnp.int32, scores.shape, 0)
    query_pos = lax.broadcasted_iota(jnp.int32, scores.shape, 1)
    return jnp.where(key_pos <= query_pos, scores, NEG)


def attend(query, blocks):
    top = None
    mixed = None
    for key, value, causal in blocks:
        scores = causal_scores(key, query) if causal else scores_of(key, query)
        block_top = jnp.max(scores, axis=0, keepdims=True) * SCALE2
        extended = jnp.concatenate([value, jnp.ones((value.shape[0], HD), BF16)], axis=1)
        if top is None:
            top = block_top
            mixed = weighted(extended, jnp.exp2(scores * SCALE2 - top).astype(BF16))
        else:
            new_top = jnp.maximum(top, block_top)
            keep = jnp.exp2(top - new_top)
            term = weighted(extended, jnp.exp2(scores * SCALE2 - new_top).astype(BF16))
            mixed = keep * mixed + term
            top = new_top
    total = mixed[HD : HD + 1]
    return mixed[:HD] / total, top + jnp.log2(total)


def split_kernel(rows, chunks, place_ref, q_ref, k_ref, v_ref, *rest):
    out_refs, sems = rest[:-1], rest[-1]
    copies = []

    def send(source, head, target, slot):
        copies.append(
            pltpu.make_async_copy(
                source.at[:, pl.ds(head * HD, HD)],
                target.at[pl.ds(slot * rows, rows), :],
                sems.at[len(copies)],
            )
        )

    for index, (offset, heads) in enumerate(chunks):
        near_ref, far_ref, kv_ref = out_refs[3 * index : 3 * index + 3]
        for j in range(heads):
            send(q_ref, offset + j, near_ref, j)
            send(q_ref, offset + j, far_ref, j)
            send(k_ref, offset + j, kv_ref, 2 * j)
            send(v_ref, offset + j, kv_ref, 2 * j + 1)
    for copy in copies:
        copy.start()
    for copy in copies:
        copy.wait()


def split_heads_out(place, attn_q, attn_k, attn_v, chunks):
    rows = attn_q.shape[0]
    shapes = []
    for _, heads in chunks:
        shapes.extend([jax.ShapeDtypeStruct((heads * rows, HD), BF16)] * 2)
        shapes.append(jax.ShapeDtypeStruct((2 * heads * rows, HD), BF16))
    total = sum(heads for _, heads in chunks)
    return pl.pallas_call(
        functools.partial(split_kernel, rows, chunks),
        in_specs=[pl.BlockSpec(memory_space=pltpu.SMEM)] + [pl.BlockSpec(memory_space=pl.ANY)] * 3,
        out_specs=[in_vmem() for _ in shapes],
        out_shape=shapes,
        scratch_shapes=[pltpu.SemaphoreType.DMA((4 * total,))],
        compiler_params=ceil_params(),
        cost_estimate=estimate(0, 12 * rows * total * HD),
        name="split_heads",
    )(place, attn_q, attn_k, attn_v)


def head_rows(ref, slot, rows):
    return ref[slot * rows : (slot + 1) * rows]


def query_tile(rows):
    return min(256, rows)


def remote_kernel(heads, place_ref, qa_ref, qb_ref, kvr_ref, kv_ref, oa_ref, ob_ref, stat_a, stat_b):
    place = place_ref[0]
    rows = oa_ref.shape[1]
    tile = query_tile(rows)

    def fill(q_ref, kv_refs, o_ref, stat_ref):
        for head in range(heads):
            blocks = [
                (head_rows(ref, 2 * head, rows), head_rows(ref, 2 * head + 1, rows), False)
                for ref in kv_refs
            ]
            for start in range(0, rows, tile):
                query = q_ref[head * rows + start : head * rows + start + tile]
                mixed, level = attend(query, blocks)
                o_ref[head * HD : (head + 1) * HD, start : start + tile] = mixed.astype(BF16)
                stat_ref[head : head + 1, start : start + tile] = level

    def pack(stat_ref, o_ref):
        level = stat_ref[...]
        high = level.astype(BF16).astype(F32)
        middle = (level - high).astype(BF16).astype(F32)
        low = level - high - middle
        row = lax.broadcasted_iota(jnp.int32, level.shape, 0)
        first = jnp.where(row < 4, high, pltpu.roll(middle, 4, 0))
        o_ref[heads * HD :] = jnp.concatenate([first, low], axis=0).astype(BF16)

    @pl.when(place == 1)
    def _():
        fill(qa_ref, [kvr_ref, kv_ref], oa_ref, stat_a)
        fill(qb_ref, [kvr_ref, kv_ref], ob_ref, stat_b)
        pack(stat_a, oa_ref)
        pack(stat_b, ob_ref)

    @pl.when(place == 2)
    def _():
        fill(qa_ref, [kv_ref], oa_ref, stat_a)
        pack(stat_a, oa_ref)


def remote_part(place, rows, qa, qb, kvr, kv):
    heads = qa.shape[0] // rows
    width = heads * HD
    shape = jax.ShapeDtypeStruct((width + STATS, rows), BF16)
    return pl.pallas_call(
        functools.partial(remote_kernel, heads),
        in_specs=[pl.BlockSpec(memory_space=pltpu.SMEM)] + [in_vmem()] * 4,
        out_specs=(in_vmem(), in_vmem()),
        out_shape=(shape, shape),
        scratch_shapes=[pltpu.VMEM((8, rows), F32), pltpu.VMEM((8, rows), F32)],
        compiler_params=ceil_params(),
        cost_estimate=estimate(heads * 16 * HD * rows * rows, 16 * rows * width, heads * 4 * rows * rows),
        name="remote_part",
    )(place, qa, qb, kvr, kv)


def level_row(stats, head):
    row = lax.broadcasted_iota(jnp.int32, stats.shape, 0)
    chosen = (row == head) | (row == head + 4) | (row == head + 8)
    return jnp.sum(jnp.where(chosen, stats, 0.0), axis=0, keepdims=True)


def final_kernel(sizes, first, aliased, place_ref, *rest):
    count = len(sizes)
    groups = [rest[5 * i : 5 * i + 5] for i in range(count)]
    out_ref, mixed_ref, level_ref, ready_ref, sem = rest[5 * count + aliased :]
    place = place_ref[0]
    rows = mixed_ref.shape[1]
    tile = query_tile(rows)
    column = 0
    for heads, (q_ref, kv_ref, kvr_ref, oa_ref, ob_ref) in zip(sizes, groups):
        for head in range(heads):
            for start in range(0, rows, tile):
                cols = slice(start, start + tile)
                query = q_ref[head * rows + start : head * rows + start + tile]
                key = head_rows(kv_ref, 2 * head, rows)
                value = head_rows(kv_ref, 2 * head + 1, rows)
                blocks = [(key[cols], value[cols], True)]
                if start:
                    blocks.append((key[:start], value[:start], False))
                passed = (
                    head_rows(kvr_ref, 2 * head, rows),
                    head_rows(kvr_ref, 2 * head + 1, rows),
                    False,
                )

                def run(these, cols=cols, query=query):
                    mixed, level = attend(query, these)
                    mixed_ref[:, cols] = mixed
                    level_ref[:, cols] = level

                pl.when(place == 1)(functools.partial(run, blocks + [passed]))
                pl.when(place != 1)(functools.partial(run, blocks))

            def merge(o_ref, head=head, heads=heads):
                other = o_ref[head * HD : (head + 1) * HD].astype(F32)
                other_level = level_row(o_ref[heads * HD :].astype(F32), head)
                level = level_ref[...]
                top = jnp.maximum(level, other_level)
                mine = jnp.exp2(level - top)
                theirs = jnp.exp2(other_level - top)
                both = mine + theirs
                mixed_ref[...] = mixed_ref[...] * (mine / both) + other * (theirs / both)
                level_ref[...] = top + jnp.log2(both)

            pl.when(place >= 2)(functools.partial(merge, oa_ref))
            pl.when(place >= 3)(functools.partial(merge, ob_ref))
            ready_ref[:, column * HD : (column + 1) * HD] = mixed_ref[...].T.astype(BF16)
            column += 1
    copy = pltpu.make_async_copy(
        ready_ref, out_ref.at[:, pl.ds(first * HD, column * HD)], sem
    )
    copy.start()
    copy.wait()


def final_part(place, rows, chans, first, groups, so_far):
    sizes = tuple(group[0].shape[0] // rows for group in groups)
    total = sum(sizes)
    operands = [place] + [value for group in groups for value in group]
    specs = [pl.BlockSpec(memory_space=pltpu.SMEM)] + [in_vmem()] * (5 * len(groups))
    aliases = {}
    if so_far is not None:
        aliases = {len(operands): 0}
        operands.append(so_far)
        specs.append(pl.BlockSpec(memory_space=pl.ANY))
    return pl.pallas_call(
        functools.partial(final_kernel, sizes, first, len(aliases)),
        in_specs=specs,
        out_specs=pl.BlockSpec(memory_space=pl.ANY),
        out_shape=jax.ShapeDtypeStruct((rows, chans), BF16),
        scratch_shapes=[
            pltpu.VMEM((HD, rows), F32),
            pltpu.VMEM((1, rows), F32),
            pltpu.VMEM((rows, total * HD), BF16),
            pltpu.SemaphoreType.DMA,
        ],
        input_output_aliases=aliases,
        compiler_params=ceil_params(),
        cost_estimate=estimate(total * 4 * HD * rows * rows, 14 * rows * total * HD, total * rows * rows),
        name="final_part",
    )(*operands)


def attention_four(attn_q, attn_k, attn_v, place, halo, hyena):
    rows, chans = attn_q.shape
    heads = chans // HD
    size = heads // 4
    arrays = tuple(in_hbm(value) for value in (attn_q, attn_k, attn_v))
    q0, far0, kv0, q1, far1, kv1, q2, far2, kv2, q3, far3, kv3 = split_heads_out(
        place, *arrays, [(size * c, size) for c in range(4)]
    )

    def to_hub(value):
        return lax.ppermute(value, "seq", [(2, 1), (3, 2)])

    def to_hub_far(value):
        return lax.ppermute(value, "seq", [(3, 1)])

    def keys_up(value):
        return lax.ppermute(value, "seq", [(0, 1)])

    def back(value):
        return lax.ppermute(value, "seq", [(1, 2), (2, 3)])

    def back_far(value):
        return lax.ppermute(value, "seq", [(1, 3)])

    qa0, qb0, kvr0 = to_hub(q0), to_hub_far(far0), keys_up(kv0)
    upper = lax.ppermute(after(halo, q0), "seq", [(1, 2), (2, 3)])
    qa1, kvr1 = to_hub(after(q1, qa0)), keys_up(after(kv1, qa0))
    qb1 = to_hub_far(after(far1, qb0, upper))
    oa0, ob0 = remote_part(place, rows, qa0, qb0, kvr0, kv0)
    ra0, rb0 = back(oa0), back_far(ob0)
    qa2 = to_hub(after(q2, qa1, oa0))
    qb2, kvr2 = to_hub_far(after(far2, qb1, kvr1, oa0)), keys_up(after(kv2, qb1, kvr1, oa0))
    oa1, ob1 = remote_part(place, rows, qa1, qb1, kvr1, kv1)
    ra1, rb1 = back(after(oa1, ra0)), back_far(after(ob1, rb0))
    qa3 = to_hub(after(q3, qa2, oa1))
    qb3, kvr3 = to_hub_far(after(far3, qb2, kvr2, oa1)), keys_up(after(kv3, qb2, kvr2, oa1))
    oa2, ob2 = remote_part(place, rows, qa2, qb2, kvr2, kv2)
    ra2, rb2 = back(after(oa2, ra1)), back_far(after(ob2, rb1))
    lower = lax.ppermute(after(halo, qa3, qb2, oa2), "seq", [(0, 1)])
    oa3, ob3 = remote_part(place, rows, qa3, qb3, kvr3, kv3)
    ra3, rb3 = back(after(oa3, ra2)), back_far(after(ob3, rb2))
    hyena_out = hyena(after(upper, oa3), lower)
    groups = [
        (q0, kv0, kvr0, ra0, rb0),
        (q1, kv1, kvr1, ra1, rb1),
        (q2, kv2, kvr2, ra2, rb2),
    ]
    out = final_part(place, rows, chans, 0, groups, None)
    out = final_part(place, rows, chans, 3 * size, [(q3, kv3, kvr3, ra3, rb3)], out)
    return out, hyena_out


def gathered_kernel(place_ref, q_ref, k_ref, v_ref, out_ref, top_ref, total_ref, mixed_ref):
    shard = pl.program_id(1)
    place = place_ref[0]

    @pl.when(shard == 0)
    def _():
        top_ref[...] = jnp.full(top_ref.shape, NEG, F32)
        total_ref[...] = jnp.zeros(total_ref.shape, F32)
        mixed_ref[...] = jnp.zeros(mixed_ref.shape, F32)

    def update(scores):
        top = jnp.maximum(top_ref[...], jnp.max(scores, axis=0, keepdims=True) * SCALE2)
        weights = jnp.exp2(scores * SCALE2 - top)
        keep = jnp.exp2(top_ref[...] - top)
        total_ref[...] = keep * total_ref[...] + jnp.sum(weights, axis=0, keepdims=True)
        mixed_ref[...] = keep * mixed_ref[...] + weighted(v_ref[...], weights.astype(BF16))
        top_ref[...] = top

    @pl.when(shard < place)
    def _():
        update(scores_of(k_ref[...], q_ref[...]))

    @pl.when(shard == place)
    def _():
        update(causal_scores(k_ref[...], q_ref[...]))
        out_ref[...] = (mixed_ref[...] / total_ref[...]).T.astype(BF16)


def attention_gathered(attn_q, attn_k, attn_v, place):
    rows, chans = attn_q.shape
    shards = lax.axis_size("seq")
    key = lax.all_gather(attn_k, "seq", axis=0, tiled=True)
    value = lax.all_gather(attn_v, "seq", axis=0, tiled=True)
    own = pl.BlockSpec((rows, HD), lambda h, s, p: (0, h))
    other = pl.BlockSpec((rows, HD), lambda h, s, p: (jnp.minimum(s, p[0]), h))
    return pl.pallas_call(
        gathered_kernel,
        grid_spec=pltpu.PrefetchScalarGridSpec(
            num_scalar_prefetch=1,
            grid=(chans // HD, shards),
            in_specs=[own, other, other],
            out_specs=own,
            scratch_shapes=[
                pltpu.VMEM((1, rows), F32),
                pltpu.VMEM((1, rows), F32),
                pltpu.VMEM((HD, rows), F32),
            ],
        ),
        out_shape=jax.ShapeDtypeStruct((rows, chans), BF16),
        compiler_params=ceil_params(),
        name="gathered_part",
    )(place, attn_q, key, value)


def per_device(
    hyena_q, hyena_k, hyena_v, short_filter, long_filter, skip_bias, attn_q, attn_k, attn_v
):
    shards = lax.axis_size("seq")
    heads = attn_q.shape[1] // HD
    place = lax.axis_index("seq").astype(jnp.int32).reshape(1)
    arrays = tuple(in_hbm(value) for value in (hyena_q, hyena_k, hyena_v))
    halo = halo_pack(*arrays, short_filter)

    def hyena(upper, lower):
        return hyena_mix(*arrays, upper, lower, short_filter, long_filter.T, skip_bias[None])

    if shards == 4 and heads in (4, 8, 12, 16):
        attn_out, hyena_out = attention_four(attn_q, attn_k, attn_v, place, halo, hyena)
    else:
        upper = lax.ppermute(halo, "seq", [(s, s + 1) for s in range(1, shards - 1)])
        lower = lax.ppermute(halo, "seq", [(0, 1)] if shards > 1 else [])
        hyena_out = hyena(upper, lower)
        attn_out = attention_gathered(attn_q, attn_k, attn_v, place)
    return hyena_out, attn_out


def solution(mesh):
    both = P(("grp", "seq"), ("mp", "rep"))
    in_specs = (
        both,
        both,
        both,
        P(None, None, ("mp", "rep")),
        P(None, ("mp", "rep")),
        P(("mp", "rep")),
        both,
        both,
        both,
    )
    return jax.shard_map(
        per_device, mesh=mesh, in_specs=in_specs, out_specs=(both, both), check_vma=False
    )
```

```python
import functools

import jax
import jax.numpy as jnp
from jax import lax
from jax.experimental import pallas as pl
from jax.experimental.pallas import tpu as pltpu
from jax.sharding import PartitionSpec as P

HD = 128
FILT = 128
SHORT = 3
GSIZE = 16
LANES = 128
TAIL = 16
STATS = 16
MiB = 1 << 20
LOG2E = 1.4426950408889634
SCALE2 = HD**-0.5 * LOG2E
NEG = -1e30
F32 = jnp.float32
BF16 = jnp.bfloat16


def ceil_params(limit=16):
    return pltpu.CompilerParams(vmem_limit_bytes=limit * MiB)


def estimate(flops, moved):
    return pl.CostEstimate(flops=int(flops) // 1000, bytes_accessed=int(moved) // 1000, transcendentals=0)


def short_conv(extended, taps, keep):
    total = taps[0][None] * extended
    total = total + taps[1][None] * pltpu.roll(extended, 1, 0)
    total = total + taps[2][None] * pltpu.roll(extended, 2, 0)
    return total[keep:]


def halo_kernel(q_ref, k_ref, v_ref, taps_ref, out_ref):
    rows = k_ref.shape[0]
    first = rows - FILT - TAIL
    k_in = k_ref[first:].astype(F32)
    v_in = v_ref[first:].astype(F32)
    k_conv = short_conv(k_in, taps_ref[1], TAIL)
    v_conv = short_conv(v_in, taps_ref[2], TAIL)
    out_ref[:FILT] = (k_conv * v_conv).astype(BF16)
    q_tail = q_ref[rows - TAIL :].astype(F32)
    k_tail = pltpu.roll(k_in[FILT:], TAIL - 2, 0)
    v_tail = pltpu.roll(v_in[FILT:], TAIL - 4, 0)
    row = lax.broadcasted_iota(jnp.int32, q_tail.shape, 0)
    packed = jnp.where(row >= TAIL - 2, q_tail, jnp.where(row >= TAIL - 4, k_tail, v_tail))
    out_ref[FILT:] = packed.astype(BF16)


def halo_pack(hyena_q, hyena_k, hyena_v, short_filter):
    rows, chans = hyena_q.shape
    width = min(256, chans)
    tail_rows = 256
    tail = pl.BlockSpec((tail_rows, width), lambda i: (rows // tail_rows - 1, i))
    return pl.pallas_call(
        halo_kernel,
        grid=(chans // width,),
        in_specs=[tail, tail, tail, pl.BlockSpec((3, SHORT, width), lambda i: (0, 0, i))],
        out_specs=pl.BlockSpec((FILT + TAIL, width), lambda i: (0, i)),
        out_shape=jax.ShapeDtypeStruct((FILT + TAIL, chans), BF16),
        compiler_params=ceil_params(16),
        cost_estimate=estimate(20 * FILT * chans, 2 * 4 * FILT * chans),
        name="halo_pack",
    )(hyena_q, hyena_k, hyena_v, short_filter)


def hyena_kernel(
    q_ref, k_ref, v_ref, upper_ref, lower_ref, taps_ref, filt_ref, skip_ref, out_ref, long_ref
):
    rows = q_ref.shape[0]
    blocks = rows // FILT
    halo = upper_ref[...].astype(F32) + lower_ref[...].astype(F32)
    tail = halo[FILT:]
    tails = (tail, pltpu.roll(tail, 2, 0), pltpu.roll(tail, 4, 0))

    def conv(which, ref):
        extended = jnp.concatenate([tails[which], ref[...].astype(F32)], axis=0)
        return short_conv(extended, taps_ref[which], TAIL)

    gated = (conv(1, k_ref) * conv(2, v_ref)).astype(BF16).astype(F32)
    signal = jnp.concatenate([halo[:FILT], gated], axis=0)
    signal = signal.T.astype(BF16)
    source = lax.broadcasted_iota(jnp.int32, (FILT, FILT), 0)
    target = lax.broadcasted_iota(jnp.int32, (FILT, FILT), 1)
    near = target >= source
    for group in range(LANES // GSIZE):
        taps = jnp.broadcast_to(filt_ref[group : group + 1], (FILT, FILT))
        turned = pltpu.roll(taps, 0, 1, stride=1, stride_axis=0)
        table = jnp.concatenate(
            [jnp.where(near, 0.0, turned), jnp.where(near, turned, 0.0)], axis=0
        ).astype(BF16)
        band = signal[group * GSIZE : (group + 1) * GSIZE]
        stacked = jnp.concatenate(
            [band[:, b * FILT : (b + 2) * FILT] for b in range(blocks)], axis=0
        )
        result = jnp.dot(stacked, table, preferred_element_type=F32)
        for b in range(blocks):
            long_ref[group * GSIZE : (group + 1) * GSIZE, b * FILT : (b + 1) * FILT] = result[
                b * GSIZE : (b + 1) * GSIZE
            ]
    long_conv = long_ref[...].T
    mixed = conv(0, q_ref) * (long_conv + skip_ref[...] * gated)
    out_ref[...] = mixed.astype(BF16)


def hyena_mix(hyena_q, hyena_k, hyena_v, upper, lower, short_filter, filter_rows, skip_row):
    rows, chans = hyena_q.shape
    tile = pl.BlockSpec((rows, LANES), lambda i: (0, i))
    return pl.pallas_call(
        hyena_kernel,
        grid=(chans // LANES,),
        in_specs=[
            tile,
            tile,
            tile,
            pl.BlockSpec((FILT + TAIL, LANES), lambda i: (0, i)),
            pl.BlockSpec((FILT + TAIL, LANES), lambda i: (0, i)),
            pl.BlockSpec((3, SHORT, LANES), lambda i: (0, 0, i)),
            pl.BlockSpec((LANES // GSIZE, FILT), lambda i: (i, 0)),
            pl.BlockSpec((1, LANES), lambda i: (0, i)),
        ],
        out_specs=tile,
        out_shape=jax.ShapeDtypeStruct((rows, chans), BF16),
        scratch_shapes=[pltpu.VMEM((LANES, rows), F32)],
        compiler_params=ceil_params(16),
        cost_estimate=estimate(2 * rows * chans * 256 * 8, 8 * rows * chans),
        name="hyena_mix",
    )(hyena_q, hyena_k, hyena_v, upper, lower, short_filter, filter_rows, skip_row)


def in_vmem():
    return pl.BlockSpec(memory_space=pltpu.VMEM)


def in_hbm(value):
    return pltpu.with_memory_space_constraint(value, pltpu.HBM)


def after(value, *others):
    return lax.optimization_barrier((value, *others))[0]


def scores_of(key, query):
    return lax.dot_general(key, query, (((1,), (1,)), ((), ())), preferred_element_type=F32)


def weighted(value, probs):
    return lax.dot_general(value, probs, (((0,), (0,)), ((), ())), preferred_element_type=F32)


def causal_scores(key, query):
    scores = scores_of(key, query)
    key_pos = lax.broadcasted_iota(jnp.int32, scores.shape, 0)
    query_pos = lax.broadcasted_iota(jnp.int32, scores.shape, 1)
    return jnp.where(key_pos <= query_pos, scores, NEG)


def attend(query, blocks):
    top = None
    mixed = None
    for key, value, causal in blocks:
        scores = causal_scores(key, query) if causal else scores_of(key, query)
        block_top = jnp.max(scores, axis=0, keepdims=True) * SCALE2
        extended = jnp.concatenate([value, jnp.ones((value.shape[0], HD), BF16)], axis=1)
        if top is None:
            top = block_top
            mixed = weighted(extended, jnp.exp2(scores * SCALE2 - top).astype(BF16))
        else:
            new_top = jnp.maximum(top, block_top)
            keep = jnp.exp2(top - new_top)
            term = weighted(extended, jnp.exp2(scores * SCALE2 - new_top).astype(BF16))
            mixed = keep * mixed + term
            top = new_top
    total = mixed[HD : HD + 1]
    return mixed[:HD] / total, top + jnp.log2(total)


def split_kernel(rows, chunks, place_ref, q_ref, k_ref, v_ref, *rest):
    out_refs, sems = rest[:-1], rest[-1]
    copies = []

    def send(source, head, target, slot):
        copies.append(
            pltpu.make_async_copy(
                source.at[:, pl.ds(head * HD, HD)],
                target.at[pl.ds(slot * rows, rows), :],
                sems.at[len(copies)],
            )
        )

    for index, (offset, heads) in enumerate(chunks):
        query_ref, kv_ref = out_refs[2 * index : 2 * index + 2]
        for j in range(heads):
            send(q_ref, offset + j, query_ref, j)
            send(k_ref, offset + j, kv_ref, 2 * j)
            send(v_ref, offset + j, kv_ref, 2 * j + 1)
    for copy in copies:
        copy.start()
    for copy in copies:
        copy.wait()


def split_heads_out(place, attn_q, attn_k, attn_v, chunks):
    rows = attn_q.shape[0]
    shapes = []
    for _, heads in chunks:
        shapes.append(jax.ShapeDtypeStruct((heads * rows, HD), BF16))
        shapes.append(jax.ShapeDtypeStruct((2 * heads * rows, HD), BF16))
    total = sum(heads for _, heads in chunks)
    return pl.pallas_call(
        functools.partial(split_kernel, rows, chunks),
        in_specs=[pl.BlockSpec(memory_space=pltpu.SMEM)] + [pl.BlockSpec(memory_space=pl.ANY)] * 3,
        out_specs=[in_vmem() for _ in shapes],
        out_shape=shapes,
        scratch_shapes=[pltpu.SemaphoreType.DMA((3 * total,))],
        compiler_params=ceil_params(),
        cost_estimate=estimate(0, 12 * rows * total * HD),
        name="split_heads",
    )(place, attn_q, attn_k, attn_v)


def head_rows(ref, slot, rows):
    return ref[slot * rows : (slot + 1) * rows]


def query_tile(rows):
    return min(256, rows)


def remote_kernel(heads, place_ref, qa_ref, qb_ref, kvr_ref, kv_ref, oa_ref, ob_ref, stat_a, stat_b):
    place = place_ref[0]
    rows = oa_ref.shape[1]
    tile = query_tile(rows)

    def fill(q_ref, kv_refs, o_ref, stat_ref):
        for head in range(heads):
            blocks = [
                (head_rows(ref, 2 * head, rows), head_rows(ref, 2 * head + 1, rows), False)
                for ref in kv_refs
            ]
            for start in range(0, rows, tile):
                query = q_ref[head * rows + start : head * rows + start + tile]
                mixed, level = attend(query, blocks)
                o_ref[head * HD : (head + 1) * HD, start : start + tile] = mixed.astype(BF16)
                stat_ref[head : head + 1, start : start + tile] = level

    def pack(stat_ref, o_ref):
        level = stat_ref[...]
        high = level.astype(BF16).astype(F32)
        middle = (level - high).astype(BF16).astype(F32)
        low = level - high - middle
        row = lax.broadcasted_iota(jnp.int32, level.shape, 0)
        first = jnp.where(row < 4, high, pltpu.roll(middle, 4, 0))
        o_ref[heads * HD :] = jnp.concatenate([first, low], axis=0).astype(BF16)

    @pl.when(place == 1)
    def _():
        fill(qa_ref, [kvr_ref, kv_ref], oa_ref, stat_a)
        fill(qb_ref, [kvr_ref, kv_ref], ob_ref, stat_b)
        pack(stat_a, oa_ref)
        pack(stat_b, ob_ref)

    @pl.when(place == 2)
    def _():
        fill(qa_ref, [kv_ref], oa_ref, stat_a)
        pack(stat_a, oa_ref)


def remote_part(place, rows, qa, qb, kvr, kv):
    heads = qa.shape[0] // rows
    width = heads * HD
    shape = jax.ShapeDtypeStruct((width + STATS, rows), BF16)
    return pl.pallas_call(
        functools.partial(remote_kernel, heads),
        in_specs=[pl.BlockSpec(memory_space=pltpu.SMEM)] + [in_vmem()] * 4,
        out_specs=(in_vmem(), in_vmem()),
        out_shape=(shape, shape),
        scratch_shapes=[pltpu.VMEM((8, rows), F32), pltpu.VMEM((8, rows), F32)],
        compiler_params=ceil_params(),
        cost_estimate=estimate(heads * 16 * HD * rows * rows, 16 * rows * width),
        name="remote_part",
    )(place, qa, qb, kvr, kv)


def level_row(stats, head):
    row = lax.broadcasted_iota(jnp.int32, stats.shape, 0)
    chosen = (row == head) | (row == head + 4) | (row == head + 8)
    return jnp.sum(jnp.where(chosen, stats, 0.0), axis=0, keepdims=True)


def own_kernel(sizes, *rest):
    count = len(sizes)
    mixed_ref, level_ref = rest[2 * count :]
    rows = mixed_ref.shape[1]
    tile = query_tile(rows)
    column = 0
    for index, heads in enumerate(sizes):
        q_ref, kv_ref = rest[2 * index : 2 * index + 2]
        for head in range(heads):
            key = head_rows(kv_ref, 2 * head, rows)
            value = head_rows(kv_ref, 2 * head + 1, rows)
            for start in range(0, rows, tile):
                cols = slice(start, start + tile)
                query = q_ref[head * rows + start : head * rows + start + tile]
                blocks = [(key[cols], value[cols], True)]
                if start:
                    blocks.append((key[:start], value[:start], False))
                mixed, level = attend(query, blocks)
                mixed_ref[column * HD : (column + 1) * HD, cols] = mixed
                level_ref[column : column + 1, cols] = level
            column += 1


def own_part(rows, messages):
    sizes = tuple(q.shape[0] // rows for q, _ in messages)
    total = sum(sizes)
    return pl.pallas_call(
        functools.partial(own_kernel, sizes),
        in_specs=[in_vmem()] * (2 * len(sizes)),
        out_specs=(in_vmem(), in_vmem()),
        out_shape=(
            jax.ShapeDtypeStruct((total * HD, rows), F32),
            jax.ShapeDtypeStruct((total, rows), F32),
        ),
        compiler_params=ceil_params(),
        cost_estimate=estimate(total * 3 * HD * rows * rows, 10 * rows * total * HD),
        name="own_part",
    )(*[value for pair in messages for value in pair])


def final_kernel(sizes, first, aliased, place_ref, own_ref, own_level_ref, *rest):
    count = len(sizes)
    groups = [rest[4 * i : 4 * i + 4] for i in range(count)]
    out_ref, mixed_ref, level_ref, ready_ref, sem = rest[4 * count + aliased :]
    place = place_ref[0]
    rows = mixed_ref.shape[1]
    tile = query_tile(rows)
    column = 0

    def merge(other, other_level, cols):
        level = level_ref[:, cols]
        top = jnp.maximum(level, other_level)
        mine = jnp.exp2(level - top)
        theirs = jnp.exp2(other_level - top)
        both = mine + theirs
        mixed_ref[:, cols] = mixed_ref[:, cols] * (mine / both) + other * (theirs / both)
        level_ref[:, cols] = top + jnp.log2(both)

    for heads, (q_ref, kvr_ref, oa_ref, ob_ref) in zip(sizes, groups):
        for head in range(heads):
            at = first + column
            mixed_ref[...] = own_ref[at * HD : (at + 1) * HD]
            level_ref[...] = own_level_ref[at : at + 1]

            def passed(head=head, q_ref=q_ref, kvr_ref=kvr_ref):
                block = (
                    head_rows(kvr_ref, 2 * head, rows),
                    head_rows(kvr_ref, 2 * head + 1, rows),
                    False,
                )
                for start in range(0, rows, tile):
                    query = q_ref[head * rows + start : head * rows + start + tile]
                    merge(*attend(query, [block]), slice(start, start + tile))

            def received(o_ref, head=head, heads=heads):
                merge(
                    o_ref[head * HD : (head + 1) * HD].astype(F32),
                    level_row(o_ref[heads * HD :].astype(F32), head),
                    slice(0, rows),
                )

            pl.when(place == 1)(passed)
            pl.when(place >= 2)(functools.partial(received, oa_ref))
            pl.when(place >= 3)(functools.partial(received, ob_ref))
            ready_ref[:, column * HD : (column + 1) * HD] = mixed_ref[...].T.astype(BF16)
            column += 1
    copy = pltpu.make_async_copy(
        ready_ref, out_ref.at[:, pl.ds(first * HD, column * HD)], sem
    )
    copy.start()
    copy.wait()


def final_part(place, rows, chans, first, own, groups, so_far):
    sizes = tuple(group[0].shape[0] // rows for group in groups)
    total = sum(sizes)
    operands = [place, *own] + [value for group in groups for value in group]
    specs = [pl.BlockSpec(memory_space=pltpu.SMEM)] + [in_vmem()] * (len(operands) - 1)
    aliases = {}
    if so_far is not None:
        aliases = {len(operands): 0}
        operands.append(so_far)
        specs.append(pl.BlockSpec(memory_space=pl.ANY))
    return pl.pallas_call(
        functools.partial(final_kernel, sizes, first, len(aliases)),
        in_specs=specs,
        out_specs=pl.BlockSpec(memory_space=pl.ANY),
        out_shape=jax.ShapeDtypeStruct((rows, chans), BF16),
        scratch_shapes=[
            pltpu.VMEM((HD, rows), F32),
            pltpu.VMEM((1, rows), F32),
            pltpu.VMEM((rows, total * HD), BF16),
            pltpu.SemaphoreType.DMA,
        ],
        input_output_aliases=aliases,
        compiler_params=ceil_params(),
        cost_estimate=estimate(total * 4 * HD * rows * rows, 14 * rows * total * HD),
        name="final_part",
    )(*operands)


def chunk_sizes(heads):
    base = heads // 3
    sizes = [base, base, base]
    for extra in range(heads - 3 * base):
        sizes[extra] += 1
    return sizes


def attention_four(attn_q, attn_k, attn_v, place, halo, hyena):
    rows, chans = attn_q.shape
    sizes = chunk_sizes(chans // HD)
    starts = [sum(sizes[:c]) for c in range(3)]
    arrays = tuple(in_hbm(value) for value in (attn_q, attn_k, attn_v))
    q0, kv0 = split_heads_out(place, *arrays, [(0, sizes[0])])
    q1, kv1, q2, kv2 = split_heads_out(place, *arrays, list(zip(starts, sizes))[1:])

    def to_hub(value):
        return lax.ppermute(value, "seq", [(2, 1), (3, 2)])

    def to_hub_far(value):
        return lax.ppermute(value, "seq", [(3, 1)])

    def keys_up(value):
        return lax.ppermute(value, "seq", [(0, 1)])

    def back(value):
        return lax.ppermute(value, "seq", [(1, 2), (2, 3)])

    def back_far(value):
        return lax.ppermute(value, "seq", [(1, 3)])

    qa0, qb0, kvr0 = to_hub(q0), to_hub_far(q0), keys_up(kv0)
    upper = lax.ppermute(halo, "seq", [(1, 2), (2, 3)])
    qa1, qb1 = to_hub(after(q1, upper)), to_hub_far(after(q1, upper))
    kvr1 = keys_up(after(kv1, qa0))
    own = own_part(rows, [(q0, kv0), (q1, kv1), (q2, after(kv2, qa0))])
    oa0, ob0 = remote_part(place, rows, qa0, qb0, after(kvr0, own[1], upper), kv0)
    ra0, rb0 = back(after(oa0, qa1)), back_far(after(ob0, qa1))
    qa2, qb2, kvr2 = (
        to_hub(after(q2, qa1, ra0)),
        to_hub_far(after(q2, qb1, ra0)),
        keys_up(after(kv2, kvr1, qb1, ra0)),
    )
    oa1, ob1 = remote_part(place, rows, qa1, qb1, kvr1, kv1)
    ra1, rb1 = back(after(oa1, ra0)), back_far(after(ob1, rb0))
    lower = lax.ppermute(after(halo, kvr2, oa1), "seq", [(0, 1)])
    oa2, ob2 = remote_part(place, rows, qa2, qb2, after(kvr2, oa1), kv2)
    ra2, rb2 = back(oa2), back_far(ob2)
    hyena_out = hyena(after(upper, oa2), lower)
    out = final_part(place, rows, chans, 0, own, [(q0, kvr0, ra0, rb0)], None)
    out, hyena_out = lax.optimization_barrier((out, hyena_out))
    out = final_part(place, rows, chans, starts[1], own, [(q1, kvr1, ra1, rb1)], out)
    out = final_part(place, rows, chans, starts[2], own, [(q2, kvr2, ra2, rb2)], out)
    return out, hyena_out


def gathered_kernel(place_ref, q_ref, k_ref, v_ref, out_ref, top_ref, total_ref, mixed_ref):
    shard = pl.program_id(1)
    place = place_ref[0]

    @pl.when(shard == 0)
    def _():
        top_ref[...] = jnp.full(top_ref.shape, NEG, F32)
        total_ref[...] = jnp.zeros(total_ref.shape, F32)
        mixed_ref[...] = jnp.zeros(mixed_ref.shape, F32)

    def update(scores):
        top = jnp.maximum(top_ref[...], jnp.max(scores, axis=0, keepdims=True) * SCALE2)
        weights = jnp.exp2(scores * SCALE2 - top)
        keep = jnp.exp2(top_ref[...] - top)
        total_ref[...] = keep * total_ref[...] + jnp.sum(weights, axis=0, keepdims=True)
        mixed_ref[...] = keep * mixed_ref[...] + weighted(v_ref[...], weights.astype(BF16))
        top_ref[...] = top

    @pl.when(shard < place)
    def _():
        update(scores_of(k_ref[...], q_ref[...]))

    @pl.when(shard == place)
    def _():
        update(causal_scores(k_ref[...], q_ref[...]))
        out_ref[...] = (mixed_ref[...] / total_ref[...]).T.astype(BF16)


def attention_gathered(attn_q, attn_k, attn_v, place):
    rows, chans = attn_q.shape
    shards = lax.axis_size("seq")
    key = lax.all_gather(attn_k, "seq", axis=0, tiled=True)
    value = lax.all_gather(attn_v, "seq", axis=0, tiled=True)
    own = pl.BlockSpec((rows, HD), lambda h, s, p: (0, h))
    other = pl.BlockSpec((rows, HD), lambda h, s, p: (jnp.minimum(s, p[0]), h))
    return pl.pallas_call(
        gathered_kernel,
        grid_spec=pltpu.PrefetchScalarGridSpec(
            num_scalar_prefetch=1,
            grid=(chans // HD, shards),
            in_specs=[own, other, other],
            out_specs=own,
            scratch_shapes=[
                pltpu.VMEM((1, rows), F32),
                pltpu.VMEM((1, rows), F32),
                pltpu.VMEM((HD, rows), F32),
            ],
        ),
        out_shape=jax.ShapeDtypeStruct((rows, chans), BF16),
        compiler_params=ceil_params(),
        name="gathered_part",
    )(place, attn_q, key, value)


def per_device(
    hyena_q, hyena_k, hyena_v, short_filter, long_filter, skip_bias, attn_q, attn_k, attn_v
):
    shards = lax.axis_size("seq")
    heads = attn_q.shape[1] // HD
    place = lax.axis_index("seq").astype(jnp.int32).reshape(1)
    arrays = tuple(in_hbm(value) for value in (hyena_q, hyena_k, hyena_v))
    halo = halo_pack(*arrays, short_filter)

    def hyena(upper, lower):
        return hyena_mix(*arrays, upper, lower, short_filter, long_filter.T, skip_bias[None])

    if shards == 4 and 3 <= heads <= 12:
        attn_out, hyena_out = attention_four(attn_q, attn_k, attn_v, place, halo, hyena)
    else:
        upper = lax.ppermute(halo, "seq", [(s, s + 1) for s in range(1, shards - 1)])
        lower = lax.ppermute(halo, "seq", [(0, 1)] if shards > 1 else [])
        hyena_out = hyena(upper, lower)
        attn_out = attention_gathered(attn_q, attn_k, attn_v, place)
    return hyena_out, attn_out


def solution(mesh):
    both = P(("grp", "seq"), ("mp", "rep"))
    in_specs = (
        both,
        both,
        both,
        P(None, None, ("mp", "rep")),
        P(None, ("mp", "rep")),
        P(("mp", "rep")),
        both,
        both,
        both,
    )
    return jax.shard_map(
        per_device, mesh=mesh, in_specs=in_specs, out_specs=(both, both), check_vma=False
    )
```

```python
import functools

import jax
import jax.numpy as jnp
from jax import lax
from jax.experimental import pallas as pl
from jax.experimental.pallas import tpu as pltpu
from jax.sharding import PartitionSpec as P

HD = 128
FILT = 128
SHORT = 3
GSIZE = 16
LANES = 128
TAIL = 16
STATS = 16
MiB = 1 << 20
LOG2E = 1.4426950408889634
SCALE2 = HD**-0.5 * LOG2E
NEG = -1e30
F32 = jnp.float32
BF16 = jnp.bfloat16


def ceil_params(limit=16):
    return pltpu.CompilerParams(vmem_limit_bytes=limit * MiB)


def estimate(flops, moved):
    return pl.CostEstimate(flops=int(flops) // 1, bytes_accessed=int(moved) // 1, transcendentals=0)


def in_vmem():
    return pl.BlockSpec(memory_space=pltpu.VMEM)


def in_hbm(value):
    return pltpu.with_memory_space_constraint(value, pltpu.HBM)


def after(value, *others):
    return lax.optimization_barrier((value, *others))[0]


def short_conv(extended, taps, keep):
    total = taps[0][None] * extended
    total = total + taps[1][None] * pltpu.roll(extended, 1, 0)
    total = total + taps[2][None] * pltpu.roll(extended, 2, 0)
    return total[keep:]


def halo_kernel(q_hbm, k_hbm, v_hbm, taps_ref, out_ref, q_in, k_in, v_in, sems):
    rows = q_hbm.shape[0]
    reach = FILT + TAIL
    copies = [
        pltpu.make_async_copy(k_hbm.at[pl.ds(rows - reach, reach)], k_in, sems.at[0]),
        pltpu.make_async_copy(v_hbm.at[pl.ds(rows - reach, reach)], v_in, sems.at[1]),
        pltpu.make_async_copy(q_hbm.at[pl.ds(rows - TAIL, TAIL)], q_in, sems.at[2]),
    ]
    for copy in copies:
        copy.start()
    for copy in copies:
        copy.wait()
    for start in range(0, out_ref.shape[1], LANES):
        cols = slice(start, start + LANES)
        k_tile = k_in[:, cols].astype(F32)
        v_tile = v_in[:, cols].astype(F32)
        k_conv = short_conv(k_tile, taps_ref[1, :, cols], TAIL)
        v_conv = short_conv(v_tile, taps_ref[2, :, cols], TAIL)
        out_ref[:FILT, cols] = (k_conv * v_conv).astype(BF16)
        q_tail = q_in[:, cols].astype(F32)
        k_tail = pltpu.roll(k_tile[FILT:], TAIL - 2, 0)
        v_tail = pltpu.roll(v_tile[FILT:], TAIL - 4, 0)
        row = lax.broadcasted_iota(jnp.int32, q_tail.shape, 0)
        packed = jnp.where(row >= TAIL - 2, q_tail, jnp.where(row >= TAIL - 4, k_tail, v_tail))
        out_ref[FILT:, cols] = packed.astype(BF16)


def halo_pack(hyena_q, hyena_k, hyena_v, short_filter):
    rows, chans = hyena_q.shape
    whole = pl.BlockSpec(memory_space=pl.ANY)
    return pl.pallas_call(
        halo_kernel,
        in_specs=[whole, whole, whole, in_vmem()],
        out_specs=in_vmem(),
        out_shape=jax.ShapeDtypeStruct((FILT + TAIL, chans), BF16),
        scratch_shapes=[
            pltpu.VMEM((TAIL, chans), BF16),
            pltpu.VMEM((FILT + TAIL, chans), BF16),
            pltpu.VMEM((FILT + TAIL, chans), BF16),
            pltpu.SemaphoreType.DMA((3,)),
        ],
        compiler_params=ceil_params(16),
        cost_estimate=estimate(20 * FILT * chans, 2 * 4 * FILT * chans),
        name="halo_pack",
    )(hyena_q, hyena_k, hyena_v, short_filter)


def hyena_kernel(late, q_ref, k_ref, v_ref, taps_ref, filt_ref, skip_ref, *rest):
    out_ref, long_ref, ready_ref, sem = rest[-4:]
    rows, chans = q_ref.shape
    half = rows // 2
    blocks = half // FILT
    groups = LANES // GSIZE
    source = lax.broadcasted_iota(jnp.int32, (FILT, FILT), 0)
    target = lax.broadcasted_iota(jnp.int32, (FILT, FILT), 1)
    near = target >= source

    def one_tile(index, carry):
        cols = pl.ds(pl.multiple_of(index * LANES, LANES), LANES)
        if late:
            halo = rest[0][:, cols].astype(F32) + rest[1][:, cols].astype(F32)
            tail = halo[FILT:]
            tails = (tail, pltpu.roll(tail, 2, 0), pltpu.roll(tail, 4, 0))

        def conv(which, ref, reach):
            if late:
                signal = jnp.concatenate([tails[which], ref[:half, cols].astype(F32)], axis=0)
            else:
                signal = ref[half - reach - TAIL :, cols].astype(F32)
            return short_conv(signal, taps_ref[which, :, cols], TAIL)

        product = (conv(1, k_ref, FILT) * conv(2, v_ref, FILT)).astype(BF16).astype(F32)
        if late:
            gated = product
            signal = jnp.concatenate([halo[:FILT], gated], axis=0)
        else:
            gated = product[FILT:]
            signal = product
        signal = signal.T.astype(BF16)
        filters = filt_ref[pl.ds(pl.multiple_of(index * groups, groups), groups), :]
        for group in range(groups):
            taps = jnp.broadcast_to(filters[group : group + 1], (8, FILT))
            base = pltpu.roll(taps, 0, 1, stride=1, stride_axis=0)
            turned = jnp.concatenate(
                [base] + [pltpu.roll(base, s, 1) for s in range(8, FILT, 8)], axis=0
            )
            table = jnp.concatenate(
                [jnp.where(near, 0.0, turned), jnp.where(near, turned, 0.0)], axis=0
            ).astype(BF16)
            band = signal[group * GSIZE : (group + 1) * GSIZE]
            stacked = jnp.concatenate(
                [band[:, b * FILT : (b + 2) * FILT] for b in range(blocks)], axis=0
            )
            result = jnp.dot(stacked, table, preferred_element_type=F32)
            for b in range(blocks):
                long_ref[
                    group * GSIZE : (group + 1) * GSIZE, b * FILT : (b + 1) * FILT
                ] = result[b * GSIZE : (b + 1) * GSIZE]
        long_conv = long_ref[...].T
        mixed = conv(0, q_ref, 0) * (long_conv + skip_ref[:, cols] * gated)
        ready_ref[:, cols] = mixed.astype(BF16)
        return carry

    lax.fori_loop(0, chans // LANES, one_tile, 0)
    copy = pltpu.make_async_copy(
        ready_ref, out_ref.at[pl.ds(0 if late else half, half), :], sem
    )
    copy.start()
    copy.wait()


def hyena_half(hyena_q, hyena_k, hyena_v, short_filter, filter_rows, skip_row, halos, so_far):
    rows, chans = hyena_q.shape
    late = so_far is not None
    half = rows // 2
    operands = [hyena_q, hyena_k, hyena_v, short_filter, filter_rows, skip_row, *halos]
    specs = [in_vmem()] * len(operands)
    aliases = {}
    if late:
        aliases = {len(operands): 0}
        operands.append(so_far)
        specs.append(pl.BlockSpec(memory_space=pl.ANY))
    return pl.pallas_call(
        functools.partial(hyena_kernel, late),
        in_specs=specs,
        out_specs=pl.BlockSpec(memory_space=pl.ANY),
        out_shape=jax.ShapeDtypeStruct((rows, chans), BF16),
        scratch_shapes=[
            pltpu.VMEM((LANES, half), F32),
            pltpu.VMEM((half, chans), BF16),
            pltpu.SemaphoreType.DMA,
        ],
        input_output_aliases=aliases,
        compiler_params=ceil_params(16),
        cost_estimate=estimate(rows * chans * 256 * 8, 8 * rows * chans),
        name="hyena_late" if late else "hyena_early",
    )(*operands)


def scores_of(key, query):
    return lax.dot_general(key, query, (((1,), (1,)), ((), ())), preferred_element_type=F32)


def weighted(value, probs):
    return lax.dot_general(value, probs, (((0,), (0,)), ((), ())), preferred_element_type=F32)


def causal_scores(key, query):
    scores = scores_of(key, query)
    key_pos = lax.broadcasted_iota(jnp.int32, scores.shape, 0)
    query_pos = lax.broadcasted_iota(jnp.int32, scores.shape, 1)
    return jnp.where(key_pos <= query_pos, scores, NEG)


def attend(query, blocks):
    top = None
    mixed = None
    for key, value, causal in blocks:
        scores = causal_scores(key, query) if causal else scores_of(key, query)
        block_top = jnp.max(scores, axis=0, keepdims=True) * SCALE2
        extended = jnp.concatenate([value, jnp.ones((value.shape[0], HD), BF16)], axis=1)
        if top is None:
            top = block_top
            mixed = weighted(extended, jnp.exp2(scores * SCALE2 - top).astype(BF16))
        else:
            new_top = jnp.maximum(top, block_top)
            keep = jnp.exp2(top - new_top)
            term = weighted(extended, jnp.exp2(scores * SCALE2 - new_top).astype(BF16))
            mixed = keep * mixed + term
            top = new_top
    total = mixed[HD : HD + 1]
    return mixed[:HD] / total, top + jnp.log2(total)


def split_kernel(rows, chunks, place_ref, q_ref, k_ref, v_ref, *rest):
    out_refs, sems = rest[:-1], rest[-1]
    copies = []

    def send(source, head, target, slot):
        copies.append(
            pltpu.make_async_copy(
                source.at[:, pl.ds(head * HD, HD)],
                target.at[pl.ds(slot * rows, rows), :],
                sems.at[len(copies)],
            )
        )

    for index, (offset, heads) in enumerate(chunks):
        query_ref, kv_ref = out_refs[2 * index : 2 * index + 2]
        for j in range(heads):
            send(q_ref, offset + j, query_ref, j)
            send(k_ref, offset + j, kv_ref, 2 * j)
            send(v_ref, offset + j, kv_ref, 2 * j + 1)
    for copy in copies:
        copy.start()
    for copy in copies:
        copy.wait()


def split_heads_out(place, attn_q, attn_k, attn_v, chunks):
    rows = attn_q.shape[0]
    shapes = []
    for _, heads in chunks:
        shapes.append(jax.ShapeDtypeStruct((heads * rows, HD), BF16))
        shapes.append(jax.ShapeDtypeStruct((2 * heads * rows, HD), BF16))
    total = sum(heads for _, heads in chunks)
    return pl.pallas_call(
        functools.partial(split_kernel, rows, chunks),
        in_specs=[pl.BlockSpec(memory_space=pltpu.SMEM)] + [pl.BlockSpec(memory_space=pl.ANY)] * 3,
        out_specs=[in_vmem() for _ in shapes],
        out_shape=shapes,
        scratch_shapes=[pltpu.SemaphoreType.DMA((3 * total,))],
        compiler_params=ceil_params(),
        cost_estimate=estimate(0, 12 * rows * total * HD),
        name="split_heads",
    )(place, attn_q, attn_k, attn_v)


def head_rows(ref, slot, rows):
    return ref[slot * rows : (slot + 1) * rows]


def query_tile(rows):
    return min(256, rows)


def remote_kernel(heads, far, place_ref, q_ref, kvr_ref, kv_ref, o_ref, stat_ref):
    place = place_ref[0]
    rows = o_ref.shape[1]
    tile = query_tile(rows)

    def fill(kv_refs):
        for head in range(heads):
            blocks = [
                (head_rows(ref, 2 * head, rows), head_rows(ref, 2 * head + 1, rows), False)
                for ref in kv_refs
            ]
            for start in range(0, rows, tile):
                query = q_ref[head * rows + start : head * rows + start + tile]
                mixed, level = attend(query, blocks)
                o_ref[head * HD : (head + 1) * HD, start : start + tile] = mixed.astype(BF16)
                stat_ref[head : head + 1, start : start + tile] = level
        level = stat_ref[...]
        high = level.astype(BF16).astype(F32)
        middle = (level - high).astype(BF16).astype(F32)
        low = level - high - middle
        row = lax.broadcasted_iota(jnp.int32, level.shape, 0)
        first = jnp.where(row < 4, high, pltpu.roll(middle, 4, 0))
        o_ref[heads * HD :] = jnp.concatenate([first, low], axis=0).astype(BF16)

    @pl.when(place == 1)
    def _():
        fill([kvr_ref, kv_ref])

    if not far:

        @pl.when(place == 2)
        def _():
            fill([kv_ref])


def remote_part(place, rows, far, q, kvr, kv):
    heads = q.shape[0] // rows
    width = heads * HD
    return pl.pallas_call(
        functools.partial(remote_kernel, heads, far),
        in_specs=[pl.BlockSpec(memory_space=pltpu.SMEM)] + [in_vmem()] * 3,
        out_specs=in_vmem(),
        out_shape=jax.ShapeDtypeStruct((width + STATS, rows), BF16),
        scratch_shapes=[pltpu.VMEM((8, rows), F32)],
        compiler_params=ceil_params(),
        cost_estimate=estimate(heads * 8 * HD * rows * rows, 10 * rows * width),
        name="remote_far" if far else "remote_near",
    )(place, q, kvr, kv)


def level_row(stats, head):
    row = lax.broadcasted_iota(jnp.int32, stats.shape, 0)
    chosen = (row == head) | (row == head + 4) | (row == head + 8)
    return jnp.sum(jnp.where(chosen, stats, 0.0), axis=0, keepdims=True)


def own_kernel(sizes, *rest):
    count = len(sizes)
    mixed_ref, level_ref = rest[2 * count :]
    rows = mixed_ref.shape[1]
    tile = query_tile(rows)
    column = 0
    for index, heads in enumerate(sizes):
        q_ref, kv_ref = rest[2 * index : 2 * index + 2]
        for head in range(heads):
            key = head_rows(kv_ref, 2 * head, rows)
            value = head_rows(kv_ref, 2 * head + 1, rows)
            for start in range(0, rows, tile):
                cols = slice(start, start + tile)
                query = q_ref[head * rows + start : head * rows + start + tile]
                blocks = [(key[cols], value[cols], True)]
                if start:
                    blocks.append((key[:start], value[:start], False))
                mixed, level = attend(query, blocks)
                mixed_ref[column * HD : (column + 1) * HD, cols] = mixed
                level_ref[column : column + 1, cols] = level
            column += 1


def own_part(rows, messages):
    sizes = tuple(q.shape[0] // rows for q, _ in messages)
    total = sum(sizes)
    return pl.pallas_call(
        functools.partial(own_kernel, sizes),
        in_specs=[in_vmem()] * (2 * len(sizes)),
        out_specs=(in_vmem(), in_vmem()),
        out_shape=(
            jax.ShapeDtypeStruct((total * HD, rows), F32),
            jax.ShapeDtypeStruct((total, rows), F32),
        ),
        compiler_params=ceil_params(),
        cost_estimate=estimate(total * 3 * HD * rows * rows, 10 * rows * total * HD),
        name="own_part",
    )(*[value for pair in messages for value in pair])


def final_kernel(sizes, first, aliased, place_ref, own_ref, own_level_ref, *rest):
    count = len(sizes)
    groups = [rest[4 * i : 4 * i + 4] for i in range(count)]
    out_ref, mixed_ref, level_ref, ready_ref, sem = rest[4 * count + aliased :]
    place = place_ref[0]
    rows = mixed_ref.shape[1]
    tile = query_tile(rows)
    column = 0

    def merge(other, other_level, cols):
        level = level_ref[:, cols]
        top = jnp.maximum(level, other_level)
        mine = jnp.exp2(level - top)
        theirs = jnp.exp2(other_level - top)
        both = mine + theirs
        mixed_ref[:, cols] = mixed_ref[:, cols] * (mine / both) + other * (theirs / both)
        level_ref[:, cols] = top + jnp.log2(both)

    for heads, (q_ref, kvr_ref, oa_ref, ob_ref) in zip(sizes, groups):
        for head in range(heads):
            at = first + column
            mixed_ref[...] = own_ref[at * HD : (at + 1) * HD]
            level_ref[...] = own_level_ref[at : at + 1]

            def passed(head=head, q_ref=q_ref, kvr_ref=kvr_ref):
                block = (
                    head_rows(kvr_ref, 2 * head, rows),
                    head_rows(kvr_ref, 2 * head + 1, rows),
                    False,
                )
                for start in range(0, rows, tile):
                    query = q_ref[head * rows + start : head * rows + start + tile]
                    merge(*attend(query, [block]), slice(start, start + tile))

            def received(o_ref, head=head, heads=heads):
                merge(
                    o_ref[head * HD : (head + 1) * HD].astype(F32),
                    level_row(o_ref[heads * HD :].astype(F32), head),
                    slice(0, rows),
                )

            pl.when(place == 1)(passed)
            pl.when(place >= 2)(functools.partial(received, oa_ref))
            pl.when(place >= 3)(functools.partial(received, ob_ref))
            ready_ref[:, column * HD : (column + 1) * HD] = mixed_ref[...].T.astype(BF16)
            column += 1
    copy = pltpu.make_async_copy(
        ready_ref, out_ref.at[:, pl.ds(first * HD, column * HD)], sem
    )
    copy.start()
    copy.wait()


def final_part(place, rows, chans, first, own, groups, so_far):
    sizes = tuple(group[0].shape[0] // rows for group in groups)
    total = sum(sizes)
    operands = [place, *own] + [value for group in groups for value in group]
    specs = [pl.BlockSpec(memory_space=pltpu.SMEM)] + [in_vmem()] * (len(operands) - 1)
    aliases = {}
    if so_far is not None:
        aliases = {len(operands): 0}
        operands.append(so_far)
        specs.append(pl.BlockSpec(memory_space=pl.ANY))
    return pl.pallas_call(
        functools.partial(final_kernel, sizes, first, len(aliases)),
        in_specs=specs,
        out_specs=pl.BlockSpec(memory_space=pl.ANY),
        out_shape=jax.ShapeDtypeStruct((rows, chans), BF16),
        scratch_shapes=[
            pltpu.VMEM((HD, rows), F32),
            pltpu.VMEM((1, rows), F32),
            pltpu.VMEM((rows, total * HD), BF16),
            pltpu.SemaphoreType.DMA,
        ],
        input_output_aliases=aliases,
        compiler_params=ceil_params(),
        cost_estimate=estimate(total * 4 * HD * rows * rows, 14 * rows * total * HD),
        name="final_part",
    )(*operands)


def chunk_sizes(heads):
    parts = 3
    base = heads // parts
    return [base + (part < heads - parts * base) for part in range(parts)]


def attention_four(attn_q, attn_k, attn_v, place, halo, hyena, early):
    rows, chans = attn_q.shape
    sizes = chunk_sizes(chans // HD)
    starts = [sum(sizes[:c]) for c in range(len(sizes))]
    arrays = tuple(in_hbm(value) for value in (attn_q, attn_k, attn_v))
    q0, kv0 = split_heads_out(place, *arrays, [(0, sizes[0])])
    rest = split_heads_out(place, *arrays, list(zip(starts, sizes))[1:])
    q, kv = [q0, *rest[0::2]], [kv0, *rest[1::2]]

    def to_hub(value):
        return lax.ppermute(value, "seq", [(2, 1), (3, 2)])

    def to_hub_far(value):
        return lax.ppermute(value, "seq", [(3, 1)])

    def keys_up(value):
        return lax.ppermute(value, "seq", [(0, 1)])

    def back(value):
        return lax.ppermute(value, "seq", [(1, 2), (2, 3)])

    def back_far(value):
        return lax.ppermute(value, "seq", [(1, 3)])

    count = len(sizes)
    upper = lax.ppermute(halo, "seq", [(1, 2), (2, 3)])
    kvr, qb, qa = [keys_up(kv[0])], [to_hub_far(q[0])], [to_hub(q[0])]
    oa, ob, ra, rb = [], [], [], []

    def work(c, gate):
        far = remote_part(place, rows, True, qb[c], after(kvr[c], gate), kv[c])
        ob.append(far)
        rb.append(back_far(after(far, rb[c - 1]) if c else far))
        gates = (far, rb[c - 1]) if c else (far,)
        near = remote_part(place, rows, False, qa[c], after(kvr[c], *gates), kv[c])
        oa.append(near)
        if c == 1:
            near = after(near, qb[2])
        ra.append(back(after(near, ra[c - 1]) if c else near))

    own_in = list(zip(q, kv))
    own_in[-1] = (q[-1], kv[-1])
    own = own_part(rows, own_in)
    own, early, halo_ready = lax.optimization_barrier((own, early, halo))
    qb.append(to_hub_far(q[1]))
    kvr.append(keys_up(kv[1]))
    work(0, own[1])
    qa.append(to_hub(after(q[1], ob[0])))
    kvr.append(keys_up(after(kv[2], kvr[1], qb[1], oa[0])))
    qb.append(to_hub_far(after(q[2], kvr[1], qb[1], oa[0])))
    work(1, oa[0])
    qa.append(to_hub(after(q[2], oa[1])))
    lower = lax.ppermute(after(halo, kvr[2], oa[1]), "seq", [(0, 1)])

    def finish(c, so_far):
        return final_part(place, rows, chans, starts[c], own, [(q[c], kvr[c], ra[c], rb[c])], so_far)

    out = finish(0, None)
    work(2, oa[1])
    out = finish(1, out)
    hyena_out = hyena((after(upper, oa[-1], out), lower), early)
    out, hyena_out = lax.optimization_barrier((out, hyena_out))
    out = finish(2, out)
    return out, hyena_out


def gathered_kernel(place_ref, q_ref, k_ref, v_ref, out_ref, top_ref, total_ref, mixed_ref):
    shard = pl.program_id(1)
    place = place_ref[0]

    @pl.when(shard == 0)
    def _():
        top_ref[...] = jnp.full(top_ref.shape, NEG, F32)
        total_ref[...] = jnp.zeros(total_ref.shape, F32)
        mixed_ref[...] = jnp.zeros(mixed_ref.shape, F32)

    def update(scores):
        top = jnp.maximum(top_ref[...], jnp.max(scores, axis=0, keepdims=True) * SCALE2)
        weights = jnp.exp2(scores * SCALE2 - top)
        keep = jnp.exp2(top_ref[...] - top)
        total_ref[...] = keep * total_ref[...] + jnp.sum(weights, axis=0, keepdims=True)
        mixed_ref[...] = keep * mixed_ref[...] + weighted(v_ref[...], weights.astype(BF16))
        top_ref[...] = top

    @pl.when(shard < place)
    def _():
        update(scores_of(k_ref[...], q_ref[...]))

    @pl.when(shard == place)
    def _():
        update(causal_scores(k_ref[...], q_ref[...]))
        out_ref[...] = (mixed_ref[...] / total_ref[...]).T.astype(BF16)


def attention_gathered(attn_q, attn_k, attn_v, place):
    rows, chans = attn_q.shape
    shards = lax.axis_size("seq")
    key = lax.all_gather(attn_k, "seq", axis=0, tiled=True)
    value = lax.all_gather(attn_v, "seq", axis=0, tiled=True)
    own = pl.BlockSpec((rows, HD), lambda h, s, p: (0, h))
    other = pl.BlockSpec((rows, HD), lambda h, s, p: (jnp.minimum(s, p[0]), h))
    return pl.pallas_call(
        gathered_kernel,
        grid_spec=pltpu.PrefetchScalarGridSpec(
            num_scalar_prefetch=1,
            grid=(chans // HD, shards),
            in_specs=[own, other, other],
            out_specs=own,
            scratch_shapes=[
                pltpu.VMEM((1, rows), F32),
                pltpu.VMEM((1, rows), F32),
                pltpu.VMEM((HD, rows), F32),
            ],
        ),
        out_shape=jax.ShapeDtypeStruct((rows, chans), BF16),
        compiler_params=ceil_params(),
        name="gathered_part",
    )(place, attn_q, key, value)


def per_device(
    hyena_q, hyena_k, hyena_v, short_filter, long_filter, skip_bias, attn_q, attn_k, attn_v
):
    shards = lax.axis_size("seq")
    heads = attn_q.shape[1] // HD
    place = lax.axis_index("seq").astype(jnp.int32).reshape(1)
    arrays = tuple(in_hbm(value) for value in (hyena_q, hyena_k, hyena_v))
    halo = halo_pack(*arrays, short_filter)

    filter_rows, skip_row = long_filter.T, skip_bias[None]

    def hyena(halos, so_far):
        return hyena_half(
            hyena_q, hyena_k, hyena_v, short_filter, filter_rows, skip_row, halos, so_far
        )

    early = hyena((), None)
    if shards == 4 and 2 <= heads <= 8:
        attn_out, hyena_out = attention_four(attn_q, attn_k, attn_v, place, halo, hyena, early)
    else:
        upper = lax.ppermute(halo, "seq", [(s, s + 1) for s in range(1, shards - 1)])
        lower = lax.ppermute(halo, "seq", [(0, 1)] if shards > 1 else [])
        hyena_out = hyena((upper, lower), early)
        attn_out = attention_gathered(attn_q, attn_k, attn_v, place)
    return hyena_out, attn_out


def solution(mesh):
    both = P(("grp", "seq"), ("mp", "rep"))
    in_specs = (
        both,
        both,
        both,
        P(None, None, ("mp", "rep")),
        P(None, ("mp", "rep")),
        P(("mp", "rep")),
        both,
        both,
        both,
    )
    return jax.shard_map(
        per_device, mesh=mesh, in_specs=in_specs, out_specs=(both, both), check_vma=False
    )
```

```python
import functools

import jax
import jax.numpy as jnp
from jax import lax
from jax.experimental import pallas as pl
from jax.experimental.pallas import tpu as pltpu
from jax.sharding import PartitionSpec as P

HD = 128
FILT = 128
SHORT = 3
GSIZE = 16
LANES = 128
TAIL = 16
STATS = 16
MiB = 1 << 20
LOG2E = 1.4426950408889634
SCALE2 = HD**-0.5 * LOG2E
NEG = -1e30
F32 = jnp.float32
BF16 = jnp.bfloat16


def ceil_params(limit=16):
    return pltpu.CompilerParams(vmem_limit_bytes=limit * MiB)


def estimate(flops, moved):
    return pl.CostEstimate(flops=int(flops) // 1, bytes_accessed=int(moved) // 1, transcendentals=0)


def in_vmem():
    return pl.BlockSpec(memory_space=pltpu.VMEM)


def in_hbm(value):
    return pltpu.with_memory_space_constraint(value, pltpu.HBM)


def after(value, *others):
    return lax.optimization_barrier((value, *others))[0]


def short_conv(extended, taps, keep):
    total = taps[0][None] * extended
    total = total + taps[1][None] * pltpu.roll(extended, 1, 0)
    total = total + taps[2][None] * pltpu.roll(extended, 2, 0)
    return total[keep:]


def halo_kernel(q_hbm, k_hbm, v_hbm, taps_ref, out_ref, q_in, k_in, v_in, sems):
    rows = q_hbm.shape[0]
    reach = FILT + TAIL
    copies = [
        pltpu.make_async_copy(k_hbm.at[pl.ds(rows - reach, reach)], k_in, sems.at[0]),
        pltpu.make_async_copy(v_hbm.at[pl.ds(rows - reach, reach)], v_in, sems.at[1]),
        pltpu.make_async_copy(q_hbm.at[pl.ds(rows - TAIL, TAIL)], q_in, sems.at[2]),
    ]
    for copy in copies:
        copy.start()
    for copy in copies:
        copy.wait()
    for start in range(0, out_ref.shape[1], LANES):
        cols = slice(start, start + LANES)
        k_tile = k_in[:, cols].astype(F32)
        v_tile = v_in[:, cols].astype(F32)
        k_conv = short_conv(k_tile, taps_ref[1, :, cols], TAIL)
        v_conv = short_conv(v_tile, taps_ref[2, :, cols], TAIL)
        out_ref[:FILT, cols] = (k_conv * v_conv).astype(BF16)
        q_tail = q_in[:, cols].astype(F32)
        k_tail = pltpu.roll(k_tile[FILT:], TAIL - 2, 0)
        v_tail = pltpu.roll(v_tile[FILT:], TAIL - 4, 0)
        row = lax.broadcasted_iota(jnp.int32, q_tail.shape, 0)
        packed = jnp.where(row >= TAIL - 2, q_tail, jnp.where(row >= TAIL - 4, k_tail, v_tail))
        out_ref[FILT:, cols] = packed.astype(BF16)


def halo_pack(hyena_q, hyena_k, hyena_v, short_filter):
    rows, chans = hyena_q.shape
    whole = pl.BlockSpec(memory_space=pl.ANY)
    return pl.pallas_call(
        halo_kernel,
        in_specs=[whole, whole, whole, in_vmem()],
        out_specs=in_vmem(),
        out_shape=jax.ShapeDtypeStruct((FILT + TAIL, chans), BF16),
        scratch_shapes=[
            pltpu.VMEM((TAIL, chans), BF16),
            pltpu.VMEM((FILT + TAIL, chans), BF16),
            pltpu.VMEM((FILT + TAIL, chans), BF16),
            pltpu.SemaphoreType.DMA((3,)),
        ],
        compiler_params=ceil_params(16),
        cost_estimate=estimate(20 * FILT * chans, 2 * 4 * FILT * chans),
        name="halo_pack",
    )(hyena_q, hyena_k, hyena_v, short_filter)


def hyena_kernel(late, q_ref, k_ref, v_ref, taps_ref, filt_ref, skip_ref, *rest):
    long_ref, ready_ref, sem = rest[-3:]
    out_ref, table_ref = (rest[-4], rest[2]) if late else rest[:2]
    rows, chans = q_ref.shape
    half = rows // 2
    blocks = half // FILT
    groups = LANES // GSIZE
    source = lax.broadcasted_iota(jnp.int32, (FILT, FILT), 0)
    target = lax.broadcasted_iota(jnp.int32, (FILT, FILT), 1)
    near = target >= source

    def one_tile(index, carry):
        cols = pl.ds(pl.multiple_of(index * LANES, LANES), LANES)
        if late:
            halo = rest[0][:, cols].astype(F32) + rest[1][:, cols].astype(F32)
            tail = halo[FILT:]
            tails = (tail, pltpu.roll(tail, 2, 0), pltpu.roll(tail, 4, 0))

        def conv(which, ref, reach):
            if late:
                signal = jnp.concatenate([tails[which], ref[:half, cols].astype(F32)], axis=0)
            else:
                signal = ref[half - reach - TAIL :, cols].astype(F32)
            return short_conv(signal, taps_ref[which, :, cols], TAIL)

        product = (conv(1, k_ref, FILT) * conv(2, v_ref, FILT)).astype(BF16).astype(F32)
        if late:
            gated = product
            signal = jnp.concatenate([halo[:FILT], gated], axis=0)
        else:
            gated = product[FILT:]
            signal = product
        signal = signal.T.astype(BF16)
        if not late:
            filters = filt_ref[pl.ds(pl.multiple_of(index * groups, groups), groups), :]
        for group in range(groups):
            place = pl.multiple_of((index * groups + group) * 2 * FILT, 2 * FILT)
            if late:
                table = table_ref[pl.ds(place, 2 * FILT), :]
            else:
                taps = jnp.broadcast_to(filters[group : group + 1], (8, FILT))
                base = pltpu.roll(taps, 0, 1, stride=1, stride_axis=0)
                turned = jnp.concatenate(
                    [base] + [pltpu.roll(base, s, 1) for s in range(8, FILT, 8)], axis=0
                )
                table = jnp.concatenate(
                    [jnp.where(near, 0.0, turned), jnp.where(near, turned, 0.0)], axis=0
                ).astype(BF16)
                table_ref[pl.ds(place, 2 * FILT), :] = table
            band = signal[group * GSIZE : (group + 1) * GSIZE]
            stacked = jnp.concatenate(
                [band[:, b * FILT : (b + 2) * FILT] for b in range(blocks)], axis=0
            )
            result = jnp.dot(stacked, table, preferred_element_type=F32)
            for b in range(blocks):
                long_ref[
                    group * GSIZE : (group + 1) * GSIZE, b * FILT : (b + 1) * FILT
                ] = result[b * GSIZE : (b + 1) * GSIZE]
        long_conv = long_ref[...].T
        mixed = conv(0, q_ref, 0) * (long_conv + skip_ref[:, cols] * gated)
        ready_ref[:, cols] = mixed.astype(BF16)
        return carry

    lax.fori_loop(0, chans // LANES, one_tile, 0)
    copy = pltpu.make_async_copy(
        ready_ref, out_ref.at[pl.ds(0 if late else half, half), :], sem
    )
    copy.start()
    copy.wait()


def hyena_half(hyena_q, hyena_k, hyena_v, short_filter, filter_rows, skip_row, halos, so_far):
    rows, chans = hyena_q.shape
    late = so_far is not None
    half = rows // 2
    operands = [hyena_q, hyena_k, hyena_v, short_filter, filter_rows, skip_row, *halos]
    specs = [in_vmem()] * len(operands)
    aliases = {}
    outs = [pl.BlockSpec(memory_space=pl.ANY)]
    shapes = [jax.ShapeDtypeStruct((rows, chans), BF16)]
    if late:
        so_far, table = so_far
        operands.append(table)
        specs.append(in_vmem())
        aliases = {len(operands): 0}
        operands.append(so_far)
        specs.append(pl.BlockSpec(memory_space=pl.ANY))
    else:
        outs.append(in_vmem())
        shapes.append(jax.ShapeDtypeStruct((chans // GSIZE * 2 * FILT, FILT), BF16))
    return pl.pallas_call(
        functools.partial(hyena_kernel, late),
        in_specs=specs,
        out_specs=outs,
        out_shape=shapes,
        scratch_shapes=[
            pltpu.VMEM((LANES, half), F32),
            pltpu.VMEM((half, chans), BF16),
            pltpu.SemaphoreType.DMA,
        ],
        input_output_aliases=aliases,
        compiler_params=ceil_params(16),
        cost_estimate=estimate(rows * chans * 256 * 8, 8 * rows * chans),
        name="hyena_late" if late else "hyena_early",
    )(*operands)


def scores_of(key, query):
    return lax.dot_general(key, query, (((1,), (1,)), ((), ())), preferred_element_type=F32)


def weighted(value, probs):
    return lax.dot_general(value, probs, (((0,), (0,)), ((), ())), preferred_element_type=F32)


def causal_scores(key, query):
    scores = scores_of(key, query)
    key_pos = lax.broadcasted_iota(jnp.int32, scores.shape, 0)
    query_pos = lax.broadcasted_iota(jnp.int32, scores.shape, 1)
    return jnp.where(key_pos <= query_pos, scores, NEG)


def attend(query, blocks):
    top = None
    mixed = None
    for key, value, causal in blocks:
        scores = causal_scores(key, query) if causal else scores_of(key, query)
        block_top = jnp.max(scores, axis=0, keepdims=True) * SCALE2
        extended = jnp.concatenate([value, jnp.ones((value.shape[0], HD), BF16)], axis=1)
        if top is None:
            top = block_top
            mixed = weighted(extended, jnp.exp2(scores * SCALE2 - top).astype(BF16))
        else:
            new_top = jnp.maximum(top, block_top)
            keep = jnp.exp2(top - new_top)
            term = weighted(extended, jnp.exp2(scores * SCALE2 - new_top).astype(BF16))
            mixed = keep * mixed + term
            top = new_top
    total = mixed[HD : HD + 1]
    return mixed[:HD] / total, top + jnp.log2(total)


def split_kernel(rows, chunks, place_ref, q_ref, k_ref, v_ref, *rest):
    out_refs, sems = rest[:-1], rest[-1]
    copies = []

    def send(source, head, target, slot):
        copies.append(
            pltpu.make_async_copy(
                source.at[:, pl.ds(head * HD, HD)],
                target.at[pl.ds(slot * rows, rows), :],
                sems.at[len(copies)],
            )
        )

    for index, (offset, heads) in enumerate(chunks):
        query_ref, kv_ref = out_refs[2 * index : 2 * index + 2]
        for j in range(heads):
            send(q_ref, offset + j, query_ref, j)
            send(k_ref, offset + j, kv_ref, 2 * j)
            send(v_ref, offset + j, kv_ref, 2 * j + 1)
    for copy in copies:
        copy.start()
    for copy in copies:
        copy.wait()


def split_heads_out(place, attn_q, attn_k, attn_v, chunks):
    rows = attn_q.shape[0]
    shapes = []
    for _, heads in chunks:
        shapes.append(jax.ShapeDtypeStruct((heads * rows, HD), BF16))
        shapes.append(jax.ShapeDtypeStruct((2 * heads * rows, HD), BF16))
    total = sum(heads for _, heads in chunks)
    return pl.pallas_call(
        functools.partial(split_kernel, rows, chunks),
        in_specs=[pl.BlockSpec(memory_space=pltpu.SMEM)] + [pl.BlockSpec(memory_space=pl.ANY)] * 3,
        out_specs=[in_vmem() for _ in shapes],
        out_shape=shapes,
        scratch_shapes=[pltpu.SemaphoreType.DMA((3 * total,))],
        compiler_params=ceil_params(),
        cost_estimate=estimate(0, 12 * rows * total * HD),
        name="split_heads",
    )(place, attn_q, attn_k, attn_v)


def head_rows(ref, slot, rows):
    return ref[slot * rows : (slot + 1) * rows]


def query_tile(rows):
    return min(256, rows)


def remote_kernel(heads, far, place_ref, q_ref, kvr_ref, kv_ref, o_ref, stat_ref):
    place = place_ref[0]
    rows = o_ref.shape[1]
    tile = query_tile(rows)

    def fill(kv_refs):
        for head in range(heads):
            blocks = [
                (head_rows(ref, 2 * head, rows), head_rows(ref, 2 * head + 1, rows), False)
                for ref in kv_refs
            ]
            for start in range(0, rows, tile):
                query = q_ref[head * rows + start : head * rows + start + tile]
                mixed, level = attend(query, blocks)
                o_ref[head * HD : (head + 1) * HD, start : start + tile] = mixed.astype(BF16)
                stat_ref[head : head + 1, start : start + tile] = level
        level = stat_ref[...]
        high = level.astype(BF16).astype(F32)
        middle = (level - high).astype(BF16).astype(F32)
        low = level - high - middle
        row = lax.broadcasted_iota(jnp.int32, level.shape, 0)
        first = jnp.where(row < 4, high, pltpu.roll(middle, 4, 0))
        o_ref[heads * HD :] = jnp.concatenate([first, low], axis=0).astype(BF16)

    @pl.when(place == 1)
    def _():
        fill([kvr_ref, kv_ref])

    if not far:

        @pl.when(place == 2)
        def _():
            fill([kv_ref])


def remote_part(place, rows, far, q, kvr, kv):
    heads = q.shape[0] // rows
    width = heads * HD
    return pl.pallas_call(
        functools.partial(remote_kernel, heads, far),
        in_specs=[pl.BlockSpec(memory_space=pltpu.SMEM)] + [in_vmem()] * 3,
        out_specs=in_vmem(),
        out_shape=jax.ShapeDtypeStruct((width + STATS, rows), BF16),
        scratch_shapes=[pltpu.VMEM((8, rows), F32)],
        compiler_params=ceil_params(),
        cost_estimate=estimate(heads * 8 * HD * rows * rows, 10 * rows * width),
        name="remote_far" if far else "remote_near",
    )(place, q, kvr, kv)


def level_row(stats, head):
    row = lax.broadcasted_iota(jnp.int32, stats.shape, 0)
    chosen = (row == head) | (row == head + 4) | (row == head + 8)
    return jnp.sum(jnp.where(chosen, stats, 0.0), axis=0, keepdims=True)


def own_kernel(sizes, *rest):
    count = len(sizes)
    mixed_ref, level_ref = rest[2 * count :]
    rows = mixed_ref.shape[1]
    tile = query_tile(rows)
    column = 0
    for index, heads in enumerate(sizes):
        q_ref, kv_ref = rest[2 * index : 2 * index + 2]
        for head in range(heads):
            key = head_rows(kv_ref, 2 * head, rows)
            value = head_rows(kv_ref, 2 * head + 1, rows)
            for start in range(0, rows, tile):
                cols = slice(start, start + tile)
                query = q_ref[head * rows + start : head * rows + start + tile]
                blocks = [(key[cols], value[cols], True)]
                if start:
                    blocks.append((key[:start], value[:start], False))
                mixed, level = attend(query, blocks)
                mixed_ref[column * HD : (column + 1) * HD, cols] = mixed
                level_ref[column : column + 1, cols] = level
            column += 1


def own_part(rows, messages):
    sizes = tuple(q.shape[0] // rows for q, _ in messages)
    total = sum(sizes)
    return pl.pallas_call(
        functools.partial(own_kernel, sizes),
        in_specs=[in_vmem()] * (2 * len(sizes)),
        out_specs=(in_vmem(), in_vmem()),
        out_shape=(
            jax.ShapeDtypeStruct((total * HD, rows), F32),
            jax.ShapeDtypeStruct((total, rows), F32),
        ),
        compiler_params=ceil_params(),
        cost_estimate=estimate(total * 3 * HD * rows * rows, 10 * rows * total * HD),
        name="own_part",
    )(*[value for pair in messages for value in pair])


def passed_kernel(heads, place_ref, q_ref, kvr_ref, own_ref, own_level_ref, mixed_ref, level_ref):
    rows = mixed_ref.shape[1]
    tile = query_tile(rows)
    mixed_ref[...] = own_ref[: heads * HD]
    level_ref[...] = own_level_ref[:heads]

    @pl.when(place_ref[0] == 1)
    def _():
        for head in range(heads):
            at = slice(head * HD, (head + 1) * HD)
            block = (
                head_rows(kvr_ref, 2 * head, rows),
                head_rows(kvr_ref, 2 * head + 1, rows),
                False,
            )
            for start in range(0, rows, tile):
                cols = slice(start, start + tile)
                query = q_ref[head * rows + start : head * rows + start + tile]
                other, other_level = attend(query, [block])
                level = level_ref[head : head + 1, cols]
                top = jnp.maximum(level, other_level)
                mine = jnp.exp2(level - top)
                theirs = jnp.exp2(other_level - top)
                both = mine + theirs
                mixed_ref[at, cols] = mixed_ref[at, cols] * (mine / both) + other * (theirs / both)
                level_ref[head : head + 1, cols] = top + jnp.log2(both)


def passed_part(place, rows, q, kvr, own):
    heads = q.shape[0] // rows
    return pl.pallas_call(
        functools.partial(passed_kernel, heads),
        in_specs=[pl.BlockSpec(memory_space=pltpu.SMEM)] + [in_vmem()] * 4,
        out_specs=(in_vmem(), in_vmem()),
        out_shape=(
            jax.ShapeDtypeStruct((heads * HD, rows), F32),
            jax.ShapeDtypeStruct((heads, rows), F32),
        ),
        compiler_params=ceil_params(),
        cost_estimate=estimate(heads * 4 * HD * rows * rows, 10 * rows * heads * HD),
        name="passed_part",
    )(place, q, kvr, *own)


def final_kernel(sizes, first, aliased, passed_done, place_ref, own_ref, own_level_ref, *rest):
    count = len(sizes)
    groups = [rest[4 * i : 4 * i + 4] for i in range(count)]
    out_ref, mixed_ref, level_ref, ready_ref, sem = rest[4 * count + aliased :]
    place = place_ref[0]
    rows = mixed_ref.shape[1]
    tile = query_tile(rows)
    column = 0

    def merge(other, other_level, cols):
        level = level_ref[:, cols]
        top = jnp.maximum(level, other_level)
        mine = jnp.exp2(level - top)
        theirs = jnp.exp2(other_level - top)
        both = mine + theirs
        mixed_ref[:, cols] = mixed_ref[:, cols] * (mine / both) + other * (theirs / both)
        level_ref[:, cols] = top + jnp.log2(both)

    for heads, (q_ref, kvr_ref, oa_ref, ob_ref) in zip(sizes, groups):
        for head in range(heads):
            at = first + column
            mixed_ref[...] = own_ref[at * HD : (at + 1) * HD]
            level_ref[...] = own_level_ref[at : at + 1]

            def passed(head=head, q_ref=q_ref, kvr_ref=kvr_ref):
                block = (
                    head_rows(kvr_ref, 2 * head, rows),
                    head_rows(kvr_ref, 2 * head + 1, rows),
                    False,
                )
                for start in range(0, rows, tile):
                    query = q_ref[head * rows + start : head * rows + start + tile]
                    merge(*attend(query, [block]), slice(start, start + tile))

            def received(o_ref, head=head, heads=heads):
                merge(
                    o_ref[head * HD : (head + 1) * HD].astype(F32),
                    level_row(o_ref[heads * HD :].astype(F32), head),
                    slice(0, rows),
                )

            if not passed_done:
                pl.when(place == 1)(passed)
            pl.when(place >= 2)(functools.partial(received, oa_ref))
            pl.when(place >= 3)(functools.partial(received, ob_ref))
            ready_ref[:, column * HD : (column + 1) * HD] = mixed_ref[...].T.astype(BF16)
            column += 1
    copy = pltpu.make_async_copy(
        ready_ref, out_ref.at[:, pl.ds(first * HD, column * HD)], sem
    )
    copy.start()
    copy.wait()


def final_part(place, rows, chans, first, own, groups, so_far, passed_done=False):
    sizes = tuple(group[0].shape[0] // rows for group in groups)
    total = sum(sizes)
    operands = [place, *own] + [value for group in groups for value in group]
    specs = [pl.BlockSpec(memory_space=pltpu.SMEM)] + [in_vmem()] * (len(operands) - 1)
    aliases = {}
    if so_far is not None:
        aliases = {len(operands): 0}
        operands.append(so_far)
        specs.append(pl.BlockSpec(memory_space=pl.ANY))
    return pl.pallas_call(
        functools.partial(final_kernel, sizes, first, len(aliases), passed_done),
        in_specs=specs,
        out_specs=pl.BlockSpec(memory_space=pl.ANY),
        out_shape=jax.ShapeDtypeStruct((rows, chans), BF16),
        scratch_shapes=[
            pltpu.VMEM((HD, rows), F32),
            pltpu.VMEM((1, rows), F32),
            pltpu.VMEM((rows, total * HD), BF16),
            pltpu.SemaphoreType.DMA,
        ],
        input_output_aliases=aliases,
        compiler_params=ceil_params(),
        cost_estimate=estimate(total * 4 * HD * rows * rows, 14 * rows * total * HD),
        name="final_part",
    )(*operands)


def chunk_sizes(heads):
    parts = 3
    base = heads // parts
    return [base + (part < heads - parts * base) for part in range(parts)]


def attention_four(attn_q, attn_k, attn_v, place, halo, hyena, early):
    rows, chans = attn_q.shape
    sizes = chunk_sizes(chans // HD)
    starts = [sum(sizes[:c]) for c in range(len(sizes))]
    arrays = tuple(in_hbm(value) for value in (attn_q, attn_k, attn_v))
    q0, kv0 = split_heads_out(place, *arrays, [(0, sizes[0])])
    rest = split_heads_out(place, *arrays, list(zip(starts, sizes))[1:])
    q, kv = [q0, *rest[0::2]], [kv0, *rest[1::2]]

    def to_hub(value):
        return lax.ppermute(value, "seq", [(2, 1), (3, 2)])

    def to_hub_far(value):
        return lax.ppermute(value, "seq", [(3, 1)])

    def keys_up(value):
        return lax.ppermute(value, "seq", [(0, 1)])

    def back(value):
        return lax.ppermute(value, "seq", [(1, 2), (2, 3)])

    def back_far(value):
        return lax.ppermute(value, "seq", [(1, 3)])

    count = len(sizes)
    kvr, qb, qa = [keys_up(kv[0])], [to_hub_far(q[0])], [to_hub(q[0])]
    oa, ob, ra, rb = [], [], [], []

    def work(c, gate):
        far = remote_part(place, rows, True, qb[c], after(kvr[c], gate), kv[c])
        ob.append(far)
        rb.append(back_far(after(far, rb[c - 1]) if c else far))
        gates = (far, rb[c - 1]) if c else (far,)
        near = remote_part(place, rows, False, qa[c], after(kvr[c], *gates), kv[c])
        oa.append(near)
        if c == 1:
            near = after(near, qb[2], upper)
        ra.append(back(after(near, ra[c - 1]) if c == 1 else near))

    own_in = list(zip(q, kv))
    own_in[-1] = (q[-1], kv[-1])
    own = own_part(rows, own_in)
    own, early, halo_ready = lax.optimization_barrier((own, early, halo))
    qb.append(to_hub_far(q[1]))
    upper = lax.ppermute(after(halo, qb[1]), "seq", [(1, 2), (2, 3)])
    kvr.append(keys_up(kv[1]))
    work(0, own[1])
    qa.append(to_hub(after(q[1], ob[0])))
    own_first = passed_part(place, rows, q[0], after(kvr[0], oa[0]), own)
    kvr.append(keys_up(after(kv[2], kvr[1], qb[1], oa[0], own_first[1])))
    qb.append(to_hub_far(after(q[2], kvr[1], qb[1], oa[0], own_first[1])))
    work(1, own_first[1])
    qa.append(to_hub(after(q[2], oa[1])))
    lower = lax.ppermute(after(halo, kvr[2], oa[1]), "seq", [(0, 1)])

    def finish(c, so_far):
        return final_part(place, rows, chans, starts[c], own, [(q[c], kvr[c], ra[c], rb[c])], so_far)

    out = final_part(
        place, rows, chans, 0, own_first, [(q[0], kvr[0], ra[0], rb[0])], None, passed_done=True
    )
    work(2, oa[1])
    out = finish(1, out)
    (hyena_out,) = hyena((after(upper, oa[-1], out), lower), early)
    out, hyena_out = lax.optimization_barrier((out, hyena_out))
    out = finish(2, out)
    return out, hyena_out


def gathered_kernel(place_ref, q_ref, k_ref, v_ref, out_ref, top_ref, total_ref, mixed_ref):
    shard = pl.program_id(1)
    place = place_ref[0]

    @pl.when(shard == 0)
    def _():
        top_ref[...] = jnp.full(top_ref.shape, NEG, F32)
        total_ref[...] = jnp.zeros(total_ref.shape, F32)
        mixed_ref[...] = jnp.zeros(mixed_ref.shape, F32)

    def update(scores):
        top = jnp.maximum(top_ref[...], jnp.max(scores, axis=0, keepdims=True) * SCALE2)
        weights = jnp.exp2(scores * SCALE2 - top)
        keep = jnp.exp2(top_ref[...] - top)
        total_ref[...] = keep * total_ref[...] + jnp.sum(weights, axis=0, keepdims=True)
        mixed_ref[...] = keep * mixed_ref[...] + weighted(v_ref[...], weights.astype(BF16))
        top_ref[...] = top

    @pl.when(shard < place)
    def _():
        update(scores_of(k_ref[...], q_ref[...]))

    @pl.when(shard == place)
    def _():
        update(causal_scores(k_ref[...], q_ref[...]))
        out_ref[...] = (mixed_ref[...] / total_ref[...]).T.astype(BF16)


def attention_gathered(attn_q, attn_k, attn_v, place):
    rows, chans = attn_q.shape
    shards = lax.axis_size("seq")
    key = lax.all_gather(attn_k, "seq", axis=0, tiled=True)
    value = lax.all_gather(attn_v, "seq", axis=0, tiled=True)
    own = pl.BlockSpec((rows, HD), lambda h, s, p: (0, h))
    other = pl.BlockSpec((rows, HD), lambda h, s, p: (jnp.minimum(s, p[0]), h))
    return pl.pallas_call(
        gathered_kernel,
        grid_spec=pltpu.PrefetchScalarGridSpec(
            num_scalar_prefetch=1,
            grid=(chans // HD, shards),
            in_specs=[own, other, other],
            out_specs=own,
            scratch_shapes=[
                pltpu.VMEM((1, rows), F32),
                pltpu.VMEM((1, rows), F32),
                pltpu.VMEM((HD, rows), F32),
            ],
        ),
        out_shape=jax.ShapeDtypeStruct((rows, chans), BF16),
        compiler_params=ceil_params(),
        name="gathered_part",
    )(place, attn_q, key, value)


def per_device(
    hyena_q, hyena_k, hyena_v, short_filter, long_filter, skip_bias, attn_q, attn_k, attn_v
):
    shards = lax.axis_size("seq")
    heads = attn_q.shape[1] // HD
    place = lax.axis_index("seq").astype(jnp.int32).reshape(1)
    arrays = tuple(in_hbm(value) for value in (hyena_q, hyena_k, hyena_v))
    halo = halo_pack(*arrays, short_filter)

    filter_rows, skip_row = long_filter.T, skip_bias[None]

    def hyena(halos, so_far):
        return hyena_half(
            hyena_q, hyena_k, hyena_v, short_filter, filter_rows, skip_row, halos, so_far
        )

    early = hyena((), None)
    if shards == 4 and 2 <= heads <= 8:
        attn_out, hyena_out = attention_four(attn_q, attn_k, attn_v, place, halo, hyena, early)
    else:
        upper = lax.ppermute(halo, "seq", [(s, s + 1) for s in range(1, shards - 1)])
        lower = lax.ppermute(halo, "seq", [(0, 1)] if shards > 1 else [])
        (hyena_out,) = hyena((upper, lower), early)
        attn_out = attention_gathered(attn_q, attn_k, attn_v, place)
    return hyena_out, attn_out


def solution(mesh):
    both = P(("grp", "seq"), ("mp", "rep"))
    in_specs = (
        both,
        both,
        both,
        P(None, None, ("mp", "rep")),
        P(None, ("mp", "rep")),
        P(("mp", "rep")),
        both,
        both,
        both,
    )
    return jax.shard_map(
        per_device, mesh=mesh, in_specs=in_specs, out_specs=(both, both), check_vma=False
    )
```

```python
import functools

import jax
import jax.numpy as jnp
from jax import lax
from jax.experimental import pallas as pl
from jax.experimental.pallas import tpu as pltpu
from jax.sharding import PartitionSpec as P

HD = 128
FILT = 128
SHORT = 3
GSIZE = 16
LANES = 128
TAIL = 16
STATS = 16
MiB = 1 << 20
LOG2E = 1.4426950408889634
SCALE2 = HD**-0.5 * LOG2E
NEG = -1e30
F32 = jnp.float32
BF16 = jnp.bfloat16


def ceil_params(limit=16):
    return pltpu.CompilerParams(vmem_limit_bytes=limit * MiB)


def estimate(flops, moved):
    return pl.CostEstimate(flops=int(4 * flops), bytes_accessed=int(4 * moved), transcendentals=0)


def in_vmem():
    return pl.BlockSpec(memory_space=pltpu.VMEM)


def in_hbm(value):
    return pltpu.with_memory_space_constraint(value, pltpu.HBM)


def after(value, *others):
    return lax.optimization_barrier((value, *others))[0]


def short_conv(extended, taps, keep):
    total = taps[0][None] * extended
    total = total + taps[1][None] * pltpu.roll(extended, 1, 0)
    total = total + taps[2][None] * pltpu.roll(extended, 2, 0)
    return total[keep:]


def halo_kernel(q_hbm, k_hbm, v_hbm, taps_ref, out_ref, q_in, k_in, v_in, sems):
    rows = q_hbm.shape[0]
    reach = FILT + TAIL
    copies = [
        pltpu.make_async_copy(k_hbm.at[pl.ds(rows - reach, reach)], k_in, sems.at[0]),
        pltpu.make_async_copy(v_hbm.at[pl.ds(rows - reach, reach)], v_in, sems.at[1]),
        pltpu.make_async_copy(q_hbm.at[pl.ds(rows - TAIL, TAIL)], q_in, sems.at[2]),
    ]
    for copy in copies:
        copy.start()
    for copy in copies:
        copy.wait()
    for start in range(0, out_ref.shape[1], LANES):
        cols = slice(start, start + LANES)
        k_tile = k_in[:, cols].astype(F32)
        v_tile = v_in[:, cols].astype(F32)
        k_conv = short_conv(k_tile, taps_ref[1, :, cols], TAIL)
        v_conv = short_conv(v_tile, taps_ref[2, :, cols], TAIL)
        out_ref[:FILT, cols] = (k_conv * v_conv).astype(BF16)
        q_tail = q_in[:, cols].astype(F32)
        k_tail = pltpu.roll(k_tile[FILT:], TAIL - 2, 0)
        v_tail = pltpu.roll(v_tile[FILT:], TAIL - 4, 0)
        row = lax.broadcasted_iota(jnp.int32, q_tail.shape, 0)
        packed = jnp.where(row >= TAIL - 2, q_tail, jnp.where(row >= TAIL - 4, k_tail, v_tail))
        out_ref[FILT:, cols] = packed.astype(BF16)


def halo_pack(hyena_q, hyena_k, hyena_v, short_filter):
    rows, chans = hyena_q.shape
    whole = pl.BlockSpec(memory_space=pl.ANY)
    return pl.pallas_call(
        halo_kernel,
        in_specs=[whole, whole, whole, in_vmem()],
        out_specs=in_vmem(),
        out_shape=jax.ShapeDtypeStruct((FILT + TAIL, chans), BF16),
        scratch_shapes=[
            pltpu.VMEM((TAIL, chans), BF16),
            pltpu.VMEM((FILT + TAIL, chans), BF16),
            pltpu.VMEM((FILT + TAIL, chans), BF16),
            pltpu.SemaphoreType.DMA((3,)),
        ],
        compiler_params=ceil_params(16),
        cost_estimate=estimate(20 * FILT * chans, 2 * 4 * FILT * chans),
        name="halo_pack",
    )(hyena_q, hyena_k, hyena_v, short_filter)


def hyena_kernel(late, q_ref, k_ref, v_ref, taps_ref, filt_ref, skip_ref, *rest):
    long_ref, ready_ref, sem = rest[-3:]
    out_ref, table_ref = (rest[-4], rest[2]) if late else rest[:2]
    rows, chans = q_ref.shape
    half = rows // 2
    blocks = half // FILT
    groups = LANES // GSIZE
    source = lax.broadcasted_iota(jnp.int32, (FILT, FILT), 0)
    target = lax.broadcasted_iota(jnp.int32, (FILT, FILT), 1)
    near = target >= source

    def one_tile(index, carry):
        cols = pl.ds(pl.multiple_of(index * LANES, LANES), LANES)
        if late:
            halo = rest[0][:, cols].astype(F32) + rest[1][:, cols].astype(F32)
            tail = halo[FILT:]
            tails = (tail, pltpu.roll(tail, 2, 0), pltpu.roll(tail, 4, 0))

        def conv(which, ref, reach):
            if late:
                signal = jnp.concatenate([tails[which], ref[:half, cols].astype(F32)], axis=0)
            else:
                signal = ref[half - reach - TAIL :, cols].astype(F32)
            return short_conv(signal, taps_ref[which, :, cols], TAIL)

        product = (conv(1, k_ref, FILT) * conv(2, v_ref, FILT)).astype(BF16).astype(F32)
        if late:
            gated = product
            signal = jnp.concatenate([halo[:FILT], gated], axis=0)
        else:
            gated = product[FILT:]
            signal = product
        signal = signal.T.astype(BF16)
        if not late:
            filters = filt_ref[pl.ds(pl.multiple_of(index * groups, groups), groups), :]
        for group in range(groups):
            place = pl.multiple_of((index * groups + group) * 2 * FILT, 2 * FILT)
            if late:
                table = table_ref[pl.ds(place, 2 * FILT), :]
            else:
                taps = jnp.broadcast_to(filters[group : group + 1], (8, FILT))
                base = pltpu.roll(taps, 0, 1, stride=1, stride_axis=0)
                turned = jnp.concatenate(
                    [base] + [pltpu.roll(base, s, 1) for s in range(8, FILT, 8)], axis=0
                )
                table = jnp.concatenate(
                    [jnp.where(near, 0.0, turned), jnp.where(near, turned, 0.0)], axis=0
                ).astype(BF16)
                table_ref[pl.ds(place, 2 * FILT), :] = table
            band = signal[group * GSIZE : (group + 1) * GSIZE]
            stacked = jnp.concatenate(
                [band[:, b * FILT : (b + 2) * FILT] for b in range(blocks)], axis=0
            )
            result = jnp.dot(stacked, table, preferred_element_type=F32)
            for b in range(blocks):
                long_ref[
                    group * GSIZE : (group + 1) * GSIZE, b * FILT : (b + 1) * FILT
                ] = result[b * GSIZE : (b + 1) * GSIZE]
        long_conv = long_ref[...].T
        mixed = conv(0, q_ref, 0) * (long_conv + skip_ref[:, cols] * gated)
        ready_ref[:, cols] = mixed.astype(BF16)
        return carry

    lax.fori_loop(0, chans // LANES, one_tile, 0)
    copy = pltpu.make_async_copy(
        ready_ref, out_ref.at[pl.ds(0 if late else half, half), :], sem
    )
    copy.start()
    copy.wait()


def hyena_half(hyena_q, hyena_k, hyena_v, short_filter, filter_rows, skip_row, halos, so_far):
    rows, chans = hyena_q.shape
    late = so_far is not None
    half = rows // 2
    operands = [hyena_q, hyena_k, hyena_v, short_filter, filter_rows, skip_row, *halos]
    specs = [in_vmem()] * len(operands)
    aliases = {}
    outs = [pl.BlockSpec(memory_space=pl.ANY)]
    shapes = [jax.ShapeDtypeStruct((rows, chans), BF16)]
    if late:
        so_far, table = so_far
        operands.append(table)
        specs.append(in_vmem())
        aliases = {len(operands): 0}
        operands.append(so_far)
        specs.append(pl.BlockSpec(memory_space=pl.ANY))
    else:
        outs.append(in_vmem())
        shapes.append(jax.ShapeDtypeStruct((chans // GSIZE * 2 * FILT, FILT), BF16))
    return pl.pallas_call(
        functools.partial(hyena_kernel, late),
        in_specs=specs,
        out_specs=outs,
        out_shape=shapes,
        scratch_shapes=[
            pltpu.VMEM((LANES, half), F32),
            pltpu.VMEM((half, chans), BF16),
            pltpu.SemaphoreType.DMA,
        ],
        input_output_aliases=aliases,
        compiler_params=ceil_params(16),
        cost_estimate=estimate(rows * chans * 256 * 8, 8 * rows * chans),
        name="hyena_late" if late else "hyena_early",
    )(*operands)


def scores_of(key, query):
    return lax.dot_general(key, query, (((1,), (1,)), ((), ())), preferred_element_type=F32)


def weighted(value, probs):
    return lax.dot_general(value, probs, (((0,), (0,)), ((), ())), preferred_element_type=F32)


def causal_scores(key, query):
    scores = scores_of(key, query)
    key_pos = lax.broadcasted_iota(jnp.int32, scores.shape, 0)
    query_pos = lax.broadcasted_iota(jnp.int32, scores.shape, 1)
    return jnp.where(key_pos <= query_pos, scores, NEG)


def attend(query, blocks):
    top = None
    mixed = None
    for key, value, causal in blocks:
        scores = causal_scores(key, query) if causal else scores_of(key, query)
        block_top = jnp.max(scores, axis=0, keepdims=True) * SCALE2
        extended = jnp.concatenate([value, jnp.ones((value.shape[0], HD), BF16)], axis=1)
        if top is None:
            top = block_top
            mixed = weighted(extended, jnp.exp2(scores * SCALE2 - top).astype(BF16))
        else:
            new_top = jnp.maximum(top, block_top)
            keep = jnp.exp2(top - new_top)
            term = weighted(extended, jnp.exp2(scores * SCALE2 - new_top).astype(BF16))
            mixed = keep * mixed + term
            top = new_top
    total = mixed[HD : HD + 1]
    return mixed[:HD] / total, top + jnp.log2(total)


def split_kernel(rows, chunks, place_ref, q_ref, k_ref, v_ref, *rest):
    out_refs, sems = rest[:-1], rest[-1]
    copies = []

    def send(source, head, target, slot):
        copies.append(
            pltpu.make_async_copy(
                source.at[:, pl.ds(head * HD, HD)],
                target.at[pl.ds(slot * rows, rows), :],
                sems.at[len(copies)],
            )
        )

    for index, (offset, heads) in enumerate(chunks):
        query_ref, kv_ref = out_refs[2 * index : 2 * index + 2]
        for j in range(heads):
            send(q_ref, offset + j, query_ref, j)
            send(k_ref, offset + j, kv_ref, 2 * j)
            send(v_ref, offset + j, kv_ref, 2 * j + 1)
    for copy in copies:
        copy.start()
    for copy in copies:
        copy.wait()


def split_heads_out(place, attn_q, attn_k, attn_v, chunks):
    rows = attn_q.shape[0]
    shapes = []
    for _, heads in chunks:
        shapes.append(jax.ShapeDtypeStruct((heads * rows, HD), BF16))
        shapes.append(jax.ShapeDtypeStruct((2 * heads * rows, HD), BF16))
    total = sum(heads for _, heads in chunks)
    return pl.pallas_call(
        functools.partial(split_kernel, rows, chunks),
        in_specs=[pl.BlockSpec(memory_space=pltpu.SMEM)] + [pl.BlockSpec(memory_space=pl.ANY)] * 3,
        out_specs=[in_vmem() for _ in shapes],
        out_shape=shapes,
        scratch_shapes=[pltpu.SemaphoreType.DMA((3 * total,))],
        compiler_params=ceil_params(),
        cost_estimate=estimate(0, 12 * rows * total * HD),
        name="split_heads",
    )(place, attn_q, attn_k, attn_v)


def head_rows(ref, slot, rows):
    return ref[slot * rows : (slot + 1) * rows]


def query_tile(rows):
    return min(256, rows)


def remote_kernel(heads, far, place_ref, q_ref, kvr_ref, kv_ref, o_ref, stat_ref):
    place = place_ref[0]
    rows = o_ref.shape[1]
    tile = query_tile(rows)

    def fill(kv_refs):
        for head in range(heads):
            blocks = [
                (head_rows(ref, 2 * head, rows), head_rows(ref, 2 * head + 1, rows), False)
                for ref in kv_refs
            ]
            for start in range(0, rows, tile):
                query = q_ref[head * rows + start : head * rows + start + tile]
                mixed, level = attend(query, blocks)
                o_ref[head * HD : (head + 1) * HD, start : start + tile] = mixed.astype(BF16)
                stat_ref[head : head + 1, start : start + tile] = level
        level = stat_ref[...]
        high = level.astype(BF16).astype(F32)
        middle = (level - high).astype(BF16).astype(F32)
        low = level - high - middle
        row = lax.broadcasted_iota(jnp.int32, level.shape, 0)
        first = jnp.where(row < 4, high, pltpu.roll(middle, 4, 0))
        o_ref[heads * HD :] = jnp.concatenate([first, low], axis=0).astype(BF16)

    @pl.when(place == 1)
    def _():
        fill([kvr_ref, kv_ref])

    if not far:

        @pl.when(place == 2)
        def _():
            fill([kv_ref])


def remote_part(place, rows, far, q, kvr, kv):
    heads = q.shape[0] // rows
    width = heads * HD
    return pl.pallas_call(
        functools.partial(remote_kernel, heads, far),
        in_specs=[pl.BlockSpec(memory_space=pltpu.SMEM)] + [in_vmem()] * 3,
        out_specs=in_vmem(),
        out_shape=jax.ShapeDtypeStruct((width + STATS, rows), BF16),
        scratch_shapes=[pltpu.VMEM((8, rows), F32)],
        compiler_params=ceil_params(),
        cost_estimate=estimate(heads * 8 * HD * rows * rows, 10 * rows * width),
        name="remote_far" if far else "remote_near",
    )(place, q, kvr, kv)


def level_row(stats, head):
    row = lax.broadcasted_iota(jnp.int32, stats.shape, 0)
    chosen = (row == head) | (row == head + 4) | (row == head + 8)
    return jnp.sum(jnp.where(chosen, stats, 0.0), axis=0, keepdims=True)


def own_kernel(sizes, *rest):
    count = len(sizes)
    mixed_ref, level_ref = rest[2 * count :]
    rows = mixed_ref.shape[1]
    tile = query_tile(rows)
    column = 0
    for index, heads in enumerate(sizes):
        q_ref, kv_ref = rest[2 * index : 2 * index + 2]
        for head in range(heads):
            key = head_rows(kv_ref, 2 * head, rows)
            value = head_rows(kv_ref, 2 * head + 1, rows)
            for start in range(0, rows, tile):
                cols = slice(start, start + tile)
                query = q_ref[head * rows + start : head * rows + start + tile]
                blocks = [(key[cols], value[cols], True)]
                if start:
                    blocks.append((key[:start], value[:start], False))
                mixed, level = attend(query, blocks)
                mixed_ref[column * HD : (column + 1) * HD, cols] = mixed
                level_ref[column : column + 1, cols] = level
            column += 1


def own_part(rows, messages):
    sizes = tuple(q.shape[0] // rows for q, _ in messages)
    total = sum(sizes)
    return pl.pallas_call(
        functools.partial(own_kernel, sizes),
        in_specs=[in_vmem()] * (2 * len(sizes)),
        out_specs=(in_vmem(), in_vmem()),
        out_shape=(
            jax.ShapeDtypeStruct((total * HD, rows), F32),
            jax.ShapeDtypeStruct((total, rows), F32),
        ),
        compiler_params=ceil_params(),
        cost_estimate=estimate(total * 3 * HD * rows * rows, 10 * rows * total * HD),
        name="own_part",
    )(*[value for pair in messages for value in pair])


def passed_kernel(heads, first, place_ref, q_ref, kvr_ref, own_ref, own_level_ref, mixed_ref, level_ref):
    rows = mixed_ref.shape[1]
    tile = query_tile(rows)
    mixed_ref[...] = own_ref[first * HD : (first + heads) * HD]
    level_ref[...] = own_level_ref[first : first + heads]

    @pl.when(place_ref[0] == 1)
    def _():
        for head in range(heads):
            at = slice(head * HD, (head + 1) * HD)
            block = (
                head_rows(kvr_ref, 2 * head, rows),
                head_rows(kvr_ref, 2 * head + 1, rows),
                False,
            )
            for start in range(0, rows, tile):
                cols = slice(start, start + tile)
                query = q_ref[head * rows + start : head * rows + start + tile]
                other, other_level = attend(query, [block])
                level = level_ref[head : head + 1, cols]
                top = jnp.maximum(level, other_level)
                mine = jnp.exp2(level - top)
                theirs = jnp.exp2(other_level - top)
                both = mine + theirs
                mixed_ref[at, cols] = mixed_ref[at, cols] * (mine / both) + other * (theirs / both)
                level_ref[head : head + 1, cols] = top + jnp.log2(both)


def passed_part(place, rows, first, q, kvr, own):
    heads = q.shape[0] // rows
    return pl.pallas_call(
        functools.partial(passed_kernel, heads, first),
        in_specs=[pl.BlockSpec(memory_space=pltpu.SMEM)] + [in_vmem()] * 4,
        out_specs=(in_vmem(), in_vmem()),
        out_shape=(
            jax.ShapeDtypeStruct((heads * HD, rows), F32),
            jax.ShapeDtypeStruct((heads, rows), F32),
        ),
        compiler_params=ceil_params(),
        cost_estimate=estimate(heads * 4 * HD * rows * rows, 10 * rows * heads * HD),
        name="passed_part",
    )(place, q, kvr, *own)


def final_kernel(sizes, first, aliased, place_ref, own_ref, own_level_ref, *rest):
    count = len(sizes)
    groups = [rest[4 * i : 4 * i + 4] for i in range(count)]
    out_ref, mixed_ref, level_ref, ready_ref, sem = rest[4 * count + aliased :]
    place = place_ref[0]
    rows = mixed_ref.shape[1]
    tile = query_tile(rows)
    column = 0

    def merge(other, other_level, cols):
        level = level_ref[:, cols]
        top = jnp.maximum(level, other_level)
        mine = jnp.exp2(level - top)
        theirs = jnp.exp2(other_level - top)
        both = mine + theirs
        mixed_ref[:, cols] = mixed_ref[:, cols] * (mine / both) + other * (theirs / both)
        level_ref[:, cols] = top + jnp.log2(both)

    for heads, (q_ref, kvr_ref, oa_ref, ob_ref) in zip(sizes, groups):
        for head in range(heads):
            at = column
            mixed_ref[...] = own_ref[at * HD : (at + 1) * HD]
            level_ref[...] = own_level_ref[at : at + 1]

            def received(o_ref, head=head, heads=heads):
                merge(
                    o_ref[head * HD : (head + 1) * HD].astype(F32),
                    level_row(o_ref[heads * HD :].astype(F32), head),
                    slice(0, rows),
                )

            pl.when(place >= 2)(functools.partial(received, oa_ref))
            pl.when(place >= 3)(functools.partial(received, ob_ref))
            ready_ref[:, column * HD : (column + 1) * HD] = mixed_ref[...].T.astype(BF16)
            column += 1
    copy = pltpu.make_async_copy(
        ready_ref, out_ref.at[:, pl.ds(first * HD, column * HD)], sem
    )
    copy.start()
    copy.wait()


def final_part(place, rows, chans, first, own, groups, so_far):
    sizes = tuple(group[0].shape[0] // rows for group in groups)
    total = sum(sizes)
    operands = [place, *own] + [value for group in groups for value in group]
    specs = [pl.BlockSpec(memory_space=pltpu.SMEM)] + [in_vmem()] * (len(operands) - 1)
    aliases = {}
    if so_far is not None:
        aliases = {len(operands): 0}
        operands.append(so_far)
        specs.append(pl.BlockSpec(memory_space=pl.ANY))
    return pl.pallas_call(
        functools.partial(final_kernel, sizes, first, len(aliases)),
        in_specs=specs,
        out_specs=pl.BlockSpec(memory_space=pl.ANY),
        out_shape=jax.ShapeDtypeStruct((rows, chans), BF16),
        scratch_shapes=[
            pltpu.VMEM((HD, rows), F32),
            pltpu.VMEM((1, rows), F32),
            pltpu.VMEM((rows, total * HD), BF16),
            pltpu.SemaphoreType.DMA,
        ],
        input_output_aliases=aliases,
        compiler_params=ceil_params(),
        cost_estimate=estimate(total * 4 * HD * rows * rows, 14 * rows * total * HD),
        name="final_part",
    )(*operands)


def chunk_sizes(heads):
    parts = 3
    base = heads // parts
    return [base + (part < heads - parts * base) for part in range(parts)]


def attention_four(attn_q, attn_k, attn_v, place, halo, hyena, early):
    rows, chans = attn_q.shape
    sizes = chunk_sizes(chans // HD)
    starts = [sum(sizes[:c]) for c in range(len(sizes))]
    arrays = tuple(in_hbm(value) for value in (attn_q, attn_k, attn_v))
    q0, kv0 = split_heads_out(place, *arrays, [(0, sizes[0])])
    rest = split_heads_out(place, *arrays, list(zip(starts, sizes))[1:])
    q, kv = [q0, *rest[0::2]], [kv0, *rest[1::2]]

    def to_hub(value):
        return lax.ppermute(value, "seq", [(2, 1), (3, 2)])

    def to_hub_far(value):
        return lax.ppermute(value, "seq", [(3, 1)])

    def keys_up(value):
        return lax.ppermute(value, "seq", [(0, 1)])

    def back(value):
        return lax.ppermute(value, "seq", [(1, 2), (2, 3)])

    def back_far(value):
        return lax.ppermute(value, "seq", [(1, 3)])

    count = len(sizes)
    kvr, qb, qa = [keys_up(kv[0])], [to_hub_far(q[0])], [to_hub(q[0])]
    oa, ob, ra, rb = [], [], [], []

    def work(c, gate):
        gates = (gate, early[1]) if c == 0 else (gate,)
        far = remote_part(place, rows, True, qb[c], after(kvr[c], *gates), kv[c])
        ob.append(far)
        rb.append(back_far(after(far, rb[c - 1]) if c else far))
        gates = (far, rb[c - 1]) if c else (far,)
        near = remote_part(place, rows, False, qa[c], after(kvr[c], *gates), kv[c])
        oa.append(near)
        if c == 1:
            near = after(near, qb[2])
        ra.append(back(after(near, ra[c - 1]) if c == 1 else near))

    own_in = list(zip(q, kv))
    own_in[-1] = (q[-1], kv[-1])
    own = own_part(rows, own_in)
    qb.append(to_hub_far(q[1]))
    upper = lax.ppermute(halo, "seq", [(1, 2), (2, 3)])
    kvr.append(keys_up(after(kv[1], upper, own[1])))
    work(0, own[1])
    qa.append(to_hub(after(q[1], ob[0])))
    own_first = passed_part(place, rows, 0, q[0], after(kvr[0], oa[0]), own)
    kvr.append(keys_up(after(kv[2], kvr[1], qb[1], oa[0], own_first[1])))
    qb.append(to_hub_far(after(q[2], kvr[1], qb[1], oa[0], own_first[1])))
    work(1, own_first[1])
    qa.append(to_hub(after(q[2], oa[1])))
    lower = lax.ppermute(after(halo, kvr[2], oa[1]), "seq", [(0, 1)])

    def finish(c, so_far):
        mine = passed_part(place, rows, starts[c], q[c], after(kvr[c], oa[2]), own)
        return final_part(
            place, rows, chans, starts[c], mine, [(q[c], kvr[c], ra[c], rb[c])], so_far
        )

    work(2, oa[1])
    out = final_part(
        place, rows, chans, 0, own_first, [(q[0], kvr[0], after(ra[0], oa[2]), rb[0])], None
    )
    out = finish(1, out)
    (hyena_out,) = hyena((after(upper, oa[-1], out), lower), early)
    out, hyena_out = lax.optimization_barrier((out, hyena_out))
    out = finish(2, out)
    return out, hyena_out


def gathered_kernel(place_ref, q_ref, k_ref, v_ref, out_ref, top_ref, total_ref, mixed_ref):
    shard = pl.program_id(1)
    place = place_ref[0]

    @pl.when(shard == 0)
    def _():
        top_ref[...] = jnp.full(top_ref.shape, NEG, F32)
        total_ref[...] = jnp.zeros(total_ref.shape, F32)
        mixed_ref[...] = jnp.zeros(mixed_ref.shape, F32)

    def update(scores):
        top = jnp.maximum(top_ref[...], jnp.max(scores, axis=0, keepdims=True) * SCALE2)
        weights = jnp.exp2(scores * SCALE2 - top)
        keep = jnp.exp2(top_ref[...] - top)
        total_ref[...] = keep * total_ref[...] + jnp.sum(weights, axis=0, keepdims=True)
        mixed_ref[...] = keep * mixed_ref[...] + weighted(v_ref[...], weights.astype(BF16))
        top_ref[...] = top

    @pl.when(shard < place)
    def _():
        update(scores_of(k_ref[...], q_ref[...]))

    @pl.when(shard == place)
    def _():
        update(causal_scores(k_ref[...], q_ref[...]))
        out_ref[...] = (mixed_ref[...] / total_ref[...]).T.astype(BF16)


def attention_gathered(attn_q, attn_k, attn_v, place):
    rows, chans = attn_q.shape
    shards = lax.axis_size("seq")
    key = lax.all_gather(attn_k, "seq", axis=0, tiled=True)
    value = lax.all_gather(attn_v, "seq", axis=0, tiled=True)
    own = pl.BlockSpec((rows, HD), lambda h, s, p: (0, h))
    other = pl.BlockSpec((rows, HD), lambda h, s, p: (jnp.minimum(s, p[0]), h))
    return pl.pallas_call(
        gathered_kernel,
        grid_spec=pltpu.PrefetchScalarGridSpec(
            num_scalar_prefetch=1,
            grid=(chans // HD, shards),
            in_specs=[own, other, other],
            out_specs=own,
            scratch_shapes=[
                pltpu.VMEM((1, rows), F32),
                pltpu.VMEM((1, rows), F32),
                pltpu.VMEM((HD, rows), F32),
            ],
        ),
        out_shape=jax.ShapeDtypeStruct((rows, chans), BF16),
        compiler_params=ceil_params(),
        name="gathered_part",
    )(place, attn_q, key, value)


def per_device(
    hyena_q, hyena_k, hyena_v, short_filter, long_filter, skip_bias, attn_q, attn_k, attn_v
):
    shards = lax.axis_size("seq")
    heads = attn_q.shape[1] // HD
    place = lax.axis_index("seq").astype(jnp.int32).reshape(1)
    arrays = tuple(in_hbm(value) for value in (hyena_q, hyena_k, hyena_v))
    halo = halo_pack(*arrays, short_filter)

    filter_rows, skip_row = long_filter.T, skip_bias[None]

    def hyena(halos, so_far):
        return hyena_half(
            hyena_q, hyena_k, hyena_v, short_filter, filter_rows, skip_row, halos, so_far
        )

    early = hyena((), None)
    if shards == 4 and 2 <= heads <= 8:
        attn_out, hyena_out = attention_four(attn_q, attn_k, attn_v, place, halo, hyena, early)
    else:
        upper = lax.ppermute(halo, "seq", [(s, s + 1) for s in range(1, shards - 1)])
        lower = lax.ppermute(halo, "seq", [(0, 1)] if shards > 1 else [])
        (hyena_out,) = hyena((upper, lower), early)
        attn_out = attention_gathered(attn_q, attn_k, attn_v, place)
    return hyena_out, attn_out


def solution(mesh):
    both = P(("grp", "seq"), ("mp", "rep"))
    in_specs = (
        both,
        both,
        both,
        P(None, None, ("mp", "rep")),
        P(None, ("mp", "rep")),
        P(("mp", "rep")),
        both,
        both,
        both,
    )
    return jax.shard_map(
        per_device, mesh=mesh, in_specs=in_specs, out_specs=(both, both), check_vma=False
    )
```

```python
import functools

import jax
import jax.numpy as jnp
from jax import lax
from jax.experimental import pallas as pl
from jax.experimental.pallas import tpu as pltpu
from jax.sharding import PartitionSpec as P

HD = 128
FILT = 128
SHORT = 3
GSIZE = 16
LANES = 128
TAIL = 16
STATS = 16
MiB = 1 << 20
LOG2E = 1.4426950408889634
SCALE2 = HD**-0.5 * LOG2E
NEG = -1e30
F32 = jnp.float32
BF16 = jnp.bfloat16


def ceil_params(limit=16):
    return pltpu.CompilerParams(vmem_limit_bytes=limit * MiB)


def estimate(flops, moved):
    return pl.CostEstimate(flops=int(4 * flops), bytes_accessed=int(4 * moved), transcendentals=0)


def in_vmem():
    return pl.BlockSpec(memory_space=pltpu.VMEM)


def in_hbm(value):
    return pltpu.with_memory_space_constraint(value, pltpu.HBM)


def after(value, *others):
    return lax.optimization_barrier((value, *others))[0]


def short_conv(extended, taps, keep):
    total = taps[0][None] * extended
    total = total + taps[1][None] * pltpu.roll(extended, 1, 0)
    total = total + taps[2][None] * pltpu.roll(extended, 2, 0)
    return total[keep:]


def halo_kernel(q_hbm, k_hbm, v_hbm, taps_hbm, out_ref, q_in, k_in, v_in, taps_ref, sems):
    rows = q_hbm.shape[0]
    reach = FILT + TAIL
    copies = [
        pltpu.make_async_copy(k_hbm.at[pl.ds(rows - reach, reach)], k_in, sems.at[0]),
        pltpu.make_async_copy(v_hbm.at[pl.ds(rows - reach, reach)], v_in, sems.at[1]),
        pltpu.make_async_copy(q_hbm.at[pl.ds(rows - TAIL, TAIL)], q_in, sems.at[2]),
        pltpu.make_async_copy(taps_hbm, taps_ref, sems.at[3]),
    ]
    for copy in copies:
        copy.start()
    for copy in copies:
        copy.wait()
    for start in range(0, out_ref.shape[1], LANES):
        cols = slice(start, start + LANES)
        k_tile = k_in[:, cols].astype(F32)
        v_tile = v_in[:, cols].astype(F32)
        k_conv = short_conv(k_tile, taps_ref[1, :, cols], TAIL)
        v_conv = short_conv(v_tile, taps_ref[2, :, cols], TAIL)
        out_ref[:FILT, cols] = (k_conv * v_conv).astype(BF16)
        q_tail = q_in[:, cols].astype(F32)
        k_tail = pltpu.roll(k_tile[FILT:], TAIL - 2, 0)
        v_tail = pltpu.roll(v_tile[FILT:], TAIL - 4, 0)
        row = lax.broadcasted_iota(jnp.int32, q_tail.shape, 0)
        packed = jnp.where(row >= TAIL - 2, q_tail, jnp.where(row >= TAIL - 4, k_tail, v_tail))
        out_ref[FILT:, cols] = packed.astype(BF16)


def halo_pack(hyena_q, hyena_k, hyena_v, short_filter):
    rows, chans = hyena_q.shape
    whole = pl.BlockSpec(memory_space=pl.ANY)
    return pl.pallas_call(
        halo_kernel,
        in_specs=[whole, whole, whole, whole],
        out_specs=in_vmem(),
        out_shape=jax.ShapeDtypeStruct((FILT + TAIL, chans), BF16),
        scratch_shapes=[
            pltpu.VMEM((TAIL, chans), BF16),
            pltpu.VMEM((FILT + TAIL, chans), BF16),
            pltpu.VMEM((FILT + TAIL, chans), BF16),
            pltpu.VMEM(short_filter.shape, F32),
            pltpu.SemaphoreType.DMA((4,)),
        ],
        compiler_params=ceil_params(16),
        cost_estimate=estimate(20 * FILT * chans, 2 * 4 * FILT * chans),
        name="halo_pack",
    )(hyena_q, hyena_k, hyena_v, in_hbm(short_filter))


def hyena_kernel(late, q_ref, k_ref, v_ref, taps_ref, filt_ref, skip_ref, *rest):
    long_ref, ready_ref, sem = rest[-3:]
    out_ref, table_ref = (rest[-4], rest[2]) if late else rest[:2]
    rows, chans = q_ref.shape
    half = rows // 2
    blocks = half // FILT
    groups = LANES // GSIZE
    source = lax.broadcasted_iota(jnp.int32, (FILT, FILT), 0)
    target = lax.broadcasted_iota(jnp.int32, (FILT, FILT), 1)
    near = target >= source

    def one_tile(index, carry):
        cols = pl.ds(pl.multiple_of(index * LANES, LANES), LANES)
        if late:
            halo = rest[0][:, cols].astype(F32) + rest[1][:, cols].astype(F32)
            tail = halo[FILT:]
            tails = (tail, pltpu.roll(tail, 2, 0), pltpu.roll(tail, 4, 0))

        def conv(which, ref, reach):
            if late:
                signal = jnp.concatenate([tails[which], ref[:half, cols].astype(F32)], axis=0)
            else:
                signal = ref[half - reach - TAIL :, cols].astype(F32)
            return short_conv(signal, taps_ref[which, :, cols], TAIL)

        product = (conv(1, k_ref, FILT) * conv(2, v_ref, FILT)).astype(BF16).astype(F32)
        if late:
            gated = product
            signal = jnp.concatenate([halo[:FILT], gated], axis=0)
        else:
            gated = product[FILT:]
            signal = product
        signal = signal.T.astype(BF16)
        if not late:
            filters = filt_ref[pl.ds(pl.multiple_of(index * groups, groups), groups), :]
        for group in range(groups):
            place = pl.multiple_of((index * groups + group) * 2 * FILT, 2 * FILT)
            if late:
                table = table_ref[pl.ds(place, 2 * FILT), :]
            else:
                taps = jnp.broadcast_to(filters[group : group + 1], (8, FILT))
                base = pltpu.roll(taps, 0, 1, stride=1, stride_axis=0)
                turned = jnp.concatenate(
                    [base] + [pltpu.roll(base, s, 1) for s in range(8, FILT, 8)], axis=0
                )
                table = jnp.concatenate(
                    [jnp.where(near, 0.0, turned), jnp.where(near, turned, 0.0)], axis=0
                ).astype(BF16)
                table_ref[pl.ds(place, 2 * FILT), :] = table
            band = signal[group * GSIZE : (group + 1) * GSIZE]
            stacked = jnp.concatenate(
                [band[:, b * FILT : (b + 2) * FILT] for b in range(blocks)], axis=0
            )
            result = jnp.dot(stacked, table, preferred_element_type=F32)
            for b in range(blocks):
                long_ref[
                    group * GSIZE : (group + 1) * GSIZE, b * FILT : (b + 1) * FILT
                ] = result[b * GSIZE : (b + 1) * GSIZE]
        long_conv = long_ref[...].T
        mixed = conv(0, q_ref, 0) * (long_conv + skip_ref[:, cols] * gated)
        ready_ref[:, cols] = mixed.astype(BF16)
        return carry

    lax.fori_loop(0, chans // LANES, one_tile, 0)
    copy = pltpu.make_async_copy(
        ready_ref, out_ref.at[pl.ds(0 if late else half, half), :], sem
    )
    copy.start()
    copy.wait()


def hyena_half(hyena_q, hyena_k, hyena_v, short_filter, filter_rows, skip_row, halos, so_far):
    rows, chans = hyena_q.shape
    late = so_far is not None
    half = rows // 2
    operands = [hyena_q, hyena_k, hyena_v, short_filter, filter_rows, skip_row, *halos]
    specs = [in_vmem()] * len(operands)
    aliases = {}
    outs = [pl.BlockSpec(memory_space=pl.ANY)]
    shapes = [jax.ShapeDtypeStruct((rows, chans), BF16)]
    if late:
        so_far, table = so_far
        operands.append(table)
        specs.append(in_vmem())
        aliases = {len(operands): 0}
        operands.append(so_far)
        specs.append(pl.BlockSpec(memory_space=pl.ANY))
    else:
        outs.append(in_vmem())
        shapes.append(jax.ShapeDtypeStruct((chans // GSIZE * 2 * FILT, FILT), BF16))
    return pl.pallas_call(
        functools.partial(hyena_kernel, late),
        in_specs=specs,
        out_specs=outs,
        out_shape=shapes,
        scratch_shapes=[
            pltpu.VMEM((LANES, half), F32),
            pltpu.VMEM((half, chans), BF16),
            pltpu.SemaphoreType.DMA,
        ],
        input_output_aliases=aliases,
        compiler_params=ceil_params(16),
        cost_estimate=estimate(rows * chans * 256 * 8, 8 * rows * chans),
        name="hyena_late" if late else "hyena_early",
    )(*operands)


def scores_of(key, query):
    return lax.dot_general(key, query, (((1,), (1,)), ((), ())), preferred_element_type=F32)


def weighted(value, probs):
    return lax.dot_general(value, probs, (((0,), (0,)), ((), ())), preferred_element_type=F32)


def causal_scores(key, query):
    scores = scores_of(key, query)
    key_pos = lax.broadcasted_iota(jnp.int32, scores.shape, 0)
    query_pos = lax.broadcasted_iota(jnp.int32, scores.shape, 1)
    return jnp.where(key_pos <= query_pos, scores, NEG)


def attend(query, blocks):
    top = None
    mixed = None
    for key, value, causal in blocks:
        scores = causal_scores(key, query) if causal else scores_of(key, query)
        block_top = jnp.max(scores, axis=0, keepdims=True) * SCALE2
        extended = jnp.concatenate([value, jnp.ones((value.shape[0], HD), BF16)], axis=1)
        if top is None:
            top = block_top
            mixed = weighted(extended, jnp.exp2(scores * SCALE2 - top).astype(BF16))
        else:
            new_top = jnp.maximum(top, block_top)
            keep = jnp.exp2(top - new_top)
            term = weighted(extended, jnp.exp2(scores * SCALE2 - new_top).astype(BF16))
            mixed = keep * mixed + term
            top = new_top
    total = mixed[HD : HD + 1]
    return mixed[:HD] / total, top + jnp.log2(total)


def split_kernel(rows, chunks, place_ref, q_ref, k_ref, v_ref, *rest):
    out_refs, sems = rest[:-1], rest[-1]
    copies = []

    def send(source, head, target, slot):
        copies.append(
            pltpu.make_async_copy(
                source.at[:, pl.ds(head * HD, HD)],
                target.at[pl.ds(slot * rows, rows), :],
                sems.at[len(copies)],
            )
        )

    for index, (offset, heads) in enumerate(chunks):
        query_ref, kv_ref = out_refs[2 * index : 2 * index + 2]
        for j in range(heads):
            send(q_ref, offset + j, query_ref, j)
            send(k_ref, offset + j, kv_ref, 2 * j)
            send(v_ref, offset + j, kv_ref, 2 * j + 1)
    for copy in copies:
        copy.start()
    for copy in copies:
        copy.wait()


def split_heads_out(place, attn_q, attn_k, attn_v, chunks):
    rows = attn_q.shape[0]
    shapes = []
    for _, heads in chunks:
        shapes.append(jax.ShapeDtypeStruct((heads * rows, HD), BF16))
        shapes.append(jax.ShapeDtypeStruct((2 * heads * rows, HD), BF16))
    total = sum(heads for _, heads in chunks)
    return pl.pallas_call(
        functools.partial(split_kernel, rows, chunks),
        in_specs=[pl.BlockSpec(memory_space=pltpu.SMEM)] + [pl.BlockSpec(memory_space=pl.ANY)] * 3,
        out_specs=[in_vmem() for _ in shapes],
        out_shape=shapes,
        scratch_shapes=[pltpu.SemaphoreType.DMA((3 * total,))],
        compiler_params=ceil_params(),
        cost_estimate=estimate(0, 12 * rows * total * HD),
        name="split_heads",
    )(place, attn_q, attn_k, attn_v)


def head_rows(ref, slot, rows):
    return ref[slot * rows : (slot + 1) * rows]


def query_tile(rows):
    return min(256, rows)


def remote_kernel(heads, far, place_ref, q_ref, kvr_ref, kv_ref, o_ref, stat_ref):
    place = place_ref[0]
    rows = o_ref.shape[1]
    tile = query_tile(rows)

    def fill(kv_refs):
        for head in range(heads):
            blocks = [
                (head_rows(ref, 2 * head, rows), head_rows(ref, 2 * head + 1, rows), False)
                for ref in kv_refs
            ]
            for start in range(0, rows, tile):
                query = q_ref[head * rows + start : head * rows + start + tile]
                mixed, level = attend(query, blocks)
                o_ref[head * HD : (head + 1) * HD, start : start + tile] = mixed.astype(BF16)
                stat_ref[head : head + 1, start : start + tile] = level
        level = stat_ref[...]
        high = level.astype(BF16).astype(F32)
        middle = (level - high).astype(BF16).astype(F32)
        low = level - high - middle
        row = lax.broadcasted_iota(jnp.int32, level.shape, 0)
        first = jnp.where(row < 4, high, pltpu.roll(middle, 4, 0))
        o_ref[heads * HD :] = jnp.concatenate([first, low], axis=0).astype(BF16)

    @pl.when(place == 1)
    def _():
        fill([kvr_ref, kv_ref])

    if not far:

        @pl.when(place == 2)
        def _():
            fill([kv_ref])


def remote_part(place, rows, far, q, kvr, kv):
    heads = q.shape[0] // rows
    width = heads * HD
    return pl.pallas_call(
        functools.partial(remote_kernel, heads, far),
        in_specs=[pl.BlockSpec(memory_space=pltpu.SMEM)] + [in_vmem()] * 3,
        out_specs=in_vmem(),
        out_shape=jax.ShapeDtypeStruct((width + STATS, rows), BF16),
        scratch_shapes=[pltpu.VMEM((8, rows), F32)],
        compiler_params=ceil_params(),
        cost_estimate=estimate(heads * 8 * HD * rows * rows, 10 * rows * width),
        name="remote_far" if far else "remote_near",
    )(place, q, kvr, kv)


def level_row(stats, head):
    row = lax.broadcasted_iota(jnp.int32, stats.shape, 0)
    chosen = (row == head) | (row == head + 4) | (row == head + 8)
    return jnp.sum(jnp.where(chosen, stats, 0.0), axis=0, keepdims=True)


def own_kernel(sizes, *rest):
    count = len(sizes)
    mixed_ref, level_ref = rest[2 * count :]
    rows = mixed_ref.shape[1]
    tile = query_tile(rows)
    column = 0
    for index, heads in enumerate(sizes):
        q_ref, kv_ref = rest[2 * index : 2 * index + 2]
        for head in range(heads):
            key = head_rows(kv_ref, 2 * head, rows)
            value = head_rows(kv_ref, 2 * head + 1, rows)
            for start in range(0, rows, tile):
                cols = slice(start, start + tile)
                query = q_ref[head * rows + start : head * rows + start + tile]
                blocks = [(key[cols], value[cols], True)]
                if start:
                    blocks.append((key[:start], value[:start], False))
                mixed, level = attend(query, blocks)
                mixed_ref[column * HD : (column + 1) * HD, cols] = mixed
                level_ref[column : column + 1, cols] = level
            column += 1


def own_part(rows, messages):
    sizes = tuple(q.shape[0] // rows for q, _ in messages)
    total = sum(sizes)
    return pl.pallas_call(
        functools.partial(own_kernel, sizes),
        in_specs=[in_vmem()] * (2 * len(sizes)),
        out_specs=(in_vmem(), in_vmem()),
        out_shape=(
            jax.ShapeDtypeStruct((total * HD, rows), F32),
            jax.ShapeDtypeStruct((total, rows), F32),
        ),
        compiler_params=ceil_params(),
        cost_estimate=estimate(total * 3 * HD * rows * rows, 10 * rows * total * HD),
        name="own_part",
    )(*[value for pair in messages for value in pair])


def passed_kernel(heads, first, place_ref, q_ref, kvr_ref, own_ref, own_level_ref, mixed_ref, level_ref):
    rows = mixed_ref.shape[1]
    tile = query_tile(rows)
    mixed_ref[...] = own_ref[first * HD : (first + heads) * HD]
    level_ref[...] = own_level_ref[first : first + heads]

    @pl.when(place_ref[0] == 1)
    def _():
        for head in range(heads):
            at = slice(head * HD, (head + 1) * HD)
            block = (
                head_rows(kvr_ref, 2 * head, rows),
                head_rows(kvr_ref, 2 * head + 1, rows),
                False,
            )
            for start in range(0, rows, tile):
                cols = slice(start, start + tile)
                query = q_ref[head * rows + start : head * rows + start + tile]
                other, other_level = attend(query, [block])
                level = level_ref[head : head + 1, cols]
                top = jnp.maximum(level, other_level)
                mine = jnp.exp2(level - top)
                theirs = jnp.exp2(other_level - top)
                both = mine + theirs
                mixed_ref[at, cols] = mixed_ref[at, cols] * (mine / both) + other * (theirs / both)
                level_ref[head : head + 1, cols] = top + jnp.log2(both)


def passed_part(place, rows, first, q, kvr, own):
    heads = q.shape[0] // rows
    return pl.pallas_call(
        functools.partial(passed_kernel, heads, first),
        in_specs=[pl.BlockSpec(memory_space=pltpu.SMEM)] + [in_vmem()] * 4,
        out_specs=(in_vmem(), in_vmem()),
        out_shape=(
            jax.ShapeDtypeStruct((heads * HD, rows), F32),
            jax.ShapeDtypeStruct((heads, rows), F32),
        ),
        compiler_params=ceil_params(),
        cost_estimate=estimate(heads * 4 * HD * rows * rows, 10 * rows * heads * HD),
        name="passed_part",
    )(place, q, kvr, *own)


def final_kernel(sizes, first, aliased, place_ref, own_ref, own_level_ref, *rest):
    count = len(sizes)
    groups = [rest[4 * i : 4 * i + 4] for i in range(count)]
    out_ref, mixed_ref, level_ref, ready_ref, sem = rest[4 * count + aliased :]
    place = place_ref[0]
    rows = mixed_ref.shape[1]
    tile = query_tile(rows)
    column = 0

    def merge(other, other_level, cols):
        level = level_ref[:, cols]
        top = jnp.maximum(level, other_level)
        mine = jnp.exp2(level - top)
        theirs = jnp.exp2(other_level - top)
        both = mine + theirs
        mixed_ref[:, cols] = mixed_ref[:, cols] * (mine / both) + other * (theirs / both)
        level_ref[:, cols] = top + jnp.log2(both)

    for heads, (q_ref, kvr_ref, oa_ref, ob_ref) in zip(sizes, groups):
        for head in range(heads):
            at = column
            mixed_ref[...] = own_ref[at * HD : (at + 1) * HD]
            level_ref[...] = own_level_ref[at : at + 1]

            def received(o_ref, head=head, heads=heads):
                merge(
                    o_ref[head * HD : (head + 1) * HD].astype(F32),
                    level_row(o_ref[heads * HD :].astype(F32), head),
                    slice(0, rows),
                )

            pl.when(place >= 2)(functools.partial(received, oa_ref))
            pl.when(place >= 3)(functools.partial(received, ob_ref))
            ready_ref[:, column * HD : (column + 1) * HD] = mixed_ref[...].T.astype(BF16)
            column += 1
    copy = pltpu.make_async_copy(
        ready_ref, out_ref.at[:, pl.ds(first * HD, column * HD)], sem
    )
    copy.start()
    copy.wait()


def final_part(place, rows, chans, first, own, groups, so_far):
    sizes = tuple(group[0].shape[0] // rows for group in groups)
    total = sum(sizes)
    operands = [place, *own] + [value for group in groups for value in group]
    specs = [pl.BlockSpec(memory_space=pltpu.SMEM)] + [in_vmem()] * (len(operands) - 1)
    aliases = {}
    if so_far is not None:
        aliases = {len(operands): 0}
        operands.append(so_far)
        specs.append(pl.BlockSpec(memory_space=pl.ANY))
    return pl.pallas_call(
        functools.partial(final_kernel, sizes, first, len(aliases)),
        in_specs=specs,
        out_specs=pl.BlockSpec(memory_space=pl.ANY),
        out_shape=jax.ShapeDtypeStruct((rows, chans), BF16),
        scratch_shapes=[
            pltpu.VMEM((HD, rows), F32),
            pltpu.VMEM((1, rows), F32),
            pltpu.VMEM((rows, total * HD), BF16),
            pltpu.SemaphoreType.DMA,
        ],
        input_output_aliases=aliases,
        compiler_params=ceil_params(),
        cost_estimate=estimate(total * 4 * HD * rows * rows, 14 * rows * total * HD),
        name="final_part",
    )(*operands)


def chunk_sizes(heads):
    parts = 3
    base = heads // parts
    return [base + (part < heads - parts * base) for part in range(parts)]


def attention_four(attn_q, attn_k, attn_v, place, halo, hyena, early):
    rows, chans = attn_q.shape
    sizes = chunk_sizes(chans // HD)
    starts = [sum(sizes[:c]) for c in range(len(sizes))]
    arrays = tuple(in_hbm(value) for value in (attn_q, attn_k, attn_v))
    q0, kv0 = split_heads_out(place, *arrays, [(0, sizes[0])])
    rest = split_heads_out(place, *arrays, list(zip(starts, sizes))[1:])
    q, kv = [q0, *rest[0::2]], [kv0, *rest[1::2]]

    def to_hub(value):
        return lax.ppermute(value, "seq", [(2, 1), (3, 2)])

    def to_hub_far(value):
        return lax.ppermute(value, "seq", [(3, 1)])

    def keys_up(value):
        return lax.ppermute(value, "seq", [(0, 1)])

    def back(value):
        return lax.ppermute(value, "seq", [(1, 2), (2, 3)])

    def back_far(value):
        return lax.ppermute(value, "seq", [(1, 3)])

    count = len(sizes)
    kvr, qb, qa = [keys_up(kv[0])], [to_hub_far(q[0])], [to_hub(q[0])]
    oa, ob, ra, rb = [], [], [], []

    def work(c, gate):
        gates = (gate, early[1]) if c == 0 else (gate,)
        far = remote_part(place, rows, True, qb[c], after(kvr[c], *gates), kv[c])
        ob.append(far)
        rb.append(back_far(after(far, rb[c - 1]) if c else far))
        gates = (far, rb[c - 1]) if c else (far,)
        near = remote_part(place, rows, False, qa[c], after(kvr[c], *gates), kv[c])
        oa.append(near)
        if c == 1:
            near = after(near, qb[2])
        ra.append(back(after(near, ra[c - 1]) if c == 1 else near))

    own_in = list(zip(q, kv))
    own_in[-1] = (q[-1], kv[-1])
    own = own_part(rows, own_in)
    qb.append(to_hub_far(q[1]))
    upper = lax.ppermute(halo, "seq", [(1, 2), (2, 3)])
    kvr.append(keys_up(after(kv[1], upper, own[1])))
    work(0, own[1])
    qa.append(to_hub(after(q[1], ob[0])))
    own_first = passed_part(place, rows, 0, q[0], after(kvr[0], oa[0]), own)
    kvr.append(keys_up(after(kv[2], kvr[1], qb[1], oa[0], own_first[1])))
    qb.append(to_hub_far(after(q[2], kvr[1], qb[1], oa[0], own_first[1])))
    work(1, own_first[1])
    qa.append(to_hub(after(q[2], oa[1])))
    lower = lax.ppermute(after(halo, kvr[2], oa[1]), "seq", [(0, 1)])

    def finish(c, so_far):
        mine = passed_part(place, rows, starts[c], q[c], after(kvr[c], oa[2]), own)
        return final_part(
            place, rows, chans, starts[c], mine, [(q[c], kvr[c], ra[c], rb[c])], so_far
        )

    work(2, oa[1])
    out = final_part(
        place, rows, chans, 0, own_first, [(q[0], kvr[0], after(ra[0], oa[2]), rb[0])], None
    )
    out = finish(1, out)
    (hyena_out,) = hyena((after(upper, oa[-1], out), lower), early)
    out, hyena_out = lax.optimization_barrier((out, hyena_out))
    out = finish(2, out)
    return out, hyena_out


def gathered_kernel(place_ref, q_ref, k_ref, v_ref, out_ref, top_ref, total_ref, mixed_ref):
    shard = pl.program_id(1)
    place = place_ref[0]

    @pl.when(shard == 0)
    def _():
        top_ref[...] = jnp.full(top_ref.shape, NEG, F32)
        total_ref[...] = jnp.zeros(total_ref.shape, F32)
        mixed_ref[...] = jnp.zeros(mixed_ref.shape, F32)

    def update(scores):
        top = jnp.maximum(top_ref[...], jnp.max(scores, axis=0, keepdims=True) * SCALE2)
        weights = jnp.exp2(scores * SCALE2 - top)
        keep = jnp.exp2(top_ref[...] - top)
        total_ref[...] = keep * total_ref[...] + jnp.sum(weights, axis=0, keepdims=True)
        mixed_ref[...] = keep * mixed_ref[...] + weighted(v_ref[...], weights.astype(BF16))
        top_ref[...] = top

    @pl.when(shard < place)
    def _():
        update(scores_of(k_ref[...], q_ref[...]))

    @pl.when(shard == place)
    def _():
        update(causal_scores(k_ref[...], q_ref[...]))
        out_ref[...] = (mixed_ref[...] / total_ref[...]).T.astype(BF16)


def attention_gathered(attn_q, attn_k, attn_v, place):
    rows, chans = attn_q.shape
    shards = lax.axis_size("seq")
    key = lax.all_gather(attn_k, "seq", axis=0, tiled=True)
    value = lax.all_gather(attn_v, "seq", axis=0, tiled=True)
    own = pl.BlockSpec((rows, HD), lambda h, s, p: (0, h))
    other = pl.BlockSpec((rows, HD), lambda h, s, p: (jnp.minimum(s, p[0]), h))
    return pl.pallas_call(
        gathered_kernel,
        grid_spec=pltpu.PrefetchScalarGridSpec(
            num_scalar_prefetch=1,
            grid=(chans // HD, shards),
            in_specs=[own, other, other],
            out_specs=own,
            scratch_shapes=[
                pltpu.VMEM((1, rows), F32),
                pltpu.VMEM((1, rows), F32),
                pltpu.VMEM((HD, rows), F32),
            ],
        ),
        out_shape=jax.ShapeDtypeStruct((rows, chans), BF16),
        compiler_params=ceil_params(),
        name="gathered_part",
    )(place, attn_q, key, value)


def per_device(
    hyena_q, hyena_k, hyena_v, short_filter, long_filter, skip_bias, attn_q, attn_k, attn_v
):
    shards = lax.axis_size("seq")
    heads = attn_q.shape[1] // HD
    place = lax.axis_index("seq").astype(jnp.int32).reshape(1)
    arrays = tuple(in_hbm(value) for value in (hyena_q, hyena_k, hyena_v))
    halo = halo_pack(*arrays, short_filter)

    filter_rows, skip_row = long_filter.T, skip_bias[None]

    def hyena(halos, so_far):
        return hyena_half(
            hyena_q, hyena_k, hyena_v, short_filter, filter_rows, skip_row, halos, so_far
        )

    early = hyena((), None)
    if shards == 4 and 2 <= heads <= 8:
        attn_out, hyena_out = attention_four(attn_q, attn_k, attn_v, place, halo, hyena, early)
    else:
        upper = lax.ppermute(halo, "seq", [(s, s + 1) for s in range(1, shards - 1)])
        lower = lax.ppermute(halo, "seq", [(0, 1)] if shards > 1 else [])
        (hyena_out,) = hyena((upper, lower), early)
        attn_out = attention_gathered(attn_q, attn_k, attn_v, place)
    return hyena_out, attn_out


def solution(mesh):
    both = P(("grp", "seq"), ("mp", "rep"))
    in_specs = (
        both,
        both,
        both,
        P(None, None, ("mp", "rep")),
        P(None, ("mp", "rep")),
        P(("mp", "rep")),
        both,
        both,
        both,
    )
    return jax.shard_map(
        per_device, mesh=mesh, in_specs=in_specs, out_specs=(both, both), check_vma=False
    )
```

```python
import functools

import jax
import jax.numpy as jnp
from jax import lax
from jax.experimental import pallas as pl
from jax.experimental.pallas import tpu as pltpu
from jax.sharding import PartitionSpec as P

HD = 128
FILT = 128
SHORT = 3
GSIZE = 16
LANES = 128
TAIL = 16
STATS = 16
MiB = 1 << 20
LOG2E = 1.4426950408889634
SCALE2 = HD**-0.5 * LOG2E
NEG = -1e30
F32 = jnp.float32
BF16 = jnp.bfloat16


def ceil_params(limit=16):
    return pltpu.CompilerParams(vmem_limit_bytes=limit * MiB)


def estimate(flops, moved):
    return pl.CostEstimate(flops=int(4 * flops), bytes_accessed=int(4 * moved), transcendentals=0)


def in_vmem():
    return pl.BlockSpec(memory_space=pltpu.VMEM)


def in_hbm(value):
    return pltpu.with_memory_space_constraint(value, pltpu.HBM)


def after(value, *others):
    return lax.optimization_barrier((value, *others))[0]


def short_conv(extended, taps, keep):
    total = taps[0][None] * extended
    total = total + taps[1][None] * pltpu.roll(extended, 1, 0)
    total = total + taps[2][None] * pltpu.roll(extended, 2, 0)
    return total[keep:]


def halo_kernel(q_hbm, k_hbm, v_hbm, taps_hbm, out_ref, q_in, k_in, v_in, taps_ref, sems):
    rows = q_hbm.shape[0]
    reach = FILT + TAIL
    copies = [
        pltpu.make_async_copy(k_hbm.at[pl.ds(rows - reach, reach)], k_in, sems.at[0]),
        pltpu.make_async_copy(v_hbm.at[pl.ds(rows - reach, reach)], v_in, sems.at[1]),
        pltpu.make_async_copy(q_hbm.at[pl.ds(rows - TAIL, TAIL)], q_in, sems.at[2]),
        pltpu.make_async_copy(taps_hbm, taps_ref, sems.at[3]),
    ]
    for copy in copies:
        copy.start()
    for copy in copies:
        copy.wait()
    for start in range(0, out_ref.shape[1], LANES):
        cols = slice(start, start + LANES)
        k_tile = k_in[:, cols].astype(F32)
        v_tile = v_in[:, cols].astype(F32)
        k_conv = short_conv(k_tile, taps_ref[1, :, cols], TAIL)
        v_conv = short_conv(v_tile, taps_ref[2, :, cols], TAIL)
        out_ref[:FILT, cols] = (k_conv * v_conv).astype(BF16)
        q_tail = q_in[:, cols].astype(F32)
        k_tail = pltpu.roll(k_tile[FILT:], TAIL - 2, 0)
        v_tail = pltpu.roll(v_tile[FILT:], TAIL - 4, 0)
        row = lax.broadcasted_iota(jnp.int32, q_tail.shape, 0)
        packed = jnp.where(row >= TAIL - 2, q_tail, jnp.where(row >= TAIL - 4, k_tail, v_tail))
        out_ref[FILT:, cols] = packed.astype(BF16)


def halo_pack(hyena_q, hyena_k, hyena_v, short_filter):
    rows, chans = hyena_q.shape
    whole = pl.BlockSpec(memory_space=pl.ANY)
    return pl.pallas_call(
        halo_kernel,
        in_specs=[whole, whole, whole, whole],
        out_specs=in_vmem(),
        out_shape=jax.ShapeDtypeStruct((FILT + TAIL, chans), BF16),
        scratch_shapes=[
            pltpu.VMEM((TAIL, chans), BF16),
            pltpu.VMEM((FILT + TAIL, chans), BF16),
            pltpu.VMEM((FILT + TAIL, chans), BF16),
            pltpu.VMEM(short_filter.shape, F32),
            pltpu.SemaphoreType.DMA((4,)),
        ],
        compiler_params=ceil_params(16),
        cost_estimate=estimate(20 * FILT * chans, 2 * 4 * FILT * chans),
        name="halo_pack",
    )(hyena_q, hyena_k, hyena_v, in_hbm(short_filter))


def hyena_kernel(late, q_ref, k_ref, v_ref, taps_ref, filt_ref, skip_ref, *rest):
    long_ref, ready_ref, sem = rest[-3:]
    out_ref, table_ref = (rest[-4], rest[2]) if late else rest[:2]
    rows, chans = q_ref.shape
    half = rows // 2
    blocks = half // FILT
    groups = LANES // GSIZE
    source = lax.broadcasted_iota(jnp.int32, (FILT, FILT), 0)
    target = lax.broadcasted_iota(jnp.int32, (FILT, FILT), 1)
    near = target >= source

    def one_tile(index, carry):
        cols = pl.ds(pl.multiple_of(index * LANES, LANES), LANES)
        if late:
            halo = rest[0][:, cols].astype(F32) + rest[1][:, cols].astype(F32)
            tail = halo[FILT:]
            tails = (tail, pltpu.roll(tail, 2, 0), pltpu.roll(tail, 4, 0))

        def conv(which, ref, reach):
            if late:
                signal = jnp.concatenate([tails[which], ref[:half, cols].astype(F32)], axis=0)
            else:
                signal = ref[half - reach - TAIL :, cols].astype(F32)
            return short_conv(signal, taps_ref[which, :, cols], TAIL)

        product = (conv(1, k_ref, FILT) * conv(2, v_ref, FILT)).astype(BF16).astype(F32)
        if late:
            gated = product
            signal = jnp.concatenate([halo[:FILT], gated], axis=0)
        else:
            gated = product[FILT:]
            signal = product
        signal = signal.T.astype(BF16)
        if not late:
            filters = filt_ref[pl.ds(pl.multiple_of(index * groups, groups), groups), :]
        for group in range(groups):
            place = pl.multiple_of((index * groups + group) * 2 * FILT, 2 * FILT)
            if late:
                table = table_ref[pl.ds(place, 2 * FILT), :]
            else:
                taps = jnp.broadcast_to(filters[group : group + 1], (8, FILT))
                base = pltpu.roll(taps, 0, 1, stride=1, stride_axis=0)
                turned = jnp.concatenate(
                    [base] + [pltpu.roll(base, s, 1) for s in range(8, FILT, 8)], axis=0
                )
                table = jnp.concatenate(
                    [jnp.where(near, 0.0, turned), jnp.where(near, turned, 0.0)], axis=0
                ).astype(BF16)
                table_ref[pl.ds(place, 2 * FILT), :] = table
            band = signal[group * GSIZE : (group + 1) * GSIZE]
            stacked = jnp.concatenate(
                [band[:, b * FILT : (b + 2) * FILT] for b in range(blocks)], axis=0
            )
            result = jnp.dot(stacked, table, preferred_element_type=F32)
            for b in range(blocks):
                long_ref[
                    group * GSIZE : (group + 1) * GSIZE, b * FILT : (b + 1) * FILT
                ] = result[b * GSIZE : (b + 1) * GSIZE]
        long_conv = long_ref[...].T
        mixed = conv(0, q_ref, 0) * (long_conv + skip_ref[:, cols] * gated)
        ready_ref[:, cols] = mixed.astype(BF16)
        return carry

    lax.fori_loop(0, chans // LANES, one_tile, 0)
    copy = pltpu.make_async_copy(
        ready_ref, out_ref.at[pl.ds(0 if late else half, half), :], sem
    )
    copy.start()
    copy.wait()


def hyena_half(hyena_q, hyena_k, hyena_v, short_filter, filter_rows, skip_row, halos, so_far):
    rows, chans = hyena_q.shape
    late = so_far is not None
    half = rows // 2
    operands = [hyena_q, hyena_k, hyena_v, short_filter, filter_rows, skip_row, *halos]
    specs = [in_vmem()] * len(operands)
    aliases = {}
    outs = [pl.BlockSpec(memory_space=pl.ANY)]
    shapes = [jax.ShapeDtypeStruct((rows, chans), BF16)]
    if late:
        so_far, table = so_far
        operands.append(table)
        specs.append(in_vmem())
        aliases = {len(operands): 0}
        operands.append(so_far)
        specs.append(pl.BlockSpec(memory_space=pl.ANY))
    else:
        outs.append(in_vmem())
        shapes.append(jax.ShapeDtypeStruct((chans // GSIZE * 2 * FILT, FILT), BF16))
    return pl.pallas_call(
        functools.partial(hyena_kernel, late),
        in_specs=specs,
        out_specs=outs,
        out_shape=shapes,
        scratch_shapes=[
            pltpu.VMEM((LANES, half), F32),
            pltpu.VMEM((half, chans), BF16),
            pltpu.SemaphoreType.DMA,
        ],
        input_output_aliases=aliases,
        compiler_params=ceil_params(16),
        cost_estimate=estimate(rows * chans * 256 * 8, 8 * rows * chans),
        name="hyena_late" if late else "hyena_early",
    )(*operands)


def scores_of(key, query):
    return lax.dot_general(key, query, (((1,), (1,)), ((), ())), preferred_element_type=F32)


def weighted(value, probs):
    return lax.dot_general(value, probs, (((0,), (0,)), ((), ())), preferred_element_type=F32)


def causal_scores(key, query):
    scores = scores_of(key, query)
    key_pos = lax.broadcasted_iota(jnp.int32, scores.shape, 0)
    query_pos = lax.broadcasted_iota(jnp.int32, scores.shape, 1)
    return jnp.where(key_pos <= query_pos, scores, NEG)


def attend(query, blocks):
    top = None
    mixed = None
    for key, value, causal in blocks:
        scores = causal_scores(key, query) if causal else scores_of(key, query)
        block_top = jnp.max(scores, axis=0, keepdims=True) * SCALE2
        extended = jnp.concatenate([value, jnp.ones((value.shape[0], HD), BF16)], axis=1)
        if top is None:
            top = block_top
            mixed = weighted(extended, jnp.exp2(scores * SCALE2 - top).astype(BF16))
        else:
            new_top = jnp.maximum(top, block_top)
            keep = jnp.exp2(top - new_top)
            term = weighted(extended, jnp.exp2(scores * SCALE2 - new_top).astype(BF16))
            mixed = keep * mixed + term
            top = new_top
    total = mixed[HD : HD + 1]
    return mixed[:HD] / total, top + jnp.log2(total)


def split_kernel(rows, chunks, place_ref, q_ref, k_ref, v_ref, *rest):
    out_refs, sems = rest[:-1], rest[-1]
    copies = []

    def send(source, head, target, slot):
        copies.append(
            pltpu.make_async_copy(
                source.at[:, pl.ds(head * HD, HD)],
                target.at[pl.ds(slot * rows, rows), :],
                sems.at[len(copies)],
            )
        )

    for index, (offset, heads) in enumerate(chunks):
        query_ref, kv_ref = out_refs[2 * index : 2 * index + 2]
        for j in range(heads):
            send(q_ref, offset + j, query_ref, j)
            send(k_ref, offset + j, kv_ref, 2 * j)
            send(v_ref, offset + j, kv_ref, 2 * j + 1)
    for copy in copies:
        copy.start()
    for copy in copies:
        copy.wait()


def split_heads_out(place, attn_q, attn_k, attn_v, chunks):
    rows = attn_q.shape[0]
    shapes = []
    for _, heads in chunks:
        shapes.append(jax.ShapeDtypeStruct((heads * rows, HD), BF16))
        shapes.append(jax.ShapeDtypeStruct((2 * heads * rows, HD), BF16))
    total = sum(heads for _, heads in chunks)
    return pl.pallas_call(
        functools.partial(split_kernel, rows, chunks),
        in_specs=[pl.BlockSpec(memory_space=pltpu.SMEM)] + [pl.BlockSpec(memory_space=pl.ANY)] * 3,
        out_specs=[in_vmem() for _ in shapes],
        out_shape=shapes,
        scratch_shapes=[pltpu.SemaphoreType.DMA((3 * total,))],
        compiler_params=ceil_params(),
        cost_estimate=estimate(0, 12 * rows * total * HD),
        name="split_heads",
    )(place, attn_q, attn_k, attn_v)


def head_rows(ref, slot, rows):
    return ref[slot * rows : (slot + 1) * rows]


def query_tile(rows):
    return min(256, rows)


def remote_kernel(heads, far, place_ref, q_ref, kvr_ref, kv_ref, o_ref, stat_ref):
    place = place_ref[0]
    rows = o_ref.shape[1]
    tile = query_tile(rows)

    def fill(kv_refs):
        for head in range(heads):
            blocks = [
                (head_rows(ref, 2 * head, rows), head_rows(ref, 2 * head + 1, rows), False)
                for ref in kv_refs
            ]
            for start in range(0, rows, tile):
                query = q_ref[head * rows + start : head * rows + start + tile]
                mixed, level = attend(query, blocks)
                o_ref[head * HD : (head + 1) * HD, start : start + tile] = mixed.astype(BF16)
                stat_ref[head : head + 1, start : start + tile] = level
        level = stat_ref[...]
        high = level.astype(BF16).astype(F32)
        middle = (level - high).astype(BF16).astype(F32)
        low = level - high - middle
        row = lax.broadcasted_iota(jnp.int32, level.shape, 0)
        first = jnp.where(row < 4, high, pltpu.roll(middle, 4, 0))
        o_ref[heads * HD :] = jnp.concatenate([first, low], axis=0).astype(BF16)

    @pl.when(place == 1)
    def _():
        fill([kvr_ref, kv_ref])

    if not far:

        @pl.when(place == 2)
        def _():
            fill([kv_ref])


def remote_part(place, rows, far, q, kvr, kv):
    heads = q.shape[0] // rows
    width = heads * HD
    return pl.pallas_call(
        functools.partial(remote_kernel, heads, far),
        in_specs=[pl.BlockSpec(memory_space=pltpu.SMEM)] + [in_vmem()] * 3,
        out_specs=in_vmem(),
        out_shape=jax.ShapeDtypeStruct((width + STATS, rows), BF16),
        scratch_shapes=[pltpu.VMEM((8, rows), F32)],
        compiler_params=ceil_params(),
        cost_estimate=estimate(heads * 8 * HD * rows * rows, 10 * rows * width),
        name="remote_far" if far else "remote_near",
    )(place, q, kvr, kv)


def level_row(stats, head):
    row = lax.broadcasted_iota(jnp.int32, stats.shape, 0)
    chosen = (row == head) | (row == head + 4) | (row == head + 8)
    return jnp.sum(jnp.where(chosen, stats, 0.0), axis=0, keepdims=True)


def own_kernel(sizes, *rest):
    count = len(sizes)
    mixed_ref, level_ref = rest[2 * count :]
    rows = mixed_ref.shape[1]
    tile = query_tile(rows)
    column = 0
    for index, heads in enumerate(sizes):
        q_ref, kv_ref = rest[2 * index : 2 * index + 2]
        for head in range(heads):
            key = head_rows(kv_ref, 2 * head, rows)
            value = head_rows(kv_ref, 2 * head + 1, rows)
            for start in range(0, rows, tile):
                cols = slice(start, start + tile)
                query = q_ref[head * rows + start : head * rows + start + tile]
                blocks = [(key[cols], value[cols], True)]
                if start:
                    blocks.append((key[:start], value[:start], False))
                mixed, level = attend(query, blocks)
                mixed_ref[column * HD : (column + 1) * HD, cols] = mixed
                level_ref[column : column + 1, cols] = level
            column += 1


def own_part(rows, messages):
    sizes = tuple(q.shape[0] // rows for q, _ in messages)
    total = sum(sizes)
    return pl.pallas_call(
        functools.partial(own_kernel, sizes),
        in_specs=[in_vmem()] * (2 * len(sizes)),
        out_specs=(in_vmem(), in_vmem()),
        out_shape=(
            jax.ShapeDtypeStruct((total * HD, rows), F32),
            jax.ShapeDtypeStruct((total, rows), F32),
        ),
        compiler_params=ceil_params(),
        cost_estimate=estimate(total * 3 * HD * rows * rows, 10 * rows * total * HD),
        name="own_part",
    )(*[value for pair in messages for value in pair])


def passed_kernel(heads, first, place_ref, q_ref, kvr_ref, own_ref, own_level_ref, mixed_ref, level_ref):
    rows = mixed_ref.shape[1]
    tile = query_tile(rows)
    mixed_ref[...] = own_ref[first * HD : (first + heads) * HD]
    level_ref[...] = own_level_ref[first : first + heads]

    @pl.when(place_ref[0] == 1)
    def _():
        for head in range(heads):
            at = slice(head * HD, (head + 1) * HD)
            block = (
                head_rows(kvr_ref, 2 * head, rows),
                head_rows(kvr_ref, 2 * head + 1, rows),
                False,
            )
            for start in range(0, rows, tile):
                cols = slice(start, start + tile)
                query = q_ref[head * rows + start : head * rows + start + tile]
                other, other_level = attend(query, [block])
                level = level_ref[head : head + 1, cols]
                top = jnp.maximum(level, other_level)
                mine = jnp.exp2(level - top)
                theirs = jnp.exp2(other_level - top)
                both = mine + theirs
                mixed_ref[at, cols] = mixed_ref[at, cols] * (mine / both) + other * (theirs / both)
                level_ref[head : head + 1, cols] = top + jnp.log2(both)


def passed_part(place, rows, first, q, kvr, own):
    heads = q.shape[0] // rows
    return pl.pallas_call(
        functools.partial(passed_kernel, heads, first),
        in_specs=[pl.BlockSpec(memory_space=pltpu.SMEM)] + [in_vmem()] * 4,
        out_specs=(in_vmem(), in_vmem()),
        out_shape=(
            jax.ShapeDtypeStruct((heads * HD, rows), F32),
            jax.ShapeDtypeStruct((heads, rows), F32),
        ),
        compiler_params=ceil_params(),
        cost_estimate=estimate(heads * 4 * HD * rows * rows, 10 * rows * heads * HD),
        name="passed_part",
    )(place, q, kvr, *own)


def final_kernel(sizes, first, aliased, place_ref, own_ref, own_level_ref, *rest):
    count = len(sizes)
    groups = [rest[4 * i : 4 * i + 4] for i in range(count)]
    out_ref, mixed_ref, level_ref, ready_ref, sem = rest[4 * count + aliased :]
    place = place_ref[0]
    rows = mixed_ref.shape[1]
    tile = query_tile(rows)
    column = 0
    copies = []

    def merge(other, other_level, cols):
        level = level_ref[:, cols]
        top = jnp.maximum(level, other_level)
        mine = jnp.exp2(level - top)
        theirs = jnp.exp2(other_level - top)
        both = mine + theirs
        mixed_ref[:, cols] = mixed_ref[:, cols] * (mine / both) + other * (theirs / both)
        level_ref[:, cols] = top + jnp.log2(both)

    for heads, (q_ref, kvr_ref, oa_ref, ob_ref) in zip(sizes, groups):
        for head in range(heads):
            at = column
            mixed_ref[...] = own_ref[at * HD : (at + 1) * HD]
            level_ref[...] = own_level_ref[at : at + 1]

            def received(o_ref, head=head, heads=heads):
                merge(
                    o_ref[head * HD : (head + 1) * HD].astype(F32),
                    level_row(o_ref[heads * HD :].astype(F32), head),
                    slice(0, rows),
                )

            pl.when(place >= 2)(functools.partial(received, oa_ref))
            pl.when(place >= 3)(functools.partial(received, ob_ref))
            span = pl.ds(column * HD, HD)
            ready_ref[:, column * HD : (column + 1) * HD] = mixed_ref[...].T.astype(BF16)
            copy = pltpu.make_async_copy(
                ready_ref.at[:, span], out_ref.at[:, pl.ds((first + column) * HD, HD)], sem.at[column]
            )
            copy.start()
            copies.append(copy)
            column += 1
    for copy in copies:
        copy.wait()


def final_part(place, rows, chans, first, own, groups, so_far):
    sizes = tuple(group[0].shape[0] // rows for group in groups)
    total = sum(sizes)
    operands = [place, *own] + [value for group in groups for value in group]
    specs = [pl.BlockSpec(memory_space=pltpu.SMEM)] + [in_vmem()] * (len(operands) - 1)
    aliases = {}
    if so_far is not None:
        aliases = {len(operands): 0}
        operands.append(so_far)
        specs.append(pl.BlockSpec(memory_space=pl.ANY))
    return pl.pallas_call(
        functools.partial(final_kernel, sizes, first, len(aliases)),
        in_specs=specs,
        out_specs=pl.BlockSpec(memory_space=pl.ANY),
        out_shape=jax.ShapeDtypeStruct((rows, chans), BF16),
        scratch_shapes=[
            pltpu.VMEM((HD, rows), F32),
            pltpu.VMEM((1, rows), F32),
            pltpu.VMEM((rows, total * HD), BF16),
            pltpu.SemaphoreType.DMA((total,)),
        ],
        input_output_aliases=aliases,
        compiler_params=ceil_params(),
        cost_estimate=estimate(total * 4 * HD * rows * rows, 14 * rows * total * HD),
        name="final_part",
    )(*operands)


def chunk_sizes(heads):
    parts = 3
    base = heads // parts
    return [base + (part < heads - parts * base) for part in range(parts)]


def attention_four(attn_q, attn_k, attn_v, place, halo, hyena, early):
    rows, chans = attn_q.shape
    sizes = chunk_sizes(chans // HD)
    starts = [sum(sizes[:c]) for c in range(len(sizes))]
    arrays = tuple(in_hbm(value) for value in (attn_q, attn_k, attn_v))
    q0, kv0 = split_heads_out(place, *arrays, [(0, sizes[0])])
    rest = split_heads_out(place, *arrays, list(zip(starts, sizes))[1:])
    q, kv = [q0, *rest[0::2]], [kv0, *rest[1::2]]

    def to_hub(value):
        return lax.ppermute(value, "seq", [(2, 1), (3, 2)])

    def to_hub_far(value):
        return lax.ppermute(value, "seq", [(3, 1)])

    def keys_up(value):
        return lax.ppermute(value, "seq", [(0, 1)])

    def back(value):
        return lax.ppermute(value, "seq", [(1, 2), (2, 3)])

    def back_far(value):
        return lax.ppermute(value, "seq", [(1, 3)])

    count = len(sizes)
    kvr, qb, qa = [keys_up(kv[0])], [to_hub_far(q[0])], [to_hub(q[0])]
    oa, ob, ra, rb = [], [], [], []

    def work(c, gate):
        gates = (gate, early[1]) if c == 0 else (gate,)
        far = remote_part(place, rows, True, qb[c], after(kvr[c], *gates), kv[c])
        ob.append(far)
        rb.append(back_far(after(far, rb[c - 1]) if c else far))
        gates = (far, rb[c - 1]) if c else (far,)
        near = remote_part(place, rows, False, qa[c], after(kvr[c], *gates), kv[c])
        oa.append(near)
        if c == 1:
            near = after(near, qb[2])
        ra.append(back(after(near, ra[c - 1]) if c == 1 else near))

    own_in = list(zip(q, kv))
    own_in[-1] = (q[-1], kv[-1])
    own = own_part(rows, own_in)
    qb.append(to_hub_far(q[1]))
    upper = lax.ppermute(halo, "seq", [(1, 2), (2, 3)])
    kvr.append(keys_up(after(kv[1], upper, own[1])))
    work(0, own[1])
    qa.append(to_hub(after(q[1], ob[0])))
    own_first = passed_part(place, rows, 0, q[0], after(kvr[0], oa[0]), own)
    kvr.append(keys_up(after(kv[2], kvr[1], qb[1], oa[0], own_first[1])))
    qb.append(to_hub_far(after(q[2], kvr[1], qb[1], oa[0], own_first[1])))
    work(1, own_first[1])
    qa.append(to_hub(after(q[2], oa[1])))
    lower = lax.ppermute(after(halo, kvr[2], oa[1]), "seq", [(0, 1)])

    def finish(c, so_far):
        mine = passed_part(place, rows, starts[c], q[c], after(kvr[c], oa[2]), own)
        return final_part(
            place, rows, chans, starts[c], mine, [(q[c], kvr[c], ra[c], rb[c])], so_far
        )

    work(2, oa[1])
    out = final_part(
        place, rows, chans, 0, own_first, [(q[0], kvr[0], after(ra[0], oa[2]), rb[0])], None
    )
    out = finish(1, out)
    (hyena_out,) = hyena((after(upper, oa[-1], out), lower), early)
    out, hyena_out = lax.optimization_barrier((out, hyena_out))
    out = finish(2, out)
    return out, hyena_out


def gathered_kernel(place_ref, q_ref, k_ref, v_ref, out_ref, top_ref, total_ref, mixed_ref):
    shard = pl.program_id(1)
    place = place_ref[0]

    @pl.when(shard == 0)
    def _():
        top_ref[...] = jnp.full(top_ref.shape, NEG, F32)
        total_ref[...] = jnp.zeros(total_ref.shape, F32)
        mixed_ref[...] = jnp.zeros(mixed_ref.shape, F32)

    def update(scores):
        top = jnp.maximum(top_ref[...], jnp.max(scores, axis=0, keepdims=True) * SCALE2)
        weights = jnp.exp2(scores * SCALE2 - top)
        keep = jnp.exp2(top_ref[...] - top)
        total_ref[...] = keep * total_ref[...] + jnp.sum(weights, axis=0, keepdims=True)
        mixed_ref[...] = keep * mixed_ref[...] + weighted(v_ref[...], weights.astype(BF16))
        top_ref[...] = top

    @pl.when(shard < place)
    def _():
        update(scores_of(k_ref[...], q_ref[...]))

    @pl.when(shard == place)
    def _():
        update(causal_scores(k_ref[...], q_ref[...]))
        out_ref[...] = (mixed_ref[...] / total_ref[...]).T.astype(BF16)


def attention_gathered(attn_q, attn_k, attn_v, place):
    rows, chans = attn_q.shape
    shards = lax.axis_size("seq")
    key = lax.all_gather(attn_k, "seq", axis=0, tiled=True)
    value = lax.all_gather(attn_v, "seq", axis=0, tiled=True)
    own = pl.BlockSpec((rows, HD), lambda h, s, p: (0, h))
    other = pl.BlockSpec((rows, HD), lambda h, s, p: (jnp.minimum(s, p[0]), h))
    return pl.pallas_call(
        gathered_kernel,
        grid_spec=pltpu.PrefetchScalarGridSpec(
            num_scalar_prefetch=1,
            grid=(chans // HD, shards),
            in_specs=[own, other, other],
            out_specs=own,
            scratch_shapes=[
                pltpu.VMEM((1, rows), F32),
                pltpu.VMEM((1, rows), F32),
                pltpu.VMEM((HD, rows), F32),
            ],
        ),
        out_shape=jax.ShapeDtypeStruct((rows, chans), BF16),
        compiler_params=ceil_params(),
        name="gathered_part",
    )(place, attn_q, key, value)


def per_device(
    hyena_q, hyena_k, hyena_v, short_filter, long_filter, skip_bias, attn_q, attn_k, attn_v
):
    shards = lax.axis_size("seq")
    heads = attn_q.shape[1] // HD
    place = lax.axis_index("seq").astype(jnp.int32).reshape(1)
    arrays = tuple(in_hbm(value) for value in (hyena_q, hyena_k, hyena_v))
    halo = halo_pack(*arrays, short_filter)

    filter_rows, skip_row = long_filter.T, skip_bias[None]

    def hyena(halos, so_far):
        return hyena_half(
            hyena_q, hyena_k, hyena_v, short_filter, filter_rows, skip_row, halos, so_far
        )

    early = hyena((), None)
    if shards == 4 and 2 <= heads <= 8:
        attn_out, hyena_out = attention_four(attn_q, attn_k, attn_v, place, halo, hyena, early)
    else:
        upper = lax.ppermute(halo, "seq", [(s, s + 1) for s in range(1, shards - 1)])
        lower = lax.ppermute(halo, "seq", [(0, 1)] if shards > 1 else [])
        (hyena_out,) = hyena((upper, lower), early)
        attn_out = attention_gathered(attn_q, attn_k, attn_v, place)
    return hyena_out, attn_out


def solution(mesh):
    both = P(("grp", "seq"), ("mp", "rep"))
    in_specs = (
        both,
        both,
        both,
        P(None, None, ("mp", "rep")),
        P(None, ("mp", "rep")),
        P(("mp", "rep")),
        both,
        both,
        both,
    )
    return jax.shard_map(
        per_device, mesh=mesh, in_specs=in_specs, out_specs=(both, both), check_vma=False
    )
```
